128 devices in a mesh: seq: 32 (over x, y, core), head: 4 (over z).
Axes of the slice: x: 4, y: 4, z: 4, core: 2. Of those that a mesh axis runs over, the one named last changes fastest.
Arguments:
- q2: bfloat16 [8192, 4096], P('seq', 'head'), may hold values from -128 to 128
- k2: bfloat16 [8192, 512], P('seq', 'head'), may hold values from -6 to 6
- v2: bfloat16 [8192, 512], P('seq', 'head'), may hold values from -6 to 6
- hidden: bfloat16 [8192, 8192], P('seq', 'head'), may hold values from -120 to 120
- w_query: bfloat16 [8192, 4096], P(None, 'head'), may hold values from -0.0625 to 0.0625
- b_query: float32 [4096], P('head'), may hold values from -3 to 3
- w_key: bfloat16 [8192, 512], P(None, 'head'), may hold values from -0.0625 to 0.0625
- b_key: float32 [512], P('head'), may hold values from -3 to 3
- w_value: bfloat16 [8192, 512], P(None, 'head'), may hold values from -0.0625 to 0.0625
- b_value: float32 [512], P('head'), may hold values from -3 to 3
- kept_index: int32 [8192], P('seq'), may hold values from 0 to 127, as said below
- block_count: int32 [64], P('seq'), may hold values from 0 to 128, as said below
- text_rows: int32 [256], replicated, may hold values from 0 to 8191, as said below
Outputs:
- attn2: bfloat16 [8192, 4096], P('seq', 'head')
- importance: float32 [8192], P('seq')
- attn3: bfloat16 [4224, 4096], P('seq', 'head')
The draws below stay inside these ranges and needn't reach their ends.
Inputs may be any that keep to these rules, and one draw needn't show every extreme that they name: `kept_index`: in each aligned block of 128 rows, the first block_count entries are the in-block indices of that block's kept rows in ascending order; the other entries are the block's remaining indices. `block_count`: every text row is kept, and exactly 4224 rows are kept in all. For every k, the rows 2 * k * 256 to (2 * k + 2) * 256 - 1 hold exactly 264 kept rows together. `text_rows`: Distinct, in ascending order.
All inputs are finite; a program needn't handle non-finite values.
Results may differ from the reference program's by a relative error of at most 0.0093.
Values may be sent and summed in bfloat16 or wider, within the bound.
No kernel may reach another device: no remote copies, remote signals or barrier semaphores. Data moves between devices by JAX's collectives and lax.ppermute only.
A program may use at most 128 MiB of HBM per device.

```python
import math
import jax
import jax.numpy as jnp
from jax import lax

D = 8192
HD = 128
GROUP = 8
KV_HEADS = 4
Q_HEADS = 32
ROWS_DEV = 256
BLOCK = 128
TEXT = 256
TOKENS = 8192
KEPT = 4224


def kept_layout(key):
    base = jax.random.fold_in(key, 7301)
    first, second, third = jax.random.split(base, 3)
    seq_count = TOKENS // ROWS_DEV
    share = TEXT // seq_count
    per_device = KEPT // seq_count
    starts = jax.random.randint(first, (seq_count,), 0, ROWS_DEV - share + 1)
    local = jnp.arange(ROWS_DEV, dtype=jnp.int32)[None, :]
    is_text = (local >= starts[:, None]) & (local < starts[:, None] + share)
    lower = jax.random.randint(second, (seq_count // 2,), share, ROWS_DEV + 1)
    counts_dev = jnp.stack([lower, 2 * per_device - lower], axis=1).reshape(-1)
    noise = jax.random.randint(third, (seq_count, ROWS_DEV), 0, 8192)
    priority = jnp.where(is_text, 3 * 8192, noise)
    distinct = priority * ROWS_DEV + local
    order_dev = jnp.argsort(-distinct, axis=1)
    rank = jnp.argsort(order_dev, axis=1)
    keep = (rank < counts_dev[:, None]).astype(jnp.int32).reshape(-1)
    grouped = keep.reshape(-1, BLOCK)
    counts = jnp.sum(grouped, axis=1).astype(jnp.int32)
    order = jnp.argsort(1 - grouped, axis=1, stable=True).astype(jnp.int32).reshape(-1)
    flat_text = is_text.reshape(-1).astype(jnp.int32)
    text_list = jnp.argsort(1 - flat_text, stable=True)[:TEXT].astype(jnp.int32)
    return (order, counts, text_list)


def draw_kept_index(key, part):
    return kept_layout(key)[0]


def draw_block_count(key, part):
    return kept_layout(key)[1]


def draw_text_rows(key, part):
    return kept_layout(key)[2]


def attention_inputs(key):
    base = jax.random.fold_in(key, 4211)
    first, second = jax.random.split(base, 2)
    queries = jax.random.truncated_normal(first, -6.0, 6.0, (TOKENS, Q_HEADS * HD), jnp.float32)
    keys = jax.random.truncated_normal(second, -6.0, 6.0, (TOKENS, KV_HEADS * HD), jnp.float32)
    return (queries, keys)


def draw_q2(key, part):
    return attention_inputs(key)[0].astype(jnp.bfloat16)


def draw_k2(key, part):
    return attention_inputs(key)[1].astype(jnp.bfloat16)


def draw_hidden(key, part):
    first = jax.random.fold_in(jax.random.fold_in(key, 5519), 0)
    states = jax.random.truncated_normal(first, -6.0, 6.0, (TOKENS, D), jnp.float32)
    return states.astype(jnp.bfloat16)


def block_scale(rng, dims, shards, least, top_value):
    gain = 1.0
    for dim, blocks in shards:
        heights = jax.random.uniform(jax.random.fold_in(jax.random.fold_in(rng, 6), dim), (blocks,), jnp.float32, least / len(shards), top_value / len(shards))
        gain = gain * jnp.repeat(jnp.exp(heights), dims[dim] // blocks).reshape((-1,) + (1,) * (len(dims) - 1 - dim))
    return gain


def centred(stream_key, shape, scale, limit, cuts=(), held_as=jnp.bfloat16):
    result = scale * jax.random.normal(stream_key, shape, jnp.float32)
    if cuts:
        result = result * block_scale(stream_key, shape, cuts, -0.22, 0.18)
    return jnp.clip(result, -limit, limit).astype(held_as)


def setup_inputs(seed: int = 0) -> dict:
    arg_keys = jax.random.split(jax.random.key(seed), 14)
    return {
        "q2": draw_q2(jax.random.fold_in(arg_keys[13], 71), 0),
        "k2": draw_k2(jax.random.fold_in(arg_keys[13], 71), 0),
        "v2": centred(arg_keys[2], (TOKENS, KV_HEADS * HD), 1.0, 6.0, ((0, 32), (1, 4))),
        "hidden": draw_hidden(jax.random.fold_in(arg_keys[13], 71), 0),
        "w_query": centred(arg_keys[4], (D, Q_HEADS * HD), D ** -0.5, 0.0625, ((1, 4),)),
        "b_query": centred(arg_keys[5], (Q_HEADS * HD,), 0.5, 3.0, ((0, 4),), jnp.float32),
        "w_key": centred(arg_keys[6], (D, KV_HEADS * HD), D ** -0.5, 0.0625, ((1, 4),)),
        "b_key": centred(arg_keys[7], (KV_HEADS * HD,), 0.5, 3.0, ((0, 4),), jnp.float32),
        "w_value": centred(arg_keys[8], (D, KV_HEADS * HD), D ** -0.5, 0.0625, ((1, 4),)),
        "b_value": centred(arg_keys[9], (KV_HEADS * HD,), 0.5, 3.0, ((0, 4),), jnp.float32),
        "kept_index": draw_kept_index(jax.random.fold_in(arg_keys[13], 71), 0),
        "block_count": draw_block_count(jax.random.fold_in(arg_keys[13], 71), 0),
        "text_rows": draw_text_rows(jax.random.fold_in(arg_keys[13], 71), 0),
    }


def rotate(values, positions):
    half = values.shape[-1] // 2
    freqs = 1000000.0 ** (-(jnp.arange(half, dtype=jnp.float32) * 2.0) / values.shape[-1])
    angles = positions.astype(jnp.float32)[:, None] * freqs[None, :]
    cosine = jnp.cos(angles)[:, None, :]
    sine = jnp.sin(angles)[:, None, :]
    first = values[..., :half]
    second = values[..., half:]
    return jnp.concatenate([first * cosine - second * sine, second * cosine + first * sine], axis=-1)

def causal_block(queries, keys, values, query_pos, key_pos):
    scores = jnp.einsum('qagd,kad->agqk', queries, keys) / math.sqrt(HD)
    allowed = key_pos[None, :] <= query_pos[:, None]
    top = lax.optimization_barrier(jnp.max(jnp.where(allowed, scores, -1e+30), axis=-1))
    weights = jnp.where(allowed, jnp.exp(scores - top[..., None]), 0.0)
    total = lax.optimization_barrier(jnp.sum(weights, axis=-1))
    rounded = weights.astype(jnp.bfloat16).astype(jnp.float32)
    summed = jnp.einsum('agqk,kad->qagd', rounded, values)
    return (summed / jnp.transpose(total, (2, 0, 1))[..., None], top, total)

def attention(queries, keys, values, positions):
    count = queries.shape[0]
    width = math.gcd(count, 256)

    def one_block(start):
        block = lax.dynamic_slice_in_dim(queries, start, width, 0)
        query_pos = lax.dynamic_slice_in_dim(positions, start, width, 0)
        out, top, total = causal_block(block, keys, values, query_pos, positions)
        return out.reshape(width, -1).astype(jnp.bfloat16)
    starts = jnp.arange(0, count, width, dtype=jnp.int32)
    return lax.map(one_block, starts).reshape(count, -1)

def reference(q2, k2, v2, hidden, w_query, b_query, w_key, b_key, w_value, b_value, kept_index, block_count, text_rows):
    positions = jnp.arange(TOKENS, dtype=jnp.int32)
    queries = q2.astype(jnp.float32).reshape(TOKENS, KV_HEADS, GROUP, HD)
    keys = k2.astype(jnp.float32).reshape(TOKENS, KV_HEADS, HD)
    values = v2.astype(jnp.float32).reshape(TOKENS, KV_HEADS, HD)
    attn2 = attention(queries, keys, values, positions)
    text_queries = queries[text_rows]
    _, top, total = causal_block(text_queries, keys, values, text_rows, positions)
    scores = jnp.einsum('tagd,kad->agtk', text_queries, keys) / math.sqrt(HD)
    allowed = positions[None, :] <= text_rows[:, None]
    probs = jnp.where(allowed, jnp.exp(scores - top[..., None]) / total[..., None], 0.0)
    importance = lax.optimization_barrier(jnp.sum(probs, axis=(0, 1, 2))) * (TOKENS / (Q_HEADS * TEXT))
    index_list = kept_index.reshape(-1, BLOCK)
    live = jnp.arange(BLOCK, dtype=jnp.int32)[None, :] < block_count[:, None]
    marks = jnp.any(live[:, :, None] & (index_list[:, :, None] == jnp.arange(BLOCK, dtype=jnp.int32)[None, None, :]), axis=1)
    flags = marks.reshape(TOKENS).astype(jnp.int32)
    kept_pos = jnp.argsort(1 - flags, stable=True)[:KEPT].astype(jnp.int32)
    rows = hidden[kept_pos]
    query_three = jnp.dot(rows, w_query, preferred_element_type=jnp.float32) + b_query
    query_three = rotate(query_three.reshape(KEPT, Q_HEADS, HD), kept_pos).astype(jnp.bfloat16)
    key_three = jnp.dot(rows, w_key, preferred_element_type=jnp.float32) + b_key
    key_three = rotate(key_three.reshape(KEPT, KV_HEADS, HD), kept_pos).astype(jnp.bfloat16)
    value_three = (jnp.dot(rows, w_value, preferred_element_type=jnp.float32) + b_value).astype(jnp.bfloat16)
    order = jnp.arange(KEPT, dtype=jnp.int32)
    attn3 = attention(query_three.astype(jnp.float32).reshape(KEPT, KV_HEADS, GROUP, HD), key_three.astype(jnp.float32).reshape(KEPT, KV_HEADS, HD), value_three.astype(jnp.float32).reshape(KEPT, KV_HEADS, HD), order)
    return (attn2, importance, attn3)
```

```python
import math

import jax
import jax.numpy as jnp
from jax import lax
from jax.experimental import pallas as pl
from jax.experimental.pallas import tpu as pltpu
from jax.sharding import PartitionSpec as P

HD = 128
GROUP = 8
BLOCK = 128
ROWS = 256
SHARE = 132
PAD = 136
WIDE = 1024
FACTOR = math.log2(math.e) / math.sqrt(HD)
LOW = -1e30
BF = jnp.bfloat16
F32 = jnp.float32


def dot(a, b):
    return jnp.dot(a, b, preferred_element_type=F32)


def dot_t(a, b):
    return lax.dot_general(a, b, (((1,), (1,)), ((), ())), preferred_element_type=F32)


def whole(shape):
    return pl.BlockSpec(shape, lambda *_: (0,) * len(shape))


def smem():
    return pl.BlockSpec(memory_space=pltpu.SMEM)


def pick_kernel(info, index_ref, hidden_ref, own_ref, send_ref):
    core, first, before, live0, live1 = (info[i] for i in range(5))
    count = live0 + live1
    start = jnp.where(core == 0, 0, 2 * SHARE - count)
    lane = lax.broadcasted_iota(jnp.int32, (PAD, ROWS), 1)
    place = lax.broadcasted_iota(jnp.int32, (PAD, ROWS), 0)
    second = lane >= BLOCK
    within = jnp.where(second, lane - BLOCK, lane)
    rank = jnp.where(second, within + live0, within)
    live = within < jnp.where(second, live1, live0)
    row = index_ref[...] + jnp.where(second, BLOCK, 0)
    column = lax.broadcasted_iota(jnp.int32, (PAD, BLOCK), 1)
    for out_ref, base in ((own_ref, SHARE * core), (send_ref, SHARE * (1 - core))):
        wanted = place + (base - start)
        match = (rank == wanted) & live & (place < SHARE)
        source = jnp.sum(jnp.where(match, (row + 1).astype(F32), 0.0), axis=1, keepdims=True)
        source = source.astype(jnp.int32) - 1
        select = jnp.where(lane == source, 1.0, 0.0).astype(BF)
        out_ref[:, : hidden_ref.shape[1]] = dot(select, hidden_ref[...]).astype(BF)
        position = jnp.where(source >= 0, source + first, 0)
        high = jnp.where(column == 0, position >> 7, 0)
        marks = jnp.where(column == 1, position & 127, high)
        out_ref[:, hidden_ref.shape[1] :] = marks.astype(F32).astype(BF)


def pick_rows(info, kept_index, hidden):
    width = hidden.shape[1] + BLOCK
    shape = jax.ShapeDtypeStruct((PAD, width), BF)
    return pl.pallas_call(
        pick_kernel,
        out_shape=(shape, shape),
        in_specs=[smem(), pl.BlockSpec(memory_space=pltpu.VMEM), pl.BlockSpec(memory_space=pltpu.VMEM)],
        out_specs=(pl.BlockSpec(memory_space=pltpu.VMEM),) * 2,
        compiler_params=pltpu.CompilerParams(vmem_limit_bytes=24 << 20),
        cost_estimate=pl.CostEstimate(
            flops=4 * PAD * ROWS * width, transcendentals=0, bytes_accessed=4 * ROWS * width
        ),
        name="pick_rows",
    )(info, kept_index.reshape(1, ROWS), hidden)


def rotated(u, cosine, sine):
    return u * cosine + pltpu.roll(u, HD // 2, 1) * sine


def project_kernel(pieces, last, blocks, *refs):
    x_refs = refs[:pieces]
    wq, wk, wv = refs[pieces : pieces + 3]
    rest = refs[pieces + 3 :]
    if last:
        q_in, kv_in, bq, bk, bv, cosine, sine, q_out, kv_out, q_acc, kv_acc = rest
    else:
        q_out, kv_out, q_acc, kv_acc = rest
    piece, tile = pl.program_id(0), pl.program_id(1)
    tiles = pl.num_programs(1)
    at = pl.ds(pl.multiple_of(tile * 256, 256), 256)
    for p in range(pieces):

        @pl.when(piece == p)
        def _(p=p):
            x = x_refs[p][...]
            got = dot(x, wq[...])
            if p > 0:
                got = got + q_acc[:, at]
            elif last:
                got = got + q_in[:, at]
            q_acc[:, at] = got

            @pl.when(tile == 0)
            def _():
                k, v = (dot(x, wk[...]), dot(x, wv[...]))
                if p > 0:
                    k, v = (k + kv_acc[:, :HD], v + kv_acc[:, HD:])
                elif last:
                    k, v = (k + kv_in[:, :HD], v + kv_in[:, HD:])
                kv_acc[:, :HD] = k
                kv_acc[:, HD:] = v

    @pl.when((piece == pieces - 1) & (tile == tiles - 1))
    def _():
        if last:
            c, s = (cosine[...], sine[...])
            for h in range(GROUP):
                part = slice(h * HD, (h + 1) * HD)
                q_out[:, part] = rotated(q_acc[:, part] + bq[:, part], c, s).astype(BF)
            kv_out[:, :HD] = rotated(kv_acc[:, :HD] + bk[...], c, s).astype(BF)
            kv_out[:, HD:] = (kv_acc[:, HD:] + bv[...]).astype(BF)
        else:
            q_out[...] = q_acc[...]
            kv_out[...] = kv_acc[...]


def project(blocks, xs, weights, extra):
    pieces = len(xs)
    last = bool(extra)
    depth = xs[0].shape[1]
    wq, wk, wv = weights
    columns = wq.shape[1]
    kind = BF if last else F32
    spec = pltpu.PrefetchScalarGridSpec(
        num_scalar_prefetch=1,
        grid=(pieces, columns // 256),
        in_specs=[whole(x.shape) for x in xs]
        + [
            pl.BlockSpec((depth, 256), lambda p, n, b: (b[p], n)),
            pl.BlockSpec((depth, HD), lambda p, n, b: (b[p], 0)),
            pl.BlockSpec((depth, HD), lambda p, n, b: (b[p], 0)),
        ]
        + [whole(e.shape) for e in extra],
        out_specs=(whole((PAD, columns)), whole((PAD, 2 * HD))),
        scratch_shapes=[pltpu.VMEM((PAD, columns), F32), pltpu.VMEM((PAD, 2 * HD), F32)],
    )

    def kernel(*refs):
        project_kernel(pieces, last, *refs)

    return pl.pallas_call(
        kernel,
        out_shape=(
            jax.ShapeDtypeStruct((PAD, columns), kind),
            jax.ShapeDtypeStruct((PAD, 2 * HD), kind),
        ),
        grid_spec=spec,
        compiler_params=pltpu.CompilerParams(vmem_limit_bytes=32 << 20),
        cost_estimate=pl.CostEstimate(
            flops=2 * pieces * PAD * depth * (columns + 2 * HD),
            transcendentals=0,
            bytes_accessed=2 * pieces * depth * (columns + 2 * HD),
        ),
        name="project_rest" if last else "project_own",
    )(blocks, *xs, wq, wk, wv, *extra)


def attend_kernel(info, q_ref, kv_ref, out_ref, q_s, top_s, sum_s, v_s, bias_s):
    step = pl.program_id(0)
    rank = info[0]
    last = (rank * ROWS) // WIDE

    @pl.when(step == 0)
    def _():
        for h in range(GROUP):
            q_s[h] = q_ref[:, h * HD : (h + 1) * HD]
        top_s[...] = jnp.full_like(top_s, LOW)
        sum_s[...] = jnp.zeros_like(sum_s)
        v_s[:, HD:] = jnp.ones((WIDE, HD), BF)

    def run(masked):
        keys = kv_ref[:, :HD]
        v_s[:, :HD] = kv_ref[:, HD:]
        if masked:
            key = lax.broadcasted_iota(jnp.int32, (ROWS, WIDE), 1)
            query = lax.broadcasted_iota(jnp.int32, (ROWS, WIDE), 0)
            shift = rank * ROWS - last * WIDE
            bias_s[...] = jnp.where(key <= query + shift, 0.0, LOW)

        def heads(i, carry):
            for h in (2 * i, 2 * i + 1):
                scores = dot_t(q_s[h], keys)
                if masked:
                    scores = scores + bias_s[...]
                before = top_s[h]
                top = jnp.maximum(before, jnp.max(scores, axis=1, keepdims=True))
                top_s[h] = top
                weights = jnp.exp2((scores - top[:, :1]) * FACTOR).astype(BF)
                fade = jnp.exp2((before - top) * FACTOR)
                fade = jnp.concatenate([fade, fade], axis=1)
                sum_s[h] = sum_s[h] * fade + dot(weights, v_s[...])
            return carry

        lax.fori_loop(0, GROUP // 2, heads, 0)

    @pl.when(step < last)
    def _():
        run(False)

    @pl.when(step == last)
    def _():
        run(True)
        for h in range(GROUP):
            total = sum_s[h]
            out_ref[:, h * HD : (h + 1) * HD] = (total[:, :HD] / total[:, HD:]).astype(BF)


def attend(info, q2, kv2):
    tokens = kv2.shape[0]
    spec = pltpu.PrefetchScalarGridSpec(
        num_scalar_prefetch=1,
        grid=(tokens // WIDE,),
        in_specs=[
            whole(q2.shape),
            pl.BlockSpec((WIDE, 2 * HD), lambda i, info: (jnp.minimum(i, info[0] * ROWS // WIDE), 0)),
        ],
        out_specs=whole(q2.shape),
        scratch_shapes=[
            pltpu.VMEM((GROUP, ROWS, HD), BF),
            pltpu.VMEM((GROUP, ROWS, HD), F32),
            pltpu.VMEM((GROUP, ROWS, 2 * HD), F32),
            pltpu.VMEM((WIDE, 2 * HD), BF),
            pltpu.VMEM((ROWS, WIDE), F32),
        ],
    )
    return pl.pallas_call(
        attend_kernel,
        out_shape=jax.ShapeDtypeStruct(q2.shape, BF),
        grid_spec=spec,
        compiler_params=pltpu.CompilerParams(vmem_limit_bytes=40 << 20),
        cost_estimate=pl.CostEstimate(
            flops=6 * GROUP * ROWS * tokens * HD,
            transcendentals=GROUP * ROWS * tokens,
            bytes_accessed=4 * tokens * HD,
        ),
        name="attend2",
    )(info, q2, kv2)


CHUNK = 8


def text_kernel(info, text, q_ref, kv_ref, out_ref, score_s):
    rank, low, count = (info[i] for i in range(3))
    first = rank * ROWS
    blocks = (first // WIDE) + 1
    out_ref[...] = jnp.zeros_like(out_ref)
    rows = GROUP * CHUNK

    def chunk(c, carry):
        place = jnp.zeros((CHUNK, ROWS), jnp.int32)
        sub = lax.broadcasted_iota(jnp.int32, (CHUNK, ROWS), 0)
        for i in range(CHUNK):
            n = c * CHUNK + i
            at = text[jnp.minimum(low + n, text.shape[0] - 1)] - first
            place = jnp.where(sub == i, jnp.where(n < count, at, -1), place)
        lane = lax.broadcasted_iota(jnp.int32, (CHUNK, ROWS), 1)
        select = jnp.where(lane == place, 1.0, 0.0).astype(BF)
        picked = dot(select, q_ref[...]).astype(BF)
        queries = jnp.concatenate(
            [picked[:, h * HD : (h + 1) * HD] for h in range(GROUP)], axis=0
        )
        place = jnp.concatenate([place[:, :HD]] * GROUP, axis=0)[:, :1]
        limit = first + jnp.maximum(place, 0)
        key = lax.broadcasted_iota(jnp.int32, (rows, WIDE), 1)

        def scored(b, top):
            at = pl.ds(pl.multiple_of(b * WIDE, WIDE), WIDE)
            scores = dot_t(queries, kv_ref[at, :HD])
            scores = jnp.where(key + b * WIDE <= limit, scores, LOW)
            score_s[:, at] = scores
            return jnp.maximum(top, jnp.max(scores, axis=1, keepdims=True))

        top = lax.fori_loop(0, blocks, scored, jnp.full((rows, 1), LOW, F32))

        def weighed(b, total):
            at = pl.ds(pl.multiple_of(b * WIDE, WIDE), WIDE)
            weights = jnp.exp2((score_s[:, at] - top) * FACTOR)
            score_s[:, at] = weights
            return total + jnp.sum(weights, axis=1, keepdims=True)

        total = lax.fori_loop(0, blocks, weighed, jnp.zeros((rows, 1), F32))
        share = jnp.where(place >= 0, 1.0 / total, 0.0)

        def summed(b, carry):
            at = pl.ds(pl.multiple_of(b * WIDE, WIDE), WIDE)
            out_ref[pl.ds(b, 1), :] += jnp.sum(score_s[:, at] * share, axis=0, keepdims=True)
            return carry

        lax.fori_loop(0, blocks, summed, 0)
        return carry

    lax.fori_loop(0, (count + CHUNK - 1) // CHUNK, chunk, 0)


def text_sums(info, text_rows, q2, kv2):
    tokens = kv2.shape[0]
    vmem = pl.BlockSpec(memory_space=pltpu.VMEM)
    return pl.pallas_call(
        text_kernel,
        out_shape=jax.ShapeDtypeStruct((tokens // WIDE, WIDE), F32),
        in_specs=[smem(), smem(), vmem, vmem],
        out_specs=vmem,
        scratch_shapes=[pltpu.VMEM((GROUP * CHUNK, tokens), F32)],
        compiler_params=pltpu.CompilerParams(vmem_limit_bytes=24 << 20),
        cost_estimate=pl.CostEstimate(
            flops=2 * GROUP * CHUNK * tokens * HD,
            transcendentals=GROUP * CHUNK * tokens,
            bytes_accessed=4 * tokens * HD,
        ),
        name="text_sums",
    )(info, text_rows, q2, kv2)


def attend3_kernel(info, q_ref, mine_ref, other_ref, out_ref, q_s, out_s, v_s, bias_s):
    chip, core = info[0], info[1]
    half = mine_ref.shape[0]
    for h in range(GROUP):
        q_s[h] = q_ref[:, h * HD : (h + 1) * HD]
    v_s[:half, :HD] = mine_ref[:, HD:]
    v_s[half:, :HD] = other_ref[:, HD:]
    v_s[:, HD:] = jnp.ones((2 * half, HD), BF)
    row = lax.broadcasted_iota(jnp.int32, (1, half), 1)
    rest = row % PAD
    live = rest < SHARE
    query = lax.broadcasted_iota(jnp.int32, (PAD, half), 0)
    start = chip * PAD
    own = (row - start <= query) & live
    bias_s[:, :half] = jnp.where(own, 0.0, LOW)
    earlier = (row < start + core * PAD) & live
    bias_s[:, half:] = jnp.where(earlier & (query >= 0), 0.0, LOW)

    def heads(h, carry):
        q = q_s[h]
        left = dot_t(q, mine_ref[:, :HD]) + bias_s[:, :half]
        right = dot_t(q, other_ref[:, :HD]) + bias_s[:, half:]
        top = jnp.maximum(
            jnp.max(left, axis=1, keepdims=True), jnp.max(right, axis=1, keepdims=True)
        )
        left = jnp.exp2((left - top) * FACTOR).astype(BF)
        right = jnp.exp2((right - top) * FACTOR).astype(BF)
        total = dot(left, v_s[:half]) + dot(right, v_s[half:])
        out_s[h] = total[:, :HD] / total[:, HD:]
        return carry

    lax.fori_loop(0, GROUP, heads, 0)
    for h in range(GROUP):
        out_ref[:, h * HD : (h + 1) * HD] = out_s[h][:SHARE].astype(BF)


def attend3(info, q3, mine, other):
    vmem = pl.BlockSpec(memory_space=pltpu.VMEM)
    keys = 2 * mine.shape[0]
    return pl.pallas_call(
        attend3_kernel,
        out_shape=jax.ShapeDtypeStruct((SHARE, q3.shape[1]), BF),
        in_specs=[smem(), vmem, vmem, vmem],
        out_specs=vmem,
        scratch_shapes=[
            pltpu.VMEM((GROUP, PAD, HD), BF),
            pltpu.VMEM((GROUP, PAD, HD), F32),
            pltpu.VMEM((keys, 2 * HD), BF),
            pltpu.VMEM((PAD, keys), F32),
        ],
        compiler_params=pltpu.CompilerParams(vmem_limit_bytes=40 << 20),
        cost_estimate=pl.CostEstimate(
            flops=6 * GROUP * PAD * keys * HD,
            transcendentals=GROUP * PAD * keys,
            bytes_accessed=4 * keys * HD,
        ),
        name="attend3",
    )(info, q3, mine, other)


def from_core(x):
    count = lax.axis_size("seq")
    return lax.ppermute(x, "seq", [(i ^ 1, i) for i in range(count)])


def from_head(x, distance):
    count = lax.axis_size("head")
    return lax.ppermute(x, "head", [((i + distance) % count, i) for i in range(count)])


def over_chips(x):
    count = lax.axis_size("seq")
    groups = [[i for i in range(count) if i % 2 == core] for core in range(2)]
    many = jnp.broadcast_to(x[None], (count // 2, *x.shape))
    return lax.all_to_all(many, "seq", 0, 0, axis_index_groups=groups, tiled=True)


def body(
    q2,
    k2,
    v2,
    hidden,
    w_query,
    b_query,
    w_key,
    b_key,
    w_value,
    b_value,
    kept_index,
    block_count,
    text_rows,
):
    rank = lax.axis_index("seq")
    head = lax.axis_index("head")
    seq_count = lax.axis_size("seq")
    head_count = lax.axis_size("head")
    core = rank % 2
    chip = rank // 2
    first = rank * ROWS
    depth = hidden.shape[1]

    kv2 = lax.all_gather(jnp.concatenate([k2, v2], axis=1), "seq", axis=0, tiled=True)

    numbers = jnp.stack([core, first, 0, block_count[0], block_count[1]])
    own, sent = pick_rows(numbers, kept_index, hidden)
    x = own + from_core(sent)
    marks = x[:, depth : depth + 2].astype(jnp.int32)
    positions = marks[:, 0] * 128 + marks[:, 1]
    x = x[:, :depth]
    freqs = 1000000.0 ** (-(jnp.arange(HD // 2, dtype=F32) * 2.0) / HD)
    angles = positions.astype(F32)[:, None] * freqs[None, :]
    cosine, sine = (jnp.cos(angles), jnp.sin(angles))
    cosine = jnp.concatenate([cosine, cosine], axis=1)
    sine = jnp.concatenate([-sine, sine], axis=1)

    distances = (-1, 1, 2)
    pieces = [from_head(x, d) for d in distances]
    weights = (w_query, w_key, w_value)
    partial = project(head[None].astype(jnp.int32), [x], weights, ())
    blocks = jnp.stack([(head + d) % head_count for d in distances]).astype(jnp.int32)
    biases = tuple(b[None, :] for b in (b_query, b_key, b_value))
    q3, kv3 = project(blocks, pieces, weights, (*partial, *biases, cosine, sine))
    mine = over_chips(kv3).reshape(-1, 2 * HD)
    other = from_core(mine)

    low = jnp.sum((text_rows < first).astype(jnp.int32))
    count = jnp.sum((text_rows < first + ROWS).astype(jnp.int32)) - low
    partial_sums = text_sums(jnp.stack([rank, low, count]), text_rows, q2, kv2)
    partial_sums = partial_sums.reshape(seq_count, 1, ROWS)
    many = jnp.broadcast_to(partial_sums, (seq_count, head_count, ROWS))
    many = many.reshape(seq_count * head_count, ROWS)
    arrived = lax.all_to_all(many, ("seq", "head"), 0, 0, tiled=True)
    tokens = seq_count * ROWS
    importance = jnp.sum(arrived, axis=0) * (tokens / (GROUP * head_count * text_rows.shape[0]))

    attn2 = attend(rank[None], q2, kv2)
    attn3 = attend3(jnp.stack([chip, core]), q3, mine, other)
    return (attn2, importance, attn3)


def solution(mesh):
    placed = (
        P("seq", "head"),
        P("seq", "head"),
        P("seq", "head"),
        P("seq", "head"),
        P(None, "head"),
        P("head"),
        P(None, "head"),
        P("head"),
        P(None, "head"),
        P("head"),
        P("seq"),
        P("seq"),
        P(),
    )
    return jax.shard_map(
        body,
        mesh=mesh,
        in_specs=placed,
        out_specs=(P("seq", "head"), P("seq"), P("seq", "head")),
        check_vma=False,
    )
```

```python
import math

import jax
import jax.numpy as jnp
from jax import lax
from jax.experimental import pallas as pl
from jax.experimental.pallas import tpu as pltpu
from jax.sharding import PartitionSpec as P

HD = 128
GROUP = 8
BLOCK = 128
ROWS = 256
SHARE = 132
PAD = 136
WIDE = 2048
TILE = 512
FACTOR = math.log2(math.e) / math.sqrt(HD)
LOW = -1e30
BF = jnp.bfloat16
F32 = jnp.float32


def dot(a, b):
    return jnp.dot(a, b, preferred_element_type=F32)


def dot_t(a, b):
    return lax.dot_general(a, b, (((1,), (1,)), ((), ())), preferred_element_type=F32)


def whole(shape):
    return pl.BlockSpec(shape, lambda *_: (0,) * len(shape))


def smem():
    return pl.BlockSpec(memory_space=pltpu.SMEM)


def pick_kernel(info, index_ref, hidden_ref, own_ref, send_ref):
    core, first, before, live0, live1 = (info[i] for i in range(5))
    count = live0 + live1
    start = jnp.where(core == 0, 0, 2 * SHARE - count)
    lane = lax.broadcasted_iota(jnp.int32, (PAD, ROWS), 1)
    place = lax.broadcasted_iota(jnp.int32, (PAD, ROWS), 0)
    second = lane >= BLOCK
    within = jnp.where(second, lane - BLOCK, lane)
    rank = jnp.where(second, within + live0, within)
    live = within < jnp.where(second, live1, live0)
    row = index_ref[...] + jnp.where(second, BLOCK, 0)
    column = lax.broadcasted_iota(jnp.int32, (PAD, BLOCK), 1)
    for out_ref, base in ((own_ref, SHARE * core), (send_ref, SHARE * (1 - core))):
        wanted = place + (base - start)
        match = (rank == wanted) & live & (place < SHARE)
        source = jnp.sum(jnp.where(match, (row + 1).astype(F32), 0.0), axis=1, keepdims=True)
        source = source.astype(jnp.int32) - 1
        select = jnp.where(lane == source, 1.0, 0.0).astype(BF)
        out_ref[:, : hidden_ref.shape[1]] = dot(select, hidden_ref[...]).astype(BF)
        position = jnp.where(source >= 0, source + first, 0)
        high = jnp.where(column == 0, position >> 7, 0)
        marks = jnp.where(column == 1, position & 127, high)
        out_ref[:, hidden_ref.shape[1] :] = marks.astype(F32).astype(BF)


def pick_rows(info, kept_index, hidden):
    width = hidden.shape[1] + BLOCK
    shape = jax.ShapeDtypeStruct((PAD, width), BF)
    return pl.pallas_call(
        pick_kernel,
        out_shape=(shape, shape),
        in_specs=[smem(), pl.BlockSpec(memory_space=pltpu.VMEM), pl.BlockSpec(memory_space=pltpu.VMEM)],
        out_specs=(pl.BlockSpec(memory_space=pltpu.VMEM),) * 2,
        compiler_params=pltpu.CompilerParams(vmem_limit_bytes=24 << 20),
        cost_estimate=pl.CostEstimate(
            flops=4 * PAD * ROWS * width, transcendentals=0, bytes_accessed=4 * ROWS * width
        ),
        name="pick_rows",
    )(info, kept_index.reshape(1, ROWS), hidden)


def rotated(u, cosine, sine):
    return u * cosine + pltpu.roll(u, HD // 2, 1) * sine


def project_kernel(pieces, last, blocks, *refs):
    x_refs = refs[:pieces]
    wq, wk, wv = refs[pieces : pieces + 3]
    rest = refs[pieces + 3 :]
    if last:
        q_in, kv_in, bq, bk, bv, cosine, sine, q_out, kv_out = rest
        c, s = (cosine[...], sine[...])
    else:
        q_out, kv_out = rest
    depth = x_refs[0].shape[1]

    def product(w, part):
        total = None
        for p in range(pieces):
            at = pl.ds(pl.multiple_of(blocks[p] * depth, depth), depth)
            got = dot(x_refs[p][...], w[at, part])
            total = got if total is None else total + got
        return total

    every = slice(0, HD)
    key, value = (product(wk, every), product(wv, every))
    if last:
        key = key + kv_in[:, :HD] + bk[...]
        kv_out[:, :HD] = rotated(key, c, s).astype(BF)
        kv_out[:, HD:] = (value + kv_in[:, HD:] + bv[...]).astype(BF)
    else:
        kv_out[:, :HD] = key
        kv_out[:, HD:] = value
    columns = wq.shape[1]
    for n in range(0, columns, TILE):
        part = slice(n, n + TILE)
        query = product(wq, part)
        if last:
            query = query + q_in[:, part] + bq[:, part]
            for h in range(0, TILE, HD):
                q_out[:, n + h : n + h + HD] = rotated(query[:, h : h + HD], c, s).astype(BF)
        else:
            q_out[:, part] = query


def project(blocks, xs, weights, extra):
    pieces = len(xs)
    last = bool(extra)
    depth = xs[0].shape[1]
    columns = weights[0].shape[1]
    kind = BF if last else F32
    vmem = pl.BlockSpec(memory_space=pltpu.VMEM)

    def kernel(*refs):
        project_kernel(pieces, last, *refs)

    return pl.pallas_call(
        kernel,
        out_shape=(
            jax.ShapeDtypeStruct((PAD, columns), kind),
            jax.ShapeDtypeStruct((PAD, 2 * HD), kind),
        ),
        in_specs=[smem()] + [vmem] * (pieces + 3 + len(extra)),
        out_specs=(vmem, vmem),
        compiler_params=pltpu.CompilerParams(vmem_limit_bytes=32 << 20),
        cost_estimate=pl.CostEstimate(
            flops=2 * pieces * PAD * depth * (columns + 2 * HD),
            transcendentals=0,
            bytes_accessed=2 * pieces * depth * (columns + 2 * HD),
        ),
        name="project_rest" if last else "project_own",
    )(blocks, *xs, *weights, *extra)


def in_turn(heads, scored, weighed):
    ahead = scored(heads[0])
    for at, h in enumerate(heads):
        scores = ahead
        if at + 1 < len(heads):
            ahead = scored(heads[at + 1])
        weighed(h, scores)


def attend_kernel(heads, info, q_ref, mine_ref, other_ref, *refs):
    out_ref, q_s, top_s, sum_s, k_s, v_s, bias_s = refs[-7:]
    step = pl.program_id(0)
    half = pl.num_programs(0) // 2
    chip, core = info[0], info[1]
    mine = step < half
    at = jnp.where(mine, step, step - half)
    limit = (jnp.where(mine, chip, chip + core)) * ROWS - at * WIDE
    ends = jnp.where(mine, limit + ROWS, limit)

    @pl.when(step == 0)
    def _():
        for h in range(heads):
            q_s[h] = q_ref[:, h * HD : (h + 1) * HD]
        top_s[...] = jnp.full_like(top_s, LOW)
        sum_s[...] = jnp.zeros_like(sum_s)
        v_s[:, HD:] = jnp.ones((WIDE, HD), BF)

    for chosen, ref in ((mine, mine_ref), (jnp.logical_not(mine), other_ref)):

        @pl.when(chosen & (ends > 0))
        def _(ref=ref):
            k_s[...] = ref[:, :HD]
            v_s[:, :HD] = ref[:, HD:]

    def run(masked):
        if masked:
            key = lax.broadcasted_iota(jnp.int32, (ROWS, WIDE), 1)
            query = lax.broadcasted_iota(jnp.int32, (ROWS, WIDE), 0)
            bound = jnp.where(mine, query + 1, 0) + limit
            bias_s[...] = jnp.where(key < bound, 0.0, LOW)

        def scored(h):
            scores = dot_t(q_s[h], k_s[...])
            if masked:
                scores = scores + bias_s[...]
            return scores

        def weighed(h, scores):
            before = top_s[h]
            top = jnp.maximum(before, jnp.max(scores, axis=1, keepdims=True))
            top_s[h] = top
            weights = jnp.exp2((scores - top[:, :1]) * FACTOR).astype(BF)
            fade = jnp.exp2((before - top) * FACTOR)
            fade = jnp.concatenate([fade, fade], axis=1)
            sum_s[h] = sum_s[h] * fade + dot(weights, v_s[...])

        in_turn(range(heads), scored, weighed)

    @pl.when(limit >= WIDE)
    def _():
        run(False)

    @pl.when((limit < WIDE) & (ends > 0))
    def _():
        run(True)

    @pl.when(step == 2 * half - 1)
    def _():
        for h in range(heads):
            total = sum_s[h]
            out_ref[:, h * HD : (h + 1) * HD] = (total[:, :HD] / total[:, HD:]).astype(BF)


def attend(info, q2, mine, other, part=0, parts=1, filled=None):
    tokens = mine.shape[0]
    half = tokens // WIDE
    heads = GROUP // parts
    block = pl.BlockSpec((q2.shape[0], heads * HD), lambda i, info: (0, part))
    spec = pltpu.PrefetchScalarGridSpec(
        num_scalar_prefetch=1,
        grid=(2 * half,),
        in_specs=[
            block,
            pl.BlockSpec((WIDE, 2 * HD), lambda i, info: (jnp.minimum(i, info[0] * ROWS // WIDE), 0)),
            pl.BlockSpec(
                (WIDE, 2 * HD),
                lambda i, info: (jnp.clip(i - half, 0, info[0] * ROWS // WIDE), 0),
            ),
        ]
        + ([] if filled is None else [pl.BlockSpec(memory_space=pl.ANY)]),
        out_specs=block,
        scratch_shapes=[
            pltpu.VMEM((heads, ROWS, HD), BF),
            pltpu.VMEM((heads, ROWS, HD), F32),
            pltpu.VMEM((heads, ROWS, 2 * HD), F32),
            pltpu.VMEM((WIDE, HD), BF),
            pltpu.VMEM((WIDE, 2 * HD), BF),
            pltpu.VMEM((ROWS, WIDE), F32),
        ],
    )

    def kernel(*refs):
        attend_kernel(heads, *refs)

    return pl.pallas_call(
        kernel,
        out_shape=jax.ShapeDtypeStruct(q2.shape, BF),
        grid_spec=spec,
        input_output_aliases={} if filled is None else {4: 0},
        compiler_params=pltpu.CompilerParams(vmem_limit_bytes=40 << 20),
        cost_estimate=pl.CostEstimate(
            flops=12 * heads * ROWS * tokens * HD,
            transcendentals=2 * heads * ROWS * tokens,
            bytes_accessed=8 * tokens * HD,
        ),
        name="attend2",
    )(info, q2, mine, other, *(() if filled is None else (filled,)))


CHUNK = 8
SPAN = 1024


def text_kernel(info, text, q_ref, mine_ref, other_ref, high_ref, low_ref, out_ref, score_s):
    chip, core, low, count = (info[i] for i in range(4))
    first = (2 * chip + core) * ROWS
    half = mine_ref.shape[0]
    blocks = SPAN // ROWS
    parts = (
        (mine_ref, 0, core, chip // blocks + 1),
        (other_ref, half, 1 - core, (chip + core + blocks - 1) // blocks),
    )
    out_ref[...] = jnp.zeros_like(out_ref)
    rows = GROUP * CHUNK

    def chunk(c, carry):
        place = jnp.zeros((CHUNK, ROWS), jnp.int32)
        sub = lax.broadcasted_iota(jnp.int32, (CHUNK, ROWS), 0)
        for i in range(CHUNK):
            n = c * CHUNK + i
            at = text[jnp.minimum(low + n, text.shape[0] - 1)] - first
            place = jnp.where(sub == i, jnp.where(n < count, at, -1), place)
        lane = lax.broadcasted_iota(jnp.int32, (CHUNK, ROWS), 1)
        select = jnp.where(lane == place, 1.0, 0.0).astype(BF)
        picked = dot(select, q_ref[...]).astype(BF)
        queries = jnp.concatenate(
            [picked[:, h * HD : (h + 1) * HD] for h in range(GROUP)], axis=0
        )
        place = jnp.concatenate([place[:, :HD]] * GROUP, axis=0)[:, :1]
        limit = first + jnp.maximum(place, 0)
        lane = lax.broadcasted_iota(jnp.int32, (1, SPAN), 1)
        spread = lane + (lane // ROWS) * ROWS

        top = jnp.full((rows, 1), LOW, F32)
        for ref, offset, parity, steps in parts:

            def scored(b, top, ref=ref, offset=offset, parity=parity):
                keys = ref[pl.ds(pl.multiple_of(b * SPAN, SPAN), SPAN), :HD]
                position = spread + (2 * b * SPAN + parity * ROWS)
                scores = jnp.where(position <= limit, dot_t(queries, keys), LOW)
                score_s[:, pl.ds(pl.multiple_of(offset + b * SPAN, SPAN), SPAN)] = scores
                return jnp.maximum(top, jnp.max(scores, axis=1, keepdims=True))

            top = lax.fori_loop(0, steps, scored, top)
        total = jnp.zeros((rows, 1), F32)
        for _, offset, _, steps in parts:

            def weighed(b, total, offset=offset):
                at = pl.ds(pl.multiple_of(offset + b * SPAN, SPAN), SPAN)
                weights = jnp.exp2((score_s[:, at] - top) * FACTOR)
                score_s[:, at] = weights
                return total + jnp.sum(weights, axis=1, keepdims=True)

            total = lax.fori_loop(0, steps, weighed, total)
        share = jnp.where(place >= 0, 1.0 / total, 0.0)
        for _, offset, parity, steps in parts:

            def summed(b, carry, offset=offset, parity=parity):
                at = pl.ds(pl.multiple_of(offset + b * SPAN, SPAN), SPAN)
                sums = jnp.sum(score_s[:, at] * share, axis=0, keepdims=True)
                for i in range(blocks):
                    to = pl.ds(2 * (b * blocks + i) + parity, 1)
                    out_ref[to, :] += sums[:, i * ROWS : (i + 1) * ROWS]
                return carry

            lax.fori_loop(0, steps, summed, 0)
        return carry

    lax.fori_loop(0, (count + CHUNK - 1) // CHUNK, chunk, 0)
    high = out_ref[...].astype(BF)
    high_ref[...] = high
    low_ref[...] = (out_ref[...] - high.astype(F32)).astype(BF)


def text_sums(info, text_rows, q2, mine, other):
    tokens = 2 * mine.shape[0]
    vmem = pl.BlockSpec(memory_space=pltpu.VMEM)
    return pl.pallas_call(
        text_kernel,
        out_shape=(jax.ShapeDtypeStruct((tokens // ROWS, ROWS), BF),) * 2,
        in_specs=[smem(), smem(), vmem, vmem, vmem],
        out_specs=(vmem, vmem),
        scratch_shapes=[
            pltpu.VMEM((tokens // ROWS, ROWS), F32),
            pltpu.VMEM((GROUP * CHUNK, tokens), F32),
        ],
        compiler_params=pltpu.CompilerParams(vmem_limit_bytes=24 << 20),
        cost_estimate=pl.CostEstimate(
            flops=2 * GROUP * CHUNK * tokens * HD,
            transcendentals=GROUP * CHUNK * tokens,
            bytes_accessed=4 * tokens * HD,
        ),
        name="text_sums",
    )(info, text_rows, q2, mine, other)


def attend3_kernel(info, q_ref, mine_ref, other_ref, out_ref, v_s, bias_s):
    chip, core = info[0], info[1]
    half = mine_ref.shape[0]
    v_s[:half, :HD] = mine_ref[:, HD:]
    v_s[half:, :HD] = other_ref[:, HD:]
    v_s[:, HD:] = jnp.ones((2 * half, HD), BF)
    row = lax.broadcasted_iota(jnp.int32, (1, half), 1)
    rest = row % PAD
    live = rest < SHARE
    query = lax.broadcasted_iota(jnp.int32, (PAD, half), 0)
    start = chip * PAD
    own = (row - start <= query) & live
    bias_s[:, :half] = jnp.where(own, 0.0, LOW)
    earlier = (row < start + core * PAD) & live
    bias_s[:, half:] = jnp.where(earlier & (query >= 0), 0.0, LOW)

    def scored(h):
        q = q_ref[:, h * HD : (h + 1) * HD]
        left = dot_t(q, mine_ref[:, :HD]) + bias_s[:, :half]
        right = dot_t(q, other_ref[:, :HD]) + bias_s[:, half:]
        return left, right

    def weighed(h, scores):
        left, right = scores
        top = jnp.maximum(
            jnp.max(left, axis=1, keepdims=True), jnp.max(right, axis=1, keepdims=True)
        )
        left = jnp.exp2((left - top) * FACTOR).astype(BF)
        right = jnp.exp2((right - top) * FACTOR).astype(BF)
        total = dot(left, v_s[:half]) + dot(right, v_s[half:])
        out = (total[:, :HD] / total[:, HD:]).astype(BF)
        out_ref[:, h * HD : (h + 1) * HD] = out[:SHARE]

    in_turn(range(GROUP), scored, weighed)


def attend3(info, q3, mine, other):
    vmem = pl.BlockSpec(memory_space=pltpu.VMEM)
    keys = 2 * mine.shape[0]
    return pl.pallas_call(
        attend3_kernel,
        out_shape=jax.ShapeDtypeStruct((SHARE, q3.shape[1]), BF),
        in_specs=[smem(), vmem, vmem, vmem],
        out_specs=vmem,
        scratch_shapes=[
            pltpu.VMEM((keys, 2 * HD), BF),
            pltpu.VMEM((PAD, keys), F32),
        ],
        compiler_params=pltpu.CompilerParams(vmem_limit_bytes=40 << 20),
        cost_estimate=pl.CostEstimate(
            flops=6 * GROUP * PAD * keys * HD,
            transcendentals=GROUP * PAD * keys,
            bytes_accessed=4 * keys * HD,
        ),
        name="attend3",
    )(info, q3, mine, other)


def from_core(x):
    count = lax.axis_size("seq")
    return lax.ppermute(x, "seq", [(i ^ 1, i) for i in range(count)])


def from_head(x, distance):
    count = lax.axis_size("head")
    return lax.ppermute(x, "head", [((i + distance) % count, i) for i in range(count)])


def over_chips(many):
    count = lax.axis_size("seq")
    groups = [[i for i in range(count) if i % 2 == core] for core in range(2)]
    return lax.all_to_all(many, "seq", 0, 0, axis_index_groups=groups, tiled=True)


def over_heads(x):
    count = lax.axis_size("head")
    step = 1
    while step < count:
        x = x + lax.ppermute(x, "head", [(i ^ step, i) for i in range(count)])
        step *= 2
    return x


def body(
    q2,
    k2,
    v2,
    hidden,
    w_query,
    b_query,
    w_key,
    b_key,
    w_value,
    b_value,
    kept_index,
    block_count,
    text_rows,
):
    rank = lax.axis_index("seq")
    head = lax.axis_index("head")
    seq_count = lax.axis_size("seq")
    head_count = lax.axis_size("head")
    core = rank % 2
    chip = rank // 2
    first = rank * ROWS
    depth = hidden.shape[1]

    chips = seq_count // 2
    kv2 = jnp.concatenate([k2, v2], axis=1)
    mine2 = over_chips(jnp.broadcast_to(kv2[None], (chips, *kv2.shape)))
    mine2 = mine2.reshape(-1, 2 * HD)

    numbers = jnp.stack([core, first, 0, block_count[0], block_count[1]])
    own, sent = pick_rows(numbers, kept_index, hidden)
    x = own + from_core(sent)
    marks = x[:, depth : depth + 2].astype(jnp.int32)
    positions = marks[:, 0] * 128 + marks[:, 1]
    x = x[:, :depth]
    freqs = 1000000.0 ** (-(jnp.arange(HD // 2, dtype=F32) * 2.0) / HD)
    angles = positions.astype(F32)[:, None] * freqs[None, :]
    cosine, sine = (jnp.cos(angles), jnp.sin(angles))
    cosine = jnp.concatenate([cosine, cosine], axis=1)
    sine = jnp.concatenate([-sine, sine], axis=1)

    distances = (-1, 1, 2)
    pieces = [from_head(x, d) for d in distances]
    weights = (w_query, w_key, w_value)
    partial = project(head[None].astype(jnp.int32), [x], weights, ())
    mine2, pieces, partial = lax.optimization_barrier((mine2, pieces, partial))
    other2 = from_core(mine2)
    blocks = jnp.stack([(head + d) % head_count for d in distances]).astype(jnp.int32)
    biases = tuple(b[None, :] for b in (b_query, b_key, b_value))
    q3, kv3 = project(blocks, pieces, weights, (*partial, *biases, cosine, sine))
    kv3, other2 = lax.optimization_barrier((kv3, other2))
    low = jnp.sum((text_rows < first).astype(jnp.int32))
    count = jnp.sum((text_rows < first + ROWS).astype(jnp.int32)) - low
    place = jnp.stack([chip, core])
    sums = text_sums(jnp.stack([chip, core, low, count]), text_rows, q2, mine2, other2)

    sums = [part.reshape(chips, 2, ROWS) for part in sums]
    kept = jnp.broadcast_to(kv3[None, :SHARE], (chips, SHARE, 2 * HD))
    many = jnp.concatenate([kept, *sums], axis=1)
    mine = over_chips(many)
    q2, many = lax.optimization_barrier((q2, many))
    attn2 = attend(place, q2, mine2, other2)
    attn2, mine = lax.optimization_barrier((attn2, mine))
    other = from_core(mine)
    attn3 = attend3(place, q3, mine.reshape(-1, 2 * HD), other.reshape(-1, 2 * HD))

    got = sum(jnp.sum(x[:, SHARE:].astype(F32), axis=0) for x in (mine, other))
    got = got[:2] + got[2:]
    got = over_heads(jnp.where(core == 0, got[0], got[1]))
    tokens = seq_count * ROWS
    importance = got * (tokens / (GROUP * head_count * text_rows.shape[0]))
    return (attn2, importance, attn3)


def solution(mesh):
    placed = (
        P("seq", "head"),
        P("seq", "head"),
        P("seq", "head"),
        P("seq", "head"),
        P(None, "head"),
        P("head"),
        P(None, "head"),
        P("head"),
        P(None, "head"),
        P("head"),
        P("seq"),
        P("seq"),
        P(),
    )
    return jax.shard_map(
        body,
        mesh=mesh,
        in_specs=placed,
        out_specs=(P("seq", "head"), P("seq"), P("seq", "head")),
        check_vma=False,
    )
```

```python
import math

import jax
import jax.numpy as jnp
from jax import lax
from jax.experimental import pallas as pl
from jax.experimental.pallas import tpu as pltpu
from jax.sharding import PartitionSpec as P

HD = 128
GROUP = 8
BLOCK = 128
ROWS = 256
SHARE = 132
PAD = 136
PART = ROWS // 2
WIDE = 1024
FACTOR = math.log2(math.e) / math.sqrt(HD)
LOW = -1e30
BF = jnp.bfloat16
F32 = jnp.float32


def dot(a, b):
    return jnp.dot(a, b, preferred_element_type=F32)


def dot_t(a, b):
    return lax.dot_general(a, b, (((1,), (1,)), ((), ())), preferred_element_type=F32)


def whole(shape):
    return pl.BlockSpec(shape, lambda *_: (0,) * len(shape))


def smem():
    return pl.BlockSpec(memory_space=pltpu.SMEM)


def pick_kernel(info, index_ref, hidden_ref, own_ref, send_ref):
    core, first, before, live0, live1 = (info[i] for i in range(5))
    count = live0 + live1
    start = jnp.where(core == 0, 0, 2 * SHARE - count)
    lane = lax.broadcasted_iota(jnp.int32, (PAD, ROWS), 1)
    place = lax.broadcasted_iota(jnp.int32, (PAD, ROWS), 0)
    second = lane >= BLOCK
    within = jnp.where(second, lane - BLOCK, lane)
    rank = jnp.where(second, within + live0, within)
    live = within < jnp.where(second, live1, live0)
    row = index_ref[...] + jnp.where(second, BLOCK, 0)
    column = lax.broadcasted_iota(jnp.int32, (PAD, BLOCK), 1)
    for out_ref, base in ((own_ref, SHARE * core), (send_ref, SHARE * (1 - core))):
        wanted = place + (base - start)
        match = (rank == wanted) & live & (place < SHARE)
        source = jnp.sum(jnp.where(match, (row + 1).astype(F32), 0.0), axis=1, keepdims=True)
        source = source.astype(jnp.int32) - 1
        select = jnp.where(lane == source, 1.0, 0.0).astype(BF)
        out_ref[:, : hidden_ref.shape[1]] = dot(select, hidden_ref[...]).astype(BF)
        position = jnp.where(source >= 0, source + first, 0)
        high = jnp.where(column == 0, position >> 7, 0)
        marks = jnp.where(column == 1, position & 127, high)
        out_ref[:, hidden_ref.shape[1] :] = marks.astype(F32).astype(BF)


def pick_rows(info, kept_index, hidden):
    width = hidden.shape[1] + BLOCK
    shape = jax.ShapeDtypeStruct((PAD, width), BF)
    return pl.pallas_call(
        pick_kernel,
        out_shape=(shape, shape),
        in_specs=[smem(), pl.BlockSpec(memory_space=pltpu.VMEM), pl.BlockSpec(memory_space=pltpu.VMEM)],
        out_specs=(pl.BlockSpec(memory_space=pltpu.VMEM),) * 2,
        compiler_params=pltpu.CompilerParams(vmem_limit_bytes=24 << 20),
        cost_estimate=pl.CostEstimate(
            flops=4 * PAD * ROWS * width, transcendentals=0, bytes_accessed=4 * ROWS * width
        ),
        name="pick_rows",
    )(info, kept_index.reshape(1, ROWS), hidden)


def rotated(u, cosine, sine):
    return u * cosine + pltpu.roll(u, HD // 2, 1) * sine


STEP = 1024


def project_kernel(pieces, last, blocks, *refs):
    x_refs = refs[:pieces]
    wq, wk, wv = refs[pieces : pieces + 3]
    rest = refs[pieces + 3 :]
    if last:
        q_in, kv_in, bq, bk, bv, cosine, sine, q_out, kv_out, q_acc, kv_acc = rest
    else:
        q_acc, kv_acc = rest
    step = pl.program_id(0)
    splits = pl.num_programs(0) // pieces
    for p in range(pieces):
        for part in range(splits):

            @pl.when(step == p * splits + part)
            def _(p=p, part=part):
                x = x_refs[p][:, part * STEP : (part + 1) * STEP]
                got = (dot(x, wq[...]), dot(x, wk[...]), dot(x, wv[...]))
                if p + part > 0:
                    held = (q_acc[...], kv_acc[:, :HD], kv_acc[:, HD:])
                elif last:
                    held = (q_in[...], kv_in[:, :HD], kv_in[:, HD:])
                else:
                    held = (0.0, 0.0, 0.0)
                q, k, v = (new + old for new, old in zip(got, held))
                if last and p == pieces - 1 and part == splits - 1:
                    c, s = (cosine[...], sine[...])
                    for h in range(GROUP):
                        at = slice(h * HD, (h + 1) * HD)
                        q_out[:, at] = rotated(q[:, at] + bq[:, at], c, s).astype(BF)
                    kv_out[:, :HD] = rotated(k + bk[...], c, s).astype(BF)
                    kv_out[:, HD:] = (v + bv[...]).astype(BF)
                else:
                    q_acc[...] = q
                    kv_acc[:, :HD] = k
                    kv_acc[:, HD:] = v


def project(blocks, xs, weights, extra):
    pieces = len(xs)
    last = bool(extra)
    depth = xs[0].shape[1]
    splits = depth // STEP
    columns = weights[0].shape[1]
    kind = BF if last else F32

    def weight(width):
        return pl.BlockSpec((STEP, width), lambda i, b: (b[i // splits] * splits + i % splits, 0))

    def kernel(*refs):
        project_kernel(pieces, last, *refs)

    outs = ((PAD, columns), (PAD, 2 * HD))
    spec = pltpu.PrefetchScalarGridSpec(
        num_scalar_prefetch=1,
        grid=(pieces * splits,),
        in_specs=[whole(x.shape) for x in xs]
        + [weight(w.shape[1]) for w in weights]
        + [whole(e.shape) for e in extra],
        out_specs=tuple(whole(o) for o in outs),
        scratch_shapes=[pltpu.VMEM(o, F32) for o in outs] if last else [],
    )
    weights = [pltpu.with_memory_space_constraint(w, pltpu.HBM) for w in weights]
    return pl.pallas_call(
        kernel,
        out_shape=tuple(jax.ShapeDtypeStruct(o, kind) for o in outs),
        grid_spec=spec,
        compiler_params=pltpu.CompilerParams(vmem_limit_bytes=24 << 20),
        cost_estimate=pl.CostEstimate(
            flops=2 * pieces * PAD * depth * (columns + 2 * HD),
            transcendentals=0,
            bytes_accessed=2 * pieces * depth * (columns + 2 * HD),
        ),
        name="project_rest" if last else "project_own",
    )(blocks, *xs, *weights, *extra)


def in_turn(heads, scored, weighed):
    ahead = scored(heads[0])
    for at, h in enumerate(heads):
        scores = ahead
        if at + 1 < len(heads):
            ahead = scored(heads[at + 1])
        weighed(h, scores)


def attend_kernel(info, own_ref, far_ref, mine_ref, other_ref, *refs):
    own_out, far_out, q_s, top_s, sum_s, v_s, bias_s = refs
    core = info[2]
    half = mine_ref.shape[0]
    pairs = GROUP // 2
    for g, ref in enumerate((own_ref, far_ref)):
        for h in range(GROUP):
            to = (h % 2) * PART
            q_s[g, h // 2, to : to + PART] = ref[:, h * HD : (h + 1) * HD]
    top_s[...] = jnp.full_like(top_s, LOW)
    sum_s[...] = jnp.zeros_like(sum_s)
    for p, ref in enumerate((mine_ref, other_ref)):
        v_s[p, :, :HD] = ref[:, HD:]
    v_s[:, :, HD:] = jnp.ones((2, half, HD), BF)

    def step(g, p, ref, b, bound):
        at = pl.ds(pl.multiple_of(b * WIDE, WIDE), WIDE)
        keys = ref[at, :HD]
        values = v_s[p, at, :]
        if bound is not None:
            key = lax.broadcasted_iota(jnp.int32, (PART, WIDE), 1)
            query = lax.broadcasted_iota(jnp.int32, (PART, WIDE), 0)
            bias = jnp.where(key + b * WIDE < bound[0] + bound[1] * query, 0.0, LOW)
            bias_s[:PART] = bias
            bias_s[PART:] = bias

        def scored(h):
            scores = dot_t(q_s[g, h], keys)
            return scores if bound is None else scores + bias_s[...]

        def weighed(h, scores):
            before = top_s[g, h]
            top = jnp.maximum(before, jnp.max(scores, axis=1, keepdims=True))
            top_s[g, h] = top
            weights = jnp.exp2((scores - top[:, :1]) * FACTOR).astype(BF)
            fade = jnp.exp2((before - top) * FACTOR)
            fade = jnp.concatenate([fade, fade], axis=1)
            sum_s[g, h] = sum_s[g, h] * fade + dot(weights, values)

        in_turn(range(pairs), scored, weighed)

    def group(g, carry):
        chip, side = info[2 * g + 1], info[2 * g + 2]
        for p, ref in enumerate((mine_ref, other_ref)):
            parity = core if p == 0 else 1 - core
            same = jnp.where(parity == side, 1, 0)
            before = (chip + jnp.where(parity < side, 1, 0)) * ROWS
            whole_steps = before // WIDE

            def plain(b, carry, p=p, ref=ref):
                step(g, p, ref, b, None)
                return carry

            lax.fori_loop(0, whole_steps, plain, 0)

            @pl.when((before % WIDE > 0) | (same > 0))
            def _(p=p, ref=ref):
                step(g, p, ref, whole_steps, (before + same * (PART * g + 1), same))

        return carry

    lax.fori_loop(0, 2, group, 0)
    for g, ref in enumerate((own_out, far_out)):
        for h in range(GROUP):
            total = sum_s[g, h // 2, (h % 2) * PART : (h % 2) * PART + PART]
            ref[:, h * HD : (h + 1) * HD] = (total[:, :HD] / total[:, HD:]).astype(BF)


def attend(info, own, far, mine, other):
    tokens = 2 * mine.shape[0]
    vmem = pl.BlockSpec(memory_space=pltpu.VMEM)
    out = jax.ShapeDtypeStruct(own.shape, BF)
    return pl.pallas_call(
        attend_kernel,
        out_shape=(out, out),
        in_specs=[smem(), vmem, vmem, vmem, vmem],
        out_specs=(vmem, vmem),
        scratch_shapes=[
            pltpu.VMEM((2, GROUP // 2, 2 * PART, HD), BF),
            pltpu.VMEM((2, GROUP // 2, 2 * PART, HD), F32),
            pltpu.VMEM((2, GROUP // 2, 2 * PART, 2 * HD), F32),
            pltpu.VMEM((2, tokens // 2, 2 * HD), BF),
            pltpu.VMEM((2 * PART, WIDE), F32),
        ],
        compiler_params=pltpu.CompilerParams(vmem_limit_bytes=40 << 20),
        cost_estimate=pl.CostEstimate(
            flops=4 * GROUP * PART * tokens * HD,
            transcendentals=GROUP * PART * tokens,
            bytes_accessed=4 * tokens * HD,
        ),
        name="attend2",
    )(info, own, far, mine, other)


CHUNK = 8


def text_kernel(info, text, q_ref, mine_ref, other_ref, high_ref, low_ref, out_ref):
    chip, core, low, count = (info[i] for i in range(4))
    first = (2 * chip + core) * ROWS
    half = mine_ref.shape[0]
    out_ref[...] = jnp.zeros_like(out_ref)
    rows = GROUP * CHUNK

    def chunk(c, carry):
        place = jnp.zeros((CHUNK, ROWS), jnp.int32)
        sub = lax.broadcasted_iota(jnp.int32, (CHUNK, ROWS), 0)
        for i in range(CHUNK):
            n = c * CHUNK + i
            at = text[jnp.minimum(low + n, text.shape[0] - 1)] - first
            place = jnp.where(sub == i, jnp.where(n < count, at, -1), place)
        lane = lax.broadcasted_iota(jnp.int32, (CHUNK, ROWS), 1)
        select = jnp.where(lane == place, 1.0, 0.0).astype(BF)
        picked = dot(select, q_ref[...]).astype(BF)
        queries = jnp.concatenate(
            [picked[:, h * HD : (h + 1) * HD] for h in range(GROUP)], axis=0
        )
        place = jnp.concatenate([place[:, :HD]] * GROUP, axis=0)[:, :1]
        limit = first + jnp.maximum(place, 0)
        lane = lax.broadcasted_iota(jnp.int32, (1, half), 1)
        spread = lane + (lane // ROWS) * ROWS
        parts = []
        for ref, parity in ((mine_ref, core), (other_ref, 1 - core)):
            live = spread + parity * ROWS <= limit
            parts.append(jnp.where(live, dot_t(queries, ref[:, :HD]), LOW))
        top = jnp.maximum(*(jnp.max(x, axis=1, keepdims=True) for x in parts))
        parts = [jnp.exp2((x - top) * FACTOR) for x in parts]
        total = sum(jnp.sum(x, axis=1, keepdims=True) for x in parts)
        share = jnp.where(place >= 0, 1.0 / total, 0.0)
        for p, x in enumerate(parts):
            out_ref[p : p + 1, :] += jnp.sum(x * share, axis=0, keepdims=True)
        return carry

    lax.fori_loop(0, (count + CHUNK - 1) // CHUNK, chunk, 0)
    mine, other = (out_ref[0:1, :], out_ref[1:2, :])
    even, odd = (jnp.where(core == 0, mine, other), jnp.where(core == 0, other, mine))
    for p, x in enumerate((even, odd)):
        high = x.astype(BF)
        high_ref[p : p + 1, :] = high
        low_ref[p : p + 1, :] = (x - high.astype(F32)).astype(BF)


def text_sums(info, text_rows, q2, mine, other):
    tokens = 2 * mine.shape[0]
    vmem = pl.BlockSpec(memory_space=pltpu.VMEM)
    return pl.pallas_call(
        text_kernel,
        out_shape=(jax.ShapeDtypeStruct((2, tokens // 2), BF),) * 2,
        in_specs=[smem(), smem(), vmem, vmem, vmem],
        out_specs=(vmem, vmem),
        scratch_shapes=[pltpu.VMEM((2, tokens // 2), F32)],
        compiler_params=pltpu.CompilerParams(vmem_limit_bytes=24 << 20),
        cost_estimate=pl.CostEstimate(
            flops=2 * GROUP * CHUNK * tokens * HD,
            transcendentals=GROUP * CHUNK * tokens,
            bytes_accessed=4 * tokens * HD,
        ),
        name="text_sums",
    )(info, text_rows, q2, mine, other)


def attend3_kernel(info, q_ref, mine_ref, other_ref, out_ref, v_s, bias_s):
    chip, core = info[0], info[1]
    half = mine_ref.shape[0]
    v_s[:half, :HD] = mine_ref[:, HD:]
    v_s[half:, :HD] = other_ref[:, HD:]
    v_s[:, HD:] = jnp.ones((2 * half, HD), BF)
    row = lax.broadcasted_iota(jnp.int32, (1, half), 1)
    rest = row % PAD
    live = rest < SHARE
    query = lax.broadcasted_iota(jnp.int32, (PAD, half), 0)
    start = chip * PAD
    own = (row - start <= query) & live
    bias_s[:, :half] = jnp.where(own, 0.0, LOW)
    earlier = (row < start + core * PAD) & live
    bias_s[:, half:] = jnp.where(earlier & (query >= 0), 0.0, LOW)

    def scored(h):
        q = q_ref[:, h * HD : (h + 1) * HD]
        left = dot_t(q, mine_ref[:, :HD]) + bias_s[:, :half]
        right = dot_t(q, other_ref[:, :HD]) + bias_s[:, half:]
        return left, right

    def weighed(h, scores):
        left, right = scores
        top = jnp.maximum(
            jnp.max(left, axis=1, keepdims=True), jnp.max(right, axis=1, keepdims=True)
        )
        left = jnp.exp2((left - top) * FACTOR).astype(BF)
        right = jnp.exp2((right - top) * FACTOR).astype(BF)
        total = dot(left, v_s[:half]) + dot(right, v_s[half:])
        out = (total[:, :HD] / total[:, HD:]).astype(BF)
        out_ref[:, h * HD : (h + 1) * HD] = out[:SHARE]

    in_turn(range(GROUP), scored, weighed)


def attend3(info, q3, mine, other):
    vmem = pl.BlockSpec(memory_space=pltpu.VMEM)
    keys = 2 * mine.shape[0]
    return pl.pallas_call(
        attend3_kernel,
        out_shape=jax.ShapeDtypeStruct((SHARE, q3.shape[1]), BF),
        in_specs=[smem(), vmem, vmem, vmem],
        out_specs=vmem,
        scratch_shapes=[
            pltpu.VMEM((keys, 2 * HD), BF),
            pltpu.VMEM((PAD, keys), F32),
        ],
        compiler_params=pltpu.CompilerParams(vmem_limit_bytes=40 << 20),
        cost_estimate=pl.CostEstimate(
            flops=6 * GROUP * PAD * keys * HD,
            transcendentals=GROUP * PAD * keys,
            bytes_accessed=4 * keys * HD,
        ),
        name="attend3",
    )(info, q3, mine, other)


def from_core(x):
    count = lax.axis_size("seq")
    return lax.ppermute(x, "seq", [(i ^ 1, i) for i in range(count)])


def from_head(x, distance):
    count = lax.axis_size("head")
    return lax.ppermute(x, "head", [((i + distance) % count, i) for i in range(count)])


def over_chips(many):
    count = lax.axis_size("seq")
    groups = [[i for i in range(count) if i % 2 == core] for core in range(2)]
    return lax.all_to_all(many, "seq", 0, 0, axis_index_groups=groups, tiled=True)


def over_heads(x):
    count = lax.axis_size("head")
    return [x] + [
        lax.ppermute(x, "head", [(i ^ step, i) for i in range(count)]) for step in range(1, count)
    ]


def from_partner(x):
    count = lax.axis_size("seq")
    return lax.ppermute(x, "seq", [(count - 1 - i, i) for i in range(count)])


def body(
    q2,
    k2,
    v2,
    hidden,
    w_query,
    b_query,
    w_key,
    b_key,
    w_value,
    b_value,
    kept_index,
    block_count,
    text_rows,
):
    rank = lax.axis_index("seq")
    head = lax.axis_index("head")
    seq_count = lax.axis_size("seq")
    head_count = lax.axis_size("head")
    core = rank % 2
    chip = rank // 2
    first = rank * ROWS
    depth = hidden.shape[1]

    chips = seq_count // 2
    kv2 = jnp.concatenate([k2, v2], axis=1)
    mine2 = over_chips(jnp.broadcast_to(kv2[None], (chips, *kv2.shape)))
    mine2 = mine2.reshape(-1, 2 * HD)

    numbers = jnp.stack([core, first, 0, block_count[0], block_count[1]])
    own, sent = pick_rows(numbers, kept_index, hidden)
    x = own + from_core(sent)
    marks = x[:, depth : depth + 2].astype(jnp.int32)
    positions = marks[:, 0] * 128 + marks[:, 1]
    x = x[:, :depth]
    freqs = 1000000.0 ** (-(jnp.arange(HD // 2, dtype=F32) * 2.0) / HD)
    angles = positions.astype(F32)[:, None] * freqs[None, :]
    cosine, sine = (jnp.cos(angles), jnp.sin(angles))
    cosine = jnp.concatenate([cosine, cosine], axis=1)
    sine = jnp.concatenate([-sine, sine], axis=1)

    distances = (-1, 1, 2)
    pieces = [from_head(x, d) for d in distances]
    weights = (w_query, w_key, w_value)
    partial = project(head[None].astype(jnp.int32), [x], weights, ())
    low = jnp.sum((text_rows < first).astype(jnp.int32))
    count = jnp.sum((text_rows < first + ROWS).astype(jnp.int32)) - low
    partner = seq_count - 1 - rank
    place = jnp.stack([0, chip, core, partner // 2, partner % 2])
    text_info = jnp.stack([chip, core, low, count])
    far = from_partner(q2[PART:])
    blocks = jnp.stack([(head + d) % head_count for d in distances]).astype(jnp.int32)
    biases = tuple(b[None, :] for b in (b_query, b_key, b_value))
    mine2, pieces, far, *ready = lax.optimization_barrier(
        (mine2, pieces, far, *partial, *biases, cosine, sine, place, text_info, blocks)
    )
    *ready, place, text_info, blocks = ready
    other2 = from_core(mine2)
    q3, kv3 = project(blocks, pieces, weights, ready)
    kv3, other2 = lax.optimization_barrier((kv3, other2))
    sums = text_sums(text_info, text_rows, q2, mine2, other2)

    sums = [part.reshape(2, chips, ROWS).swapaxes(0, 1) for part in sums]
    kept = jnp.broadcast_to(kv3[None, :SHARE], (chips, SHARE, 2 * HD))
    many = jnp.concatenate([kept, *sums], axis=1)
    mine = over_chips(many)
    far, many = lax.optimization_barrier((far, many))
    near, far = attend(place, q2[:PART], far, mine2, other2)
    far, mine = lax.optimization_barrier((far, mine))
    other = from_core(mine)
    far = from_partner(far)

    got = sum(jnp.sum(x[:, SHARE:].astype(F32), axis=0) for x in (mine, other))
    got = got[:2] + got[2:]
    got = over_heads(jnp.where(core == 0, got[0], got[1]))
    attn3 = attend3(place[1:3], q3, mine.reshape(-1, 2 * HD), other.reshape(-1, 2 * HD))
    attn3, far, *got = lax.optimization_barrier((attn3, far, *got))
    attn2 = jnp.concatenate([near, far], axis=0)
    tokens = seq_count * ROWS
    importance = (got[0] + got[1]) + (got[2] + got[3])
    importance = importance * (tokens / (GROUP * head_count * text_rows.shape[0]))
    return (attn2, importance, attn3)


def solution(mesh):
    placed = (
        P("seq", "head"),
        P("seq", "head"),
        P("seq", "head"),
        P("seq", "head"),
        P(None, "head"),
        P("head"),
        P(None, "head"),
        P("head"),
        P(None, "head"),
        P("head"),
        P("seq"),
        P("seq"),
        P(),
    )
    return jax.shard_map(
        body,
        mesh=mesh,
        in_specs=placed,
        out_specs=(P("seq", "head"), P("seq"), P("seq", "head")),
        check_vma=False,
    )
```

```python
import math

import jax
import jax.numpy as jnp
from jax import lax
from jax.experimental import pallas as pl
from jax.experimental.pallas import tpu as pltpu
from jax.sharding import PartitionSpec as P

HD = 128
GROUP = 8
BLOCK = 128
ROWS = 256
SHARE = 132
PAD = 136
PART = ROWS // 2
WIDE = 1024
FACTOR = math.log2(math.e) / math.sqrt(HD)
LOW = -1e30
BF = jnp.bfloat16
F32 = jnp.float32


def dot(a, b):
    return jnp.dot(a, b, preferred_element_type=F32)


def dot_t(a, b):
    return lax.dot_general(a, b, (((1,), (1,)), ((), ())), preferred_element_type=F32)


def whole(shape):
    return pl.BlockSpec(shape, lambda *_: (0,) * len(shape))


def smem():
    return pl.BlockSpec(memory_space=pltpu.SMEM)


def pick_kernel(info, index_ref, hidden_ref, own_ref, send_ref):
    core, first, before, live0, live1 = (info[i] for i in range(5))
    count = live0 + live1
    start = jnp.where(core == 0, 0, 2 * SHARE - count)
    lane = lax.broadcasted_iota(jnp.int32, (PAD, ROWS), 1)
    place = lax.broadcasted_iota(jnp.int32, (PAD, ROWS), 0)
    second = lane >= BLOCK
    within = jnp.where(second, lane - BLOCK, lane)
    rank = jnp.where(second, within + live0, within)
    live = within < jnp.where(second, live1, live0)
    row = index_ref[...] + jnp.where(second, BLOCK, 0)
    column = lax.broadcasted_iota(jnp.int32, (PAD, BLOCK), 1)
    for out_ref, base in ((own_ref, SHARE * core), (send_ref, SHARE * (1 - core))):
        wanted = place + (base - start)
        match = (rank == wanted) & live & (place < SHARE)
        source = jnp.sum(jnp.where(match, (row + 1).astype(F32), 0.0), axis=1, keepdims=True)
        source = source.astype(jnp.int32) - 1
        select = jnp.where(lane == source, 1.0, 0.0).astype(BF)
        out_ref[:, : hidden_ref.shape[1]] = dot(select, hidden_ref[...]).astype(BF)
        position = jnp.where(source >= 0, source + first, 0)
        high = jnp.where(column == 0, position >> 7, 0)
        marks = jnp.where(column == 1, position & 127, high)
        out_ref[:, hidden_ref.shape[1] :] = marks.astype(F32).astype(BF)


def pick_rows(info, kept_index, hidden):
    width = hidden.shape[1] + BLOCK
    shape = jax.ShapeDtypeStruct((PAD, width), BF)
    return pl.pallas_call(
        pick_kernel,
        out_shape=(shape, shape),
        in_specs=[smem(), pl.BlockSpec(memory_space=pltpu.VMEM), pl.BlockSpec(memory_space=pltpu.VMEM)],
        out_specs=(pl.BlockSpec(memory_space=pltpu.VMEM),) * 2,
        compiler_params=pltpu.CompilerParams(vmem_limit_bytes=16 << 20),
        cost_estimate=pl.CostEstimate(
            flops=4 * PAD * ROWS * width, transcendentals=0, bytes_accessed=4 * ROWS * width
        ),
        name="pick_rows",
    )(info, kept_index.reshape(1, ROWS), hidden)


def rotated(u, cosine, sine):
    return u * cosine + pltpu.roll(u, HD // 2, 1) * sine


STEP = 1024


def project_kernel(pieces, first, last, blocks, *refs):
    x_refs = refs[:pieces]
    weights = refs[pieces : pieces + 3]
    rest = refs[pieces + 3 :]
    if not first:
        before = rest[:2]
        rest = rest[2:]
    if last:
        bq, bk, bv, cosine, sine = rest[:5]
        rest = rest[5:]
    q_to, kv_out, *held, kv_s, q_s, q_out, sems, part_sems = rest
    sums = (q_s, kv_s)
    loads = []
    if not first:
        loads = [
            pltpu.make_async_copy(x, to, part_sems.at[i])
            for i, (x, to) in enumerate(zip(before, sums))
        ]
    depth = x_refs[0].shape[1]
    copies = []
    for p in range(pieces):
        for part in range(depth // STEP):
            at = len(copies) * STEP
            start = pl.multiple_of(blocks[p] * depth + part * STEP, STEP)
            copies.append(
                [
                    pltpu.make_async_copy(
                        w.at[pl.ds(start, STEP), :], to.at[at : at + STEP, :], sems.at[len(copies), i]
                    )
                    for i, (w, to) in enumerate(zip(weights, held))
                ]
            )
    for group in [*copies, loads]:
        for copy in group:
            copy.start()
    totals = [0.0, 0.0, 0.0]
    for n, group in enumerate(copies):
        p, part = divmod(n, depth // STEP)
        x = x_refs[p][:, part * STEP : (part + 1) * STEP]
        for copy in group:
            copy.wait()
        at = slice(n * STEP, (n + 1) * STEP)
        totals = [old + dot(x, w[at, :]) for old, w in zip(totals, held)]
    for copy in loads:
        copy.wait()
    q, k, v = totals
    if not first:
        q, k, v = (q + q_s[...], k + kv_s[:, :HD], v + kv_s[:, HD:])
    if last:
        c, s = (cosine[...], sine[...])
        for h in range(GROUP):
            at = slice(h * HD, (h + 1) * HD)
            q_out[:, at] = rotated(q[:, at] + bq[:, at], c, s).astype(BF)
        kv_out[:, :HD] = rotated(k + bk[...], c, s).astype(BF)
        kv_out[:, HD:] = (v + bv[...]).astype(BF)
        stores = [pltpu.make_async_copy(q_out, q_to, part_sems.at[2])]
    else:
        q_out[...] = q
        kv_s[:, :HD] = k
        kv_s[:, HD:] = v
        stores = [
            pltpu.make_async_copy(q_out, q_to, part_sems.at[2]),
            pltpu.make_async_copy(kv_s, kv_out, part_sems.at[3]),
        ]
    for copy in stores:
        copy.start()
    for copy in stores:
        copy.wait()


def project(blocks, xs, weights, partial=(), finish=()):
    pieces = len(xs)
    depth = xs[0].shape[1]
    widths = [w.shape[1] for w in weights]
    kind = BF if finish else F32
    vmem = pl.BlockSpec(memory_space=pltpu.VMEM)
    weights = [pltpu.with_memory_space_constraint(w, pltpu.HBM) for w in weights]
    hbm = pl.BlockSpec(memory_space=pl.ANY)
    partial = [pltpu.with_memory_space_constraint(part, pltpu.HBM) for part in partial]

    def kernel(*refs):
        project_kernel(pieces, not partial, bool(finish), *refs)

    outs = ((PAD, widths[0]), (PAD, 2 * HD))
    return pl.pallas_call(
        kernel,
        out_shape=(
            pltpu.HBM(outs[0], kind),
            jax.ShapeDtypeStruct(outs[1], kind) if finish else pltpu.HBM(outs[1], kind),
        ),
        in_specs=[smem()]
        + [vmem] * pieces
        + [hbm] * (3 + len(partial))
        + [vmem] * len(finish),
        out_specs=(hbm, vmem if finish else hbm),
        scratch_shapes=[pltpu.VMEM((pieces * depth, width), BF) for width in widths]
        + [
            pltpu.VMEM(outs[1], F32),
            pltpu.VMEM(outs[0], F32),
            pltpu.VMEM(outs[0], kind),
            pltpu.SemaphoreType.DMA((pieces * depth // STEP, 3)),
            pltpu.SemaphoreType.DMA((4,)),
        ],
        compiler_params=pltpu.CompilerParams(vmem_limit_bytes=28 << 20),
        cost_estimate=pl.CostEstimate(
            flops=2 * pieces * PAD * depth * sum(widths),
            transcendentals=0,
            bytes_accessed=2 * pieces * depth * sum(widths),
        ),
        name="project",
    )(blocks, *xs, *weights, *partial, *finish)


def in_turn(heads, scored, weighed):
    ahead = scored(heads[0])
    for at, h in enumerate(heads):
        scores = ahead
        if at + 1 < len(heads):
            ahead = scored(heads[at + 1])
        weighed(h, scores)


def attend_kernel(info, own_ref, far_ref, mine_ref, other_ref, *refs):
    own_to, far_to, q_s, top_s, sum_s, v_s, bias_s, other_s, own_out, far_out, sems = refs
    fetch = pltpu.make_async_copy(other_ref, other_s, sems.at[0])
    fetch.start()
    core = info[2]
    half = mine_ref.shape[0]
    pairs = GROUP // 2
    for g, ref in enumerate((own_ref, far_ref)):
        for h in range(GROUP):
            to = (h % 2) * PART
            q_s[g, h // 2, to : to + PART] = ref[:, h * HD : (h + 1) * HD]
    top_s[...] = jnp.full_like(top_s, LOW)
    sum_s[...] = jnp.zeros_like(sum_s)
    v_s[0, :, :HD] = mine_ref[:, HD:]
    v_s[:, :, HD:] = jnp.ones((2, half, HD), BF)
    fetch.wait()
    v_s[1, :, :HD] = other_s[:, HD:]

    def step(g, p, ref, b, bound):
        at = pl.ds(pl.multiple_of(b * WIDE, WIDE), WIDE)
        keys = ref[at, :HD]
        values = v_s[p, at, :]
        if bound is not None:
            key = lax.broadcasted_iota(jnp.int32, (PART, WIDE), 1)
            query = lax.broadcasted_iota(jnp.int32, (PART, WIDE), 0)
            bias = jnp.where(key + b * WIDE < bound[0] + bound[1] * query, 0.0, LOW)
            bias_s[:PART] = bias
            bias_s[PART:] = bias

        def scored(h):
            scores = dot_t(q_s[g, h], keys)
            return scores if bound is None else scores + bias_s[...]

        def weighed(h, scores):
            before = top_s[g, h]
            top = jnp.maximum(before, jnp.max(scores, axis=1, keepdims=True))
            top_s[g, h] = top
            weights = jnp.exp2((scores - top[:, :1]) * FACTOR).astype(BF)
            fade = jnp.exp2((before - top) * FACTOR)
            fade = jnp.concatenate([fade, fade], axis=1)
            sum_s[g, h] = sum_s[g, h] * fade + dot(weights, values)

        in_turn(range(pairs), scored, weighed)

    def group(g, carry):
        chip, side = info[2 * g + 1], info[2 * g + 2]
        for p, ref in enumerate((mine_ref, other_s)):
            parity = core if p == 0 else 1 - core
            same = jnp.where(parity == side, 1, 0)
            before = (chip + jnp.where(parity < side, 1, 0)) * ROWS
            whole_steps = before // WIDE

            def plain(b, carry, p=p, ref=ref):
                step(g, p, ref, b, None)
                return carry

            lax.fori_loop(0, whole_steps, plain, 0)

            @pl.when((before % WIDE > 0) | (same > 0))
            def _(p=p, ref=ref):
                step(g, p, ref, whole_steps, (before + same * (PART * g + 1), same))

        return carry

    lax.fori_loop(0, 2, group, 0)
    for g, ref in enumerate((own_out, far_out)):
        for h in range(GROUP):
            total = sum_s[g, h // 2, (h % 2) * PART : (h % 2) * PART + PART]
            ref[:, h * HD : (h + 1) * HD] = (total[:, :HD] / total[:, HD:]).astype(BF)
    stores = [
        pltpu.make_async_copy(own_out, own_to, sems.at[1]),
        pltpu.make_async_copy(far_out, far_to, sems.at[2]),
    ]
    for copy in stores:
        copy.start()
    for copy in stores:
        copy.wait()


def attend(info, own, far, mine, other):
    tokens = 2 * mine.shape[0]
    vmem = pl.BlockSpec(memory_space=pltpu.VMEM)
    hbm = pl.BlockSpec(memory_space=pl.ANY)
    other = pltpu.with_memory_space_constraint(other, pltpu.HBM)
    out = pltpu.HBM(own.shape, BF)
    return pl.pallas_call(
        attend_kernel,
        out_shape=(out, out),
        in_specs=[smem(), vmem, vmem, vmem, hbm],
        out_specs=(hbm, hbm),
        scratch_shapes=[
            pltpu.VMEM((2, GROUP // 2, 2 * PART, HD), BF),
            pltpu.VMEM((2, GROUP // 2, 2 * PART, HD), F32),
            pltpu.VMEM((2, GROUP // 2, 2 * PART, 2 * HD), F32),
            pltpu.VMEM((2, tokens // 2, 2 * HD), BF),
            pltpu.VMEM((2 * PART, WIDE), F32),
            pltpu.VMEM(other.shape, BF),
            pltpu.VMEM(own.shape, BF),
            pltpu.VMEM(own.shape, BF),
            pltpu.SemaphoreType.DMA((3,)),
        ],
        compiler_params=pltpu.CompilerParams(vmem_limit_bytes=28 << 20),
        cost_estimate=pl.CostEstimate(
            flops=4 * GROUP * PART * tokens * HD,
            transcendentals=GROUP * PART * tokens,
            bytes_accessed=4 * tokens * HD,
        ),
        name="attend2",
    )(info, own, far, mine, other)


CHUNK = 8


def text_kernel(info, text, q_ref, mine_ref, other_hbm, high_ref, low_ref, out_ref, other_ref, sem):
    chip, core, low, count = (info[i] for i in range(4))
    first = (2 * chip + core) * ROWS
    half = mine_ref.shape[0]
    fetch = pltpu.make_async_copy(other_hbm, other_ref, sem)
    fetch.start()
    out_ref[...] = jnp.zeros_like(out_ref)
    rows = GROUP * CHUNK
    fetch.wait()

    def chunk(c, carry):
        place = jnp.zeros((CHUNK, ROWS), jnp.int32)
        sub = lax.broadcasted_iota(jnp.int32, (CHUNK, ROWS), 0)
        for i in range(CHUNK):
            n = c * CHUNK + i
            at = text[jnp.minimum(low + n, text.shape[0] - 1)] - first
            place = jnp.where(sub == i, jnp.where(n < count, at, -1), place)
        lane = lax.broadcasted_iota(jnp.int32, (CHUNK, ROWS), 1)
        select = jnp.where(lane == place, 1.0, 0.0).astype(BF)
        picked = dot(select, q_ref[...]).astype(BF)
        queries = jnp.concatenate(
            [picked[:, h * HD : (h + 1) * HD] for h in range(GROUP)], axis=0
        )
        place = jnp.concatenate([place[:, :HD]] * GROUP, axis=0)[:, :1]
        limit = first + jnp.maximum(place, 0)
        lane = lax.broadcasted_iota(jnp.int32, (1, half), 1)
        spread = lane + (lane // ROWS) * ROWS
        parts = []
        for ref, parity in ((mine_ref, core), (other_ref, 1 - core)):
            live = spread + parity * ROWS <= limit
            parts.append(jnp.where(live, dot_t(queries, ref[:, :HD]), LOW))
        top = jnp.maximum(*(jnp.max(x, axis=1, keepdims=True) for x in parts))
        parts = [jnp.exp2((x - top) * FACTOR) for x in parts]
        total = sum(jnp.sum(x, axis=1, keepdims=True) for x in parts)
        share = jnp.where(place >= 0, 1.0 / total, 0.0)
        for p, x in enumerate(parts):
            out_ref[p : p + 1, :] += jnp.sum(x * share, axis=0, keepdims=True)
        return carry

    lax.fori_loop(0, (count + CHUNK - 1) // CHUNK, chunk, 0)
    mine, other = (out_ref[0:1, :], out_ref[1:2, :])
    even, odd = (jnp.where(core == 0, mine, other), jnp.where(core == 0, other, mine))
    for p, x in enumerate((even, odd)):
        high = x.astype(BF)
        high_ref[p : p + 1, :] = high
        low_ref[p : p + 1, :] = (x - high.astype(F32)).astype(BF)


def text_sums(info, text_rows, q2, mine, other):
    tokens = 2 * mine.shape[0]
    vmem = pl.BlockSpec(memory_space=pltpu.VMEM)
    return pl.pallas_call(
        text_kernel,
        out_shape=(jax.ShapeDtypeStruct((2, tokens // 2), BF),) * 2,
        in_specs=[smem(), smem(), vmem, vmem, pl.BlockSpec(memory_space=pl.ANY)],
        out_specs=(vmem, vmem),
        scratch_shapes=[
            pltpu.VMEM((2, tokens // 2), F32),
            pltpu.VMEM(other.shape, BF),
            pltpu.SemaphoreType.DMA(()),
        ],
        compiler_params=pltpu.CompilerParams(vmem_limit_bytes=24 << 20),
        cost_estimate=pl.CostEstimate(
            flops=2 * GROUP * CHUNK * tokens * HD,
            transcendentals=GROUP * CHUNK * tokens,
            bytes_accessed=4 * tokens * HD,
        ),
        name="text_sums",
    )(info, text_rows, q2, mine, other)


def attend3_kernel(info, q_hbm, mine_ref, other_ref, out_ref, v_s, bias_s, q_ref, sem):
    fetch = pltpu.make_async_copy(q_hbm, q_ref, sem)
    fetch.start()
    chip, core = info[0], info[1]
    half = mine_ref.shape[0]
    v_s[:half, :HD] = mine_ref[:, HD:]
    v_s[half:, :HD] = other_ref[:, HD:]
    v_s[:, HD:] = jnp.ones((2 * half, HD), BF)
    row = lax.broadcasted_iota(jnp.int32, (1, half), 1)
    rest = row % PAD
    live = rest < SHARE
    query = lax.broadcasted_iota(jnp.int32, (PAD, half), 0)
    start = chip * PAD
    own = (row - start <= query) & live
    bias_s[:, :half] = jnp.where(own, 0.0, LOW)
    earlier = (row < start + core * PAD) & live
    bias_s[:, half:] = jnp.where(earlier & (query >= 0), 0.0, LOW)

    def scored(h):
        q = q_ref[:, h * HD : (h + 1) * HD]
        left = dot_t(q, mine_ref[:, :HD]) + bias_s[:, :half]
        right = dot_t(q, other_ref[:, :HD]) + bias_s[:, half:]
        return left, right

    def weighed(h, scores):
        left, right = scores
        top = jnp.maximum(
            jnp.max(left, axis=1, keepdims=True), jnp.max(right, axis=1, keepdims=True)
        )
        left = jnp.exp2((left - top) * FACTOR).astype(BF)
        right = jnp.exp2((right - top) * FACTOR).astype(BF)
        total = dot(left, v_s[:half]) + dot(right, v_s[half:])
        out = (total[:, :HD] / total[:, HD:]).astype(BF)
        out_ref[:, h * HD : (h + 1) * HD] = out[:SHARE]

    fetch.wait()
    in_turn(range(GROUP), scored, weighed)


def attend3(info, q3, mine, other):
    vmem = pl.BlockSpec(memory_space=pltpu.VMEM)
    keys = 2 * mine.shape[0]
    q3 = pltpu.with_memory_space_constraint(q3, pltpu.HBM)
    return pl.pallas_call(
        attend3_kernel,
        out_shape=jax.ShapeDtypeStruct((SHARE, q3.shape[1]), BF),
        in_specs=[smem(), pl.BlockSpec(memory_space=pl.ANY), vmem, vmem],
        out_specs=vmem,
        scratch_shapes=[
            pltpu.VMEM((keys, 2 * HD), BF),
            pltpu.VMEM((PAD, keys), F32),
            pltpu.VMEM(q3.shape, BF),
            pltpu.SemaphoreType.DMA(()),
        ],
        compiler_params=pltpu.CompilerParams(vmem_limit_bytes=28 << 20),
        cost_estimate=pl.CostEstimate(
            flops=6 * GROUP * PAD * keys * HD,
            transcendentals=GROUP * PAD * keys,
            bytes_accessed=4 * keys * HD,
        ),
        name="attend3",
    )(info, q3, mine, other)


def from_core(x):
    count = lax.axis_size("seq")
    return lax.ppermute(x, "seq", [(i ^ 1, i) for i in range(count)])


def from_head(x, distance):
    count = lax.axis_size("head")
    return lax.ppermute(x, "head", [((i + distance) % count, i) for i in range(count)])


def over_chips(many):
    count = lax.axis_size("seq")
    groups = [[i for i in range(count) if i % 2 == core] for core in range(2)]
    return lax.all_to_all(many, "seq", 0, 0, axis_index_groups=groups, tiled=True)


def over_heads(x):
    count = lax.axis_size("head")
    return [x] + [
        lax.ppermute(x, "head", [(i ^ step, i) for i in range(count)]) for step in range(1, count)
    ]


def from_partner(x):
    count = lax.axis_size("seq")
    return lax.ppermute(x, "seq", [(count - 1 - i, i) for i in range(count)])


def body(
    q2,
    k2,
    v2,
    hidden,
    w_query,
    b_query,
    w_key,
    b_key,
    w_value,
    b_value,
    kept_index,
    block_count,
    text_rows,
):
    rank = lax.axis_index("seq")
    head = lax.axis_index("head")
    seq_count = lax.axis_size("seq")
    head_count = lax.axis_size("head")
    core = rank % 2
    chip = rank // 2
    first = rank * ROWS
    depth = hidden.shape[1]

    chips = seq_count // 2
    kv2 = jnp.concatenate([k2, v2], axis=1)
    mine2 = over_chips(jnp.broadcast_to(kv2[None], (chips, *kv2.shape)))
    mine2 = mine2.reshape(-1, 2 * HD)

    numbers = jnp.stack([core, first, 0, block_count[0], block_count[1]])
    own, sent = pick_rows(numbers, kept_index, hidden)
    x = own + from_core(sent)
    marks = x[:, depth : depth + 2].astype(jnp.int32)
    positions = marks[:, 0] * 128 + marks[:, 1]
    x = x[:, :depth]
    freqs = 1000000.0 ** (-(jnp.arange(HD // 2, dtype=F32) * 2.0) / HD)
    angles = positions.astype(F32)[:, None] * freqs[None, :]
    cosine, sine = (jnp.cos(angles), jnp.sin(angles))
    cosine = jnp.concatenate([cosine, cosine], axis=1)
    sine = jnp.concatenate([-sine, sine], axis=1)

    weights = (w_query, w_key, w_value)
    here = head.astype(jnp.int32)

    def block(distance):
        return (here + distance) % head_count

    pieces = {d: from_head(x, d) for d in (2, 1, -1)}
    partial = project(here[None], [x], weights)
    sums, text_rows, q2 = lax.optimization_barrier((partial[1], text_rows, q2))
    partial = (partial[0], sums)
    far = from_partner(q2[PART:])
    low = jnp.sum((text_rows < first).astype(jnp.int32))
    count = jnp.sum((text_rows < first + ROWS).astype(jnp.int32)) - low
    partner = seq_count - 1 - rank
    place = jnp.stack([0, chip, core, partner // 2, partner % 2])
    text_info = jnp.stack([chip, core, low, count])
    partial = project(block(2)[None], [pieces[2]], weights, partial)
    biases = tuple(b[None, :] for b in (b_query, b_key, b_value))
    blocks = jnp.stack([block(1), block(-1)])
    mine2, far, partial, two, ready, place, text_info, blocks = lax.optimization_barrier(
        (
            mine2,
            far,
            partial,
            [pieces[1], pieces[-1]],
            (*biases, cosine, sine),
            place,
            text_info,
            blocks,
        )
    )
    other2 = from_core(mine2)
    q3, kv3 = project(blocks, two, weights, partial, ready)
    kv3, other2 = lax.optimization_barrier((kv3, other2))
    sums = text_sums(text_info, text_rows, q2, mine2, other2)

    sums = [part.reshape(2, chips, ROWS).swapaxes(0, 1) for part in sums]
    kept = jnp.broadcast_to(kv3[None, :SHARE], (chips, SHARE, 2 * HD))
    many = jnp.concatenate([kept, *sums], axis=1)
    mine = over_chips(many)
    far, many = lax.optimization_barrier((far, many))
    near, far = attend(place, q2[:PART], far, mine2, other2)
    far, mine = lax.optimization_barrier((far, mine))
    other = from_core(mine)
    far = from_partner(far)

    got = sum(jnp.sum(x[:, SHARE:].astype(F32), axis=0) for x in (mine, other))
    got = got[:2] + got[2:]
    got = over_heads(jnp.where(core == 0, got[0], got[1]))
    attn3 = attend3(place[1:3], q3, mine.reshape(-1, 2 * HD), other.reshape(-1, 2 * HD))
    attn3, far, *got = lax.optimization_barrier((attn3, far, *got))
    attn2 = jnp.concatenate([near, far], axis=0)
    tokens = seq_count * ROWS
    importance = (got[0] + got[1]) + (got[2] + got[3])
    importance = importance * (tokens / (GROUP * head_count * text_rows.shape[0]))
    return (attn2, importance, attn3)


def solution(mesh):
    placed = (
        P("seq", "head"),
        P("seq", "head"),
        P("seq", "head"),
        P("seq", "head"),
        P(None, "head"),
        P("head"),
        P(None, "head"),
        P("head"),
        P(None, "head"),
        P("head"),
        P("seq"),
        P("seq"),
        P(),
    )
    return jax.shard_map(
        body,
        mesh=mesh,
        in_specs=placed,
        out_specs=(P("seq", "head"), P("seq"), P("seq", "head")),
        check_vma=False,
    )
```

```python
import math

import jax
import jax.numpy as jnp
from jax import lax
from jax.experimental import pallas as pl
from jax.experimental.pallas import tpu as pltpu
from jax.sharding import PartitionSpec as P

HD = 128
GROUP = 8
BLOCK = 128
ROWS = 256
SHARE = 132
PAD = 136
PART = ROWS // 2
WIDE = 1024
FACTOR = math.log2(math.e) / math.sqrt(HD)
LOW = -1e30
BF = jnp.bfloat16
F32 = jnp.float32


def dot(a, b):
    return jnp.dot(a, b, preferred_element_type=F32)


def dot_t(a, b):
    return lax.dot_general(a, b, (((1,), (1,)), ((), ())), preferred_element_type=F32)


def whole(shape):
    return pl.BlockSpec(shape, lambda *_: (0,) * len(shape))


def smem():
    return pl.BlockSpec(memory_space=pltpu.SMEM)


def pick_kernel(info, index_ref, hidden_ref, own_ref, send_ref):
    core, first, before, live0, live1 = (info[i] for i in range(5))
    count = live0 + live1
    start = jnp.where(core == 0, 0, 2 * SHARE - count)
    lane = lax.broadcasted_iota(jnp.int32, (PAD, ROWS), 1)
    place = lax.broadcasted_iota(jnp.int32, (PAD, ROWS), 0)
    second = lane >= BLOCK
    within = jnp.where(second, lane - BLOCK, lane)
    rank = jnp.where(second, within + live0, within)
    live = within < jnp.where(second, live1, live0)
    row = index_ref[...] + jnp.where(second, BLOCK, 0)
    column = lax.broadcasted_iota(jnp.int32, (PAD, BLOCK), 1)
    for out_ref, base in ((own_ref, SHARE * core), (send_ref, SHARE * (1 - core))):
        wanted = place + (base - start)
        match = (rank == wanted) & live & (place < SHARE)
        source = jnp.sum(jnp.where(match, (row + 1).astype(F32), 0.0), axis=1, keepdims=True)
        source = source.astype(jnp.int32) - 1
        select = jnp.where(lane == source, 1.0, 0.0).astype(BF)
        out_ref[:, : hidden_ref.shape[1]] = dot(select, hidden_ref[...]).astype(BF)
        position = jnp.where(source >= 0, source + first, 0)
        high = jnp.where(column == 0, position >> 7, 0)
        marks = jnp.where(column == 1, position & 127, high)
        out_ref[:, hidden_ref.shape[1] :] = marks.astype(F32).astype(BF)


def pick_rows(info, kept_index, hidden):
    width = hidden.shape[1] + BLOCK
    shape = jax.ShapeDtypeStruct((PAD, width), BF)
    return pl.pallas_call(
        pick_kernel,
        out_shape=(shape, shape),
        in_specs=[smem(), pl.BlockSpec(memory_space=pltpu.VMEM), pl.BlockSpec(memory_space=pltpu.VMEM)],
        out_specs=(pl.BlockSpec(memory_space=pltpu.VMEM),) * 2,
        compiler_params=pltpu.CompilerParams(vmem_limit_bytes=16 << 20),
        cost_estimate=pl.CostEstimate(
            flops=4 * PAD * ROWS * width, transcendentals=0, bytes_accessed=4 * ROWS * width
        ),
        name="pick_rows",
    )(info, kept_index.reshape(1, ROWS), hidden)


def rotated(u, cosine, sine):
    return u * cosine + pltpu.roll(u, HD // 2, 1) * sine


STEP = 1024


def project_kernel(pieces, first, last, blocks, *refs):
    x_refs = refs[:pieces]
    weights = refs[pieces : pieces + 3]
    rest = refs[pieces + 3 :]
    if not first:
        before = rest[:2]
        rest = rest[2:]
    if last:
        bq, bk, bv, cosine, sine = rest[:5]
        rest = rest[5:]
    q_to, kv_out, *held, kv_s, q_s, q_out, sems, part_sems = rest
    if last:
        q_out = q_to
    sums = (q_s, kv_s)
    loads = []
    if not first:
        loads = [
            pltpu.make_async_copy(x, to, part_sems.at[i])
            for i, (x, to) in enumerate(zip(before, sums))
        ]
    depth = x_refs[0].shape[1]
    copies = []
    for p in range(pieces):
        for part in range(depth // STEP):
            at = len(copies) * STEP
            start = pl.multiple_of(blocks[p] * depth + part * STEP, STEP)
            copies.append(
                [
                    pltpu.make_async_copy(
                        w.at[pl.ds(start, STEP), :], to.at[at : at + STEP, :], sems.at[len(copies), i]
                    )
                    for i, (w, to) in enumerate(zip(weights, held))
                ]
            )
    for group in [*copies, loads]:
        for copy in group:
            copy.start()
    totals = [0.0, 0.0, 0.0]
    for n, group in enumerate(copies):
        p, part = divmod(n, depth // STEP)
        x = x_refs[p][:, part * STEP : (part + 1) * STEP]
        for copy in group:
            copy.wait()
        at = slice(n * STEP, (n + 1) * STEP)
        totals = [old + dot(x, w[at, :]) for old, w in zip(totals, held)]
    for copy in loads:
        copy.wait()
    q, k, v = totals
    if not first:
        q, k, v = (q + q_s[...], k + kv_s[:, :HD], v + kv_s[:, HD:])
    if last:
        c, s = (cosine[...], sine[...])
        for h in range(GROUP):
            at = slice(h * HD, (h + 1) * HD)
            q_out[:, at] = rotated(q[:, at] + bq[:, at], c, s).astype(BF)
        kv_out[:, :HD] = rotated(k + bk[...], c, s).astype(BF)
        kv_out[:, HD:] = (v + bv[...]).astype(BF)
        stores = []
    else:
        q_out[...] = q
        kv_s[:, :HD] = k
        kv_s[:, HD:] = v
        stores = [
            pltpu.make_async_copy(q_out, q_to, part_sems.at[2]),
            pltpu.make_async_copy(kv_s, kv_out, part_sems.at[3]),
        ]
    for copy in stores:
        copy.start()
    for copy in stores:
        copy.wait()


def project(blocks, xs, weights, partial=(), finish=()):
    pieces = len(xs)
    depth = xs[0].shape[1]
    widths = [w.shape[1] for w in weights]
    kind = BF if finish else F32
    vmem = pl.BlockSpec(memory_space=pltpu.VMEM)
    weights = [pltpu.with_memory_space_constraint(w, pltpu.HBM) for w in weights]
    hbm = pl.BlockSpec(memory_space=pl.ANY)
    partial = [pltpu.with_memory_space_constraint(part, pltpu.HBM) for part in partial]

    def kernel(*refs):
        project_kernel(pieces, not partial, bool(finish), *refs)

    outs = ((PAD, widths[0]), (PAD, 2 * HD))
    return pl.pallas_call(
        kernel,
        out_shape=(
            *(jax.ShapeDtypeStruct(o, kind) if finish else pltpu.HBM(o, kind) for o in outs),
        ),
        in_specs=[smem()]
        + [vmem] * pieces
        + [hbm] * (3 + len(partial))
        + [vmem] * len(finish),
        out_specs=(vmem, vmem) if finish else (hbm, hbm),
        scratch_shapes=[pltpu.VMEM((pieces * depth, width), BF) for width in widths]
        + [
            pltpu.VMEM(outs[1], F32),
            pltpu.VMEM(outs[0], F32),
            pltpu.VMEM(outs[0], kind),
            pltpu.SemaphoreType.DMA((pieces * depth // STEP, 3)),
            pltpu.SemaphoreType.DMA((4,)),
        ],
        compiler_params=pltpu.CompilerParams(vmem_limit_bytes=28 << 20),
        cost_estimate=pl.CostEstimate(
            flops=2 * pieces * PAD * depth * sum(widths),
            transcendentals=0,
            bytes_accessed=2 * pieces * depth * sum(widths),
        ),
        name="project",
    )(blocks, *xs, *weights, *partial, *finish)


def in_turn(heads, scored, weighed):
    ahead = scored(heads[0])
    for at, h in enumerate(heads):
        scores = ahead
        if at + 1 < len(heads):
            ahead = scored(heads[at + 1])
        weighed(h, scores)


def attend_kernel(info, own_ref, far_ref, mine_ref, other_ref, *refs):
    own_to, far_to, q_s, top_s, sum_s, v_s, bias_s, other_s, own_out, far_out, sems = refs
    fetch = pltpu.make_async_copy(other_ref, other_s, sems.at[0])
    fetch.start()
    core = info[2]
    half = mine_ref.shape[0]
    pairs = GROUP // 2
    for g, ref in enumerate((own_ref, far_ref)):
        for h in range(GROUP):
            to = (h % 2) * PART
            q_s[g, h // 2, to : to + PART] = ref[:, h * HD : (h + 1) * HD]
    top_s[...] = jnp.full_like(top_s, LOW)
    sum_s[...] = jnp.zeros_like(sum_s)
    v_s[0, :, :HD] = mine_ref[:, HD:]
    v_s[:, :, HD:] = jnp.ones((2, half, HD), BF)
    fetch.wait()
    v_s[1, :, :HD] = other_s[:, HD:]

    def step(g, p, ref, b, bound):
        at = pl.ds(pl.multiple_of(b * WIDE, WIDE), WIDE)
        keys = ref[at, :HD]
        values = v_s[p, at, :]
        if bound is not None:
            key = lax.broadcasted_iota(jnp.int32, (PART, WIDE), 1)
            query = lax.broadcasted_iota(jnp.int32, (PART, WIDE), 0)
            bias = jnp.where(key + b * WIDE < bound[0] + bound[1] * query, 0.0, LOW)
            bias_s[:PART] = bias
            bias_s[PART:] = bias

        def scored(h):
            scores = dot_t(q_s[g, h], keys)
            return scores if bound is None else scores + bias_s[...]

        def weighed(h, scores):
            before = top_s[g, h]
            top = jnp.maximum(before, jnp.max(scores, axis=1, keepdims=True))
            top_s[g, h] = top
            weights = jnp.exp2((scores - top[:, :1]) * FACTOR).astype(BF)
            fade = jnp.exp2((before - top) * FACTOR)
            fade = jnp.concatenate([fade, fade], axis=1)
            sum_s[g, h] = sum_s[g, h] * fade + dot(weights, values)

        in_turn(range(pairs), scored, weighed)

    def group(g, carry):
        chip, side = info[2 * g + 1], info[2 * g + 2]
        for p, ref in enumerate((mine_ref, other_s)):
            parity = core if p == 0 else 1 - core
            same = jnp.where(parity == side, 1, 0)
            before = (chip + jnp.where(parity < side, 1, 0)) * ROWS
            whole_steps = before // WIDE

            def plain(b, carry, p=p, ref=ref):
                step(g, p, ref, b, None)
                return carry

            lax.fori_loop(0, whole_steps, plain, 0)

            @pl.when((before % WIDE > 0) | (same > 0))
            def _(p=p, ref=ref):
                step(g, p, ref, whole_steps, (before + same * (PART * g + 1), same))

        return carry

    lax.fori_loop(0, 2, group, 0)
    for g, ref in enumerate((own_out, far_out)):
        for h in range(GROUP):
            total = sum_s[g, h // 2, (h % 2) * PART : (h % 2) * PART + PART]
            ref[:, h * HD : (h + 1) * HD] = (total[:, :HD] / total[:, HD:]).astype(BF)
    stores = [
        pltpu.make_async_copy(own_out, own_to, sems.at[1]),
        pltpu.make_async_copy(far_out, far_to, sems.at[2]),
    ]
    for copy in stores:
        copy.start()
    for copy in stores:
        copy.wait()


def attend(info, own, far, mine, other):
    tokens = 2 * mine.shape[0]
    vmem = pl.BlockSpec(memory_space=pltpu.VMEM)
    hbm = pl.BlockSpec(memory_space=pl.ANY)
    other = pltpu.with_memory_space_constraint(other, pltpu.HBM)
    out = pltpu.HBM(own.shape, BF)
    return pl.pallas_call(
        attend_kernel,
        out_shape=(out, out),
        in_specs=[smem(), vmem, vmem, vmem, hbm],
        out_specs=(hbm, hbm),
        scratch_shapes=[
            pltpu.VMEM((2, GROUP // 2, 2 * PART, HD), BF),
            pltpu.VMEM((2, GROUP // 2, 2 * PART, HD), F32),
            pltpu.VMEM((2, GROUP // 2, 2 * PART, 2 * HD), F32),
            pltpu.VMEM((2, tokens // 2, 2 * HD), BF),
            pltpu.VMEM((2 * PART, WIDE), F32),
            pltpu.VMEM(other.shape, BF),
            pltpu.VMEM(own.shape, BF),
            pltpu.VMEM(own.shape, BF),
            pltpu.SemaphoreType.DMA((3,)),
        ],
        compiler_params=pltpu.CompilerParams(vmem_limit_bytes=28 << 20),
        cost_estimate=pl.CostEstimate(
            flops=4 * GROUP * PART * tokens * HD,
            transcendentals=GROUP * PART * tokens,
            bytes_accessed=4 * tokens * HD,
        ),
        name="attend2",
    )(info, own, far, mine, other)


CHUNK = 8


def text_kernel(info, text, q_ref, mine_ref, other_hbm, high_ref, low_ref, out_ref, other_ref, sem):
    chip, core, low, count = (info[i] for i in range(4))
    first = (2 * chip + core) * ROWS
    half = mine_ref.shape[0]
    fetch = pltpu.make_async_copy(other_hbm, other_ref, sem)
    fetch.start()
    out_ref[...] = jnp.zeros_like(out_ref)
    rows = GROUP * CHUNK
    fetch.wait()

    def chunk(c, carry):
        place = jnp.zeros((CHUNK, ROWS), jnp.int32)
        sub = lax.broadcasted_iota(jnp.int32, (CHUNK, ROWS), 0)
        for i in range(CHUNK):
            n = c * CHUNK + i
            at = text[jnp.minimum(low + n, text.shape[0] - 1)] - first
            place = jnp.where(sub == i, jnp.where(n < count, at, -1), place)
        lane = lax.broadcasted_iota(jnp.int32, (CHUNK, ROWS), 1)
        select = jnp.where(lane == place, 1.0, 0.0).astype(BF)
        picked = dot(select, q_ref[...]).astype(BF)
        queries = jnp.concatenate(
            [picked[:, h * HD : (h + 1) * HD] for h in range(GROUP)], axis=0
        )
        place = jnp.concatenate([place[:, :HD]] * GROUP, axis=0)[:, :1]
        limit = first + jnp.maximum(place, 0)
        lane = lax.broadcasted_iota(jnp.int32, (1, half), 1)
        spread = lane + (lane // ROWS) * ROWS
        parts = []
        for ref, parity in ((mine_ref, core), (other_ref, 1 - core)):
            live = spread + parity * ROWS <= limit
            parts.append(jnp.where(live, dot_t(queries, ref[:, :HD]), LOW))
        top = jnp.maximum(*(jnp.max(x, axis=1, keepdims=True) for x in parts))
        parts = [jnp.exp2((x - top) * FACTOR) for x in parts]
        total = sum(jnp.sum(x, axis=1, keepdims=True) for x in parts)
        share = jnp.where(place >= 0, 1.0 / total, 0.0)
        for p, x in enumerate(parts):
            out_ref[p : p + 1, :] += jnp.sum(x * share, axis=0, keepdims=True)
        return carry

    lax.fori_loop(0, (count + CHUNK - 1) // CHUNK, chunk, 0)
    mine, other = (out_ref[0:1, :], out_ref[1:2, :])
    even, odd = (jnp.where(core == 0, mine, other), jnp.where(core == 0, other, mine))
    for p, x in enumerate((even, odd)):
        high = x.astype(BF)
        high_ref[p : p + 1, :] = high
        low_ref[p : p + 1, :] = (x - high.astype(F32)).astype(BF)


def text_sums(info, text_rows, q2, mine, other):
    tokens = 2 * mine.shape[0]
    vmem = pl.BlockSpec(memory_space=pltpu.VMEM)
    return pl.pallas_call(
        text_kernel,
        out_shape=(jax.ShapeDtypeStruct((2, tokens // 2), BF),) * 2,
        in_specs=[smem(), smem(), vmem, vmem, pl.BlockSpec(memory_space=pl.ANY)],
        out_specs=(vmem, vmem),
        scratch_shapes=[
            pltpu.VMEM((2, tokens // 2), F32),
            pltpu.VMEM(other.shape, BF),
            pltpu.SemaphoreType.DMA(()),
        ],
        compiler_params=pltpu.CompilerParams(vmem_limit_bytes=24 << 20),
        cost_estimate=pl.CostEstimate(
            flops=2 * GROUP * CHUNK * tokens * HD,
            transcendentals=GROUP * CHUNK * tokens,
            bytes_accessed=4 * tokens * HD,
        ),
        name="text_sums",
    )(info, text_rows, q2, mine, other)


def attend3_kernel(info, q_hbm, mine_ref, other_ref, out_ref, v_s, bias_s, q_ref, sem):
    fetch = pltpu.make_async_copy(q_hbm, q_ref, sem)
    fetch.start()
    chip, core = info[0], info[1]
    half = mine_ref.shape[0]
    v_s[:half, :HD] = mine_ref[:, HD:]
    v_s[half:, :HD] = other_ref[:, HD:]
    v_s[:, HD:] = jnp.ones((2 * half, HD), BF)
    row = lax.broadcasted_iota(jnp.int32, (1, half), 1)
    rest = row % PAD
    live = rest < SHARE
    query = lax.broadcasted_iota(jnp.int32, (PAD, half), 0)
    start = chip * PAD
    own = (row - start <= query) & live
    bias_s[:, :half] = jnp.where(own, 0.0, LOW)
    earlier = (row < start + core * PAD) & live
    bias_s[:, half:] = jnp.where(earlier & (query >= 0), 0.0, LOW)

    def scored(h):
        q = q_ref[:, h * HD : (h + 1) * HD]
        left = dot_t(q, mine_ref[:, :HD]) + bias_s[:, :half]
        right = dot_t(q, other_ref[:, :HD]) + bias_s[:, half:]
        return left, right

    def weighed(h, scores):
        left, right = scores
        top = jnp.maximum(
            jnp.max(left, axis=1, keepdims=True), jnp.max(right, axis=1, keepdims=True)
        )
        left = jnp.exp2((left - top) * FACTOR).astype(BF)
        right = jnp.exp2((right - top) * FACTOR).astype(BF)
        total = dot(left, v_s[:half]) + dot(right, v_s[half:])
        out = (total[:, :HD] / total[:, HD:]).astype(BF)
        out_ref[:, h * HD : (h + 1) * HD] = out[:SHARE]

    fetch.wait()
    in_turn(range(GROUP), scored, weighed)


def attend3(info, q3, mine, other):
    vmem = pl.BlockSpec(memory_space=pltpu.VMEM)
    keys = 2 * mine.shape[0]
    q3 = pltpu.with_memory_space_constraint(q3, pltpu.HBM)
    return pl.pallas_call(
        attend3_kernel,
        out_shape=jax.ShapeDtypeStruct((SHARE, q3.shape[1]), BF),
        in_specs=[smem(), pl.BlockSpec(memory_space=pl.ANY), vmem, vmem],
        out_specs=vmem,
        scratch_shapes=[
            pltpu.VMEM((keys, 2 * HD), BF),
            pltpu.VMEM((PAD, keys), F32),
            pltpu.VMEM(q3.shape, BF),
            pltpu.SemaphoreType.DMA(()),
        ],
        compiler_params=pltpu.CompilerParams(vmem_limit_bytes=28 << 20),
        cost_estimate=pl.CostEstimate(
            flops=6 * GROUP * PAD * keys * HD,
            transcendentals=GROUP * PAD * keys,
            bytes_accessed=4 * keys * HD,
        ),
        name="attend3",
    )(info, q3, mine, other)


def from_core(x):
    count = lax.axis_size("seq")
    return lax.ppermute(x, "seq", [(i ^ 1, i) for i in range(count)])


def from_head(x, distance):
    count = lax.axis_size("head")
    return lax.ppermute(x, "head", [((i + distance) % count, i) for i in range(count)])


def over_chips(many):
    count = lax.axis_size("seq")
    groups = [[i for i in range(count) if i % 2 == core] for core in range(2)]
    return lax.all_to_all(many, "seq", 0, 0, axis_index_groups=groups, tiled=True)


def over_heads(x):
    count = lax.axis_size("head")
    return [x] + [
        lax.ppermute(x, "head", [(i ^ step, i) for i in range(count)]) for step in range(1, count)
    ]


def from_partner(x):
    count = lax.axis_size("seq")
    return lax.ppermute(x, "seq", [(count - 1 - i, i) for i in range(count)])


def body(
    q2,
    k2,
    v2,
    hidden,
    w_query,
    b_query,
    w_key,
    b_key,
    w_value,
    b_value,
    kept_index,
    block_count,
    text_rows,
):
    rank = lax.axis_index("seq")
    head = lax.axis_index("head")
    seq_count = lax.axis_size("seq")
    head_count = lax.axis_size("head")
    core = rank % 2
    chip = rank // 2
    first = rank * ROWS
    depth = hidden.shape[1]

    chips = seq_count // 2
    kv2 = jnp.concatenate([k2, v2], axis=1)
    mine2 = over_chips(jnp.broadcast_to(kv2[None], (chips, *kv2.shape)))
    mine2 = mine2.reshape(-1, 2 * HD)

    numbers = jnp.stack([core, first, 0, block_count[0], block_count[1]])
    own, sent = pick_rows(numbers, kept_index, hidden)
    x = own + from_core(sent)
    marks = x[:, depth : depth + 2].astype(jnp.int32)
    half = depth // 2
    low, high = (x[:, :half], x[:, half:depth])

    weights = (w_query, w_key, w_value)
    here = head.astype(jnp.int32)

    def half_blocks(*pieces):
        return jnp.stack([2 * ((here + d) % head_count) + side for d, side in pieces])

    low_before, high_next = (from_head(low, -1), from_head(high, 1))
    high_before, low_next = (from_head(high, -1), from_head(low, 1))
    partial = project(half_blocks((0, 0), (0, 1)), [low, high], weights)
    low_far, high_far = (from_head(low_before, -1), from_head(high_next, 1))

    sums, marks, text_rows, q2 = lax.optimization_barrier((partial[1], marks, text_rows, q2))
    partial = (partial[0], sums)
    far = from_partner(q2[PART:])
    positions = marks[:, 0] * 128 + marks[:, 1]
    freqs = 1000000.0 ** (-(jnp.arange(HD // 2, dtype=F32) * 2.0) / HD)
    angles = positions.astype(F32)[:, None] * freqs[None, :]
    cosine, sine = (jnp.cos(angles), jnp.sin(angles))
    cosine = jnp.concatenate([cosine, cosine], axis=1)
    sine = jnp.concatenate([-sine, sine], axis=1)
    before = jnp.sum((text_rows < first).astype(jnp.int32))
    count = jnp.sum((text_rows < first + ROWS).astype(jnp.int32)) - before
    partner = seq_count - 1 - rank
    place = jnp.stack([0, chip, core, partner // 2, partner % 2])
    text_info = jnp.stack([chip, core, before, count])
    biases = tuple(b[None, :] for b in (b_query, b_key, b_value))
    partial = project(
        half_blocks((-1, 0), (1, 1), (-1, 1), (1, 0)),
        [low_before, high_next, high_before, low_next],
        weights,
        partial,
    )
    last = [pltpu.with_memory_space_constraint(x, pltpu.HBM) for x in (low_far, high_far)]
    sums, far, text_info, cosine, sine, mine2, last = lax.optimization_barrier(
        (partial[1], far, text_info, cosine, sine, mine2, last)
    )
    partial = (partial[0], sums)
    other2 = from_core(mine2)
    q3, kv3 = project(
        half_blocks((-2, 0), (2, 1)), last, weights, partial, (*biases, cosine, sine)
    )
    kv3, other2 = lax.optimization_barrier((kv3, other2))
    sums = text_sums(text_info, text_rows, q2, mine2, other2)

    sums = [part.reshape(2, chips, ROWS).swapaxes(0, 1) for part in sums]
    kept = jnp.broadcast_to(kv3[None, :SHARE], (chips, SHARE, 2 * HD))
    many = jnp.concatenate([kept, *sums], axis=1)
    mine = over_chips(many)
    far, many = lax.optimization_barrier((far, many))
    near, far = attend(place, q2[:PART], far, mine2, other2)
    far, mine = lax.optimization_barrier((far, mine))
    other = from_core(mine)
    far = from_partner(far)

    got = sum(jnp.sum(x[:, SHARE:].astype(F32), axis=0) for x in (mine, other))
    got = got[:2] + got[2:]
    got = over_heads(jnp.where(core == 0, got[0], got[1]))
    attn3 = attend3(place[1:3], q3, mine.reshape(-1, 2 * HD), other.reshape(-1, 2 * HD))
    attn3, far, *got = lax.optimization_barrier((attn3, far, *got))
    attn2 = jnp.concatenate([near, far], axis=0)
    tokens = seq_count * ROWS
    importance = (got[0] + got[1]) + (got[2] + got[3])
    importance = importance * (tokens / (GROUP * head_count * text_rows.shape[0]))
    return (attn2, importance, attn3)


def solution(mesh):
    placed = (
        P("seq", "head"),
        P("seq", "head"),
        P("seq", "head"),
        P("seq", "head"),
        P(None, "head"),
        P("head"),
        P(None, "head"),
        P("head"),
        P(None, "head"),
        P("head"),
        P("seq"),
        P("seq"),
        P(),
    )
    return jax.shard_map(
        body,
        mesh=mesh,
        in_specs=placed,
        out_specs=(P("seq", "head"), P("seq"), P("seq", "head")),
        check_vma=False,
    )
```

```python
import math

import jax
import jax.numpy as jnp
from jax import lax
from jax.experimental import pallas as pl
from jax.experimental.pallas import tpu as pltpu
from jax.sharding import PartitionSpec as P

HD = 128
GROUP = 8
BLOCK = 128
ROWS = 256
SHARE = 132
PAD = 136
PART = ROWS // 2
WIDE = 1024
FACTOR = math.log2(math.e) / math.sqrt(HD)
LOW = -1e30
BF = jnp.bfloat16
F32 = jnp.float32


def dot(a, b):
    return jnp.dot(a, b, preferred_element_type=F32)


def dot_t(a, b):
    return lax.dot_general(a, b, (((1,), (1,)), ((), ())), preferred_element_type=F32)


def whole(shape):
    return pl.BlockSpec(shape, lambda *_: (0,) * len(shape))


def smem():
    return pl.BlockSpec(memory_space=pltpu.SMEM)


def pick_kernel(counts, index_ref, hidden_ref, own_ref, send_ref):
    rank = lax.axis_index("seq")
    core, first = (rank % 2, rank * ROWS)
    live0, live1 = (counts[0], counts[1])
    count = live0 + live1
    start = jnp.where(core == 0, 0, 2 * SHARE - count)
    lane = lax.broadcasted_iota(jnp.int32, (PAD, ROWS), 1)
    place = lax.broadcasted_iota(jnp.int32, (PAD, ROWS), 0)
    second = lane >= BLOCK
    within = jnp.where(second, lane - BLOCK, lane)
    rank = jnp.where(second, within + live0, within)
    live = within < jnp.where(second, live1, live0)
    row = index_ref[...] + jnp.where(second, BLOCK, 0)
    column = lax.broadcasted_iota(jnp.int32, (PAD, BLOCK), 1)
    for out_ref, base in ((own_ref, SHARE * core), (send_ref, SHARE * (1 - core))):
        wanted = place + (base - start)
        match = (rank == wanted) & live & (place < SHARE)
        source = jnp.sum(jnp.where(match, (row + 1).astype(F32), 0.0), axis=1, keepdims=True)
        source = source.astype(jnp.int32) - 1
        select = jnp.where(lane == source, 1.0, 0.0).astype(BF)
        out_ref[:, : hidden_ref.shape[1]] = dot(select, hidden_ref[...]).astype(BF)
        position = jnp.where(source >= 0, source + first, 0)
        high = jnp.where(column == 0, position >> 7, 0)
        marks = jnp.where(column == 1, position & 127, high)
        out_ref[:, hidden_ref.shape[1] :] = marks.astype(F32).astype(BF)


def pick_rows(block_count, kept_index, hidden):
    width = hidden.shape[1] + BLOCK
    shape = jax.ShapeDtypeStruct((PAD, width), BF)
    return pl.pallas_call(
        pick_kernel,
        out_shape=(shape, shape),
        in_specs=[smem(), pl.BlockSpec(memory_space=pltpu.VMEM), pl.BlockSpec(memory_space=pltpu.VMEM)],
        out_specs=(pl.BlockSpec(memory_space=pltpu.VMEM),) * 2,
        compiler_params=pltpu.CompilerParams(vmem_limit_bytes=16 << 20),
        cost_estimate=pl.CostEstimate(
            flops=4 * PAD * ROWS * width, transcendentals=0, bytes_accessed=4 * ROWS * width
        ),
        name="pick_rows",
    )(block_count, kept_index.reshape(1, ROWS), hidden)


def rotated(u, cosine, sine):
    return u * cosine + pltpu.roll(u, HD // 2, 1) * sine


STEP = 1024


def project_kernel(places, first, last, *refs):
    pieces = len(places)
    here, heads = (lax.axis_index("head"), lax.axis_size("head"))
    x_refs = refs[:pieces]
    weights = refs[pieces : pieces + 3]
    rest = refs[pieces + 3 :]
    if not first:
        before = rest[:2]
        rest = rest[2:]
    if last:
        bq, bk, bv, cosine, sine = rest[:5]
        rest = rest[5:]
    q_to, kv_out, *held, kv_s, q_s, q_out, sems, part_sems = rest
    if last:
        q_out = q_to
    sums = (q_s, kv_s)
    loads = []
    if not first:
        loads = [
            pltpu.make_async_copy(x, to, part_sems.at[i])
            for i, (x, to) in enumerate(zip(before, sums))
        ]
    depth = x_refs[0].shape[1]
    copies = []
    for p in range(pieces):
        for part in range(depth // STEP):
            at = len(copies) * STEP
            distance, side = places[p]
            block = 2 * ((here + heads + distance) % heads) + side
            start = pl.multiple_of(block * depth + part * STEP, STEP)
            copies.append(
                [
                    pltpu.make_async_copy(
                        w.at[pl.ds(start, STEP), :], to.at[at : at + STEP, :], sems.at[len(copies), i]
                    )
                    for i, (w, to) in enumerate(zip(weights, held))
                ]
            )
    for group in [*copies, loads]:
        for copy in group:
            copy.start()
    totals = [0.0, 0.0, 0.0]
    for n, group in enumerate(copies):
        p, part = divmod(n, depth // STEP)
        x = x_refs[p][:, part * STEP : (part + 1) * STEP]
        for copy in group:
            copy.wait()
        at = slice(n * STEP, (n + 1) * STEP)
        totals = [old + dot(x, w[at, :]) for old, w in zip(totals, held)]
    for copy in loads:
        copy.wait()
    q, k, v = totals
    if not first:
        q, k, v = (q + q_s[...], k + kv_s[:, :HD], v + kv_s[:, HD:])
    if last:
        c, s = (cosine[...], sine[...])
        for h in range(GROUP):
            at = slice(h * HD, (h + 1) * HD)
            q_out[:, at] = rotated(q[:, at] + bq[:, at], c, s).astype(BF)
        kv_out[:, :HD] = rotated(k + bk[...], c, s).astype(BF)
        kv_out[:, HD:] = (v + bv[...]).astype(BF)
        stores = []
    else:
        q_out[...] = q
        kv_s[:, :HD] = k
        kv_s[:, HD:] = v
        stores = [
            pltpu.make_async_copy(q_out, q_to, part_sems.at[2]),
            pltpu.make_async_copy(kv_s, kv_out, part_sems.at[3]),
        ]
    for copy in stores:
        copy.start()
    for copy in stores:
        copy.wait()


def project(places, xs, weights, partial=(), finish=()):
    pieces = len(xs)
    depth = xs[0].shape[1]
    widths = [w.shape[1] for w in weights]
    kind = BF if finish else F32
    vmem = pl.BlockSpec(memory_space=pltpu.VMEM)
    weights = [pltpu.with_memory_space_constraint(w, pltpu.HBM) for w in weights]
    hbm = pl.BlockSpec(memory_space=pl.ANY)
    partial = [pltpu.with_memory_space_constraint(part, pltpu.HBM) for part in partial]

    def kernel(*refs):
        project_kernel(places, not partial, bool(finish), *refs)

    outs = ((PAD, widths[0]), (PAD, 2 * HD))
    return pl.pallas_call(
        kernel,
        out_shape=(
            *(jax.ShapeDtypeStruct(o, kind) if finish else pltpu.HBM(o, kind) for o in outs),
        ),
        in_specs=[vmem] * pieces
        + [hbm] * (3 + len(partial))
        + [vmem] * len(finish),
        out_specs=(vmem, vmem) if finish else (hbm, hbm),
        scratch_shapes=[pltpu.VMEM((pieces * depth, width), BF) for width in widths]
        + [
            pltpu.VMEM(outs[1], F32),
            pltpu.VMEM(outs[0], F32),
            pltpu.VMEM(outs[0], kind),
            pltpu.SemaphoreType.DMA((pieces * depth // STEP, 3)),
            pltpu.SemaphoreType.DMA((4,)),
        ],
        compiler_params=pltpu.CompilerParams(vmem_limit_bytes=28 << 20),
        cost_estimate=pl.CostEstimate(
            flops=2 * pieces * PAD * depth * sum(widths),
            transcendentals=0,
            bytes_accessed=2 * pieces * depth * sum(widths),
        ),
        name="project",
    )(*xs, *weights, *partial, *finish)


def in_turn(heads, scored, weighed):
    ahead = scored(heads[0])
    for at, h in enumerate(heads):
        scores = ahead
        if at + 1 < len(heads):
            ahead = scored(heads[at + 1])
        weighed(h, scores)


def attend_kernel(own_ref, far_ref, mine_ref, other_ref, *refs):
    rank = lax.axis_index("seq")
    partner = lax.axis_size("seq") - 1 - rank
    own_to, far_to, q_s, top_s, sum_s, v_s, bias_s, other_s, own_out, far_out, sems = refs
    fetch = pltpu.make_async_copy(other_ref, other_s, sems.at[0])
    fetch.start()
    core = rank % 2
    half = mine_ref.shape[0]
    pairs = GROUP // 2
    for g, ref in enumerate((own_ref, far_ref)):
        for h in range(GROUP):
            to = (h % 2) * PART
            q_s[g, h // 2, to : to + PART] = ref[:, h * HD : (h + 1) * HD]
    top_s[...] = jnp.full_like(top_s, LOW)
    sum_s[...] = jnp.zeros_like(sum_s)
    v_s[0, :, :HD] = mine_ref[:, HD:]
    v_s[:, :, HD:] = jnp.ones((2, half, HD), BF)
    fetch.wait()
    v_s[1, :, :HD] = other_s[:, HD:]

    def step(g, p, ref, b, bound):
        at = pl.ds(pl.multiple_of(b * WIDE, WIDE), WIDE)
        keys = ref[at, :HD]
        values = v_s[p, at, :]
        if bound is not None:
            key = lax.broadcasted_iota(jnp.int32, (PART, WIDE), 1)
            query = lax.broadcasted_iota(jnp.int32, (PART, WIDE), 0)
            bias = jnp.where(key + b * WIDE < bound[0] + bound[1] * query, 0.0, LOW)
            bias_s[:PART] = bias
            bias_s[PART:] = bias

        def scored(h):
            scores = dot_t(q_s[g, h], keys)
            return scores if bound is None else scores + bias_s[...]

        def weighed(h, scores):
            before = top_s[g, h]
            top = jnp.maximum(before, jnp.max(scores, axis=1, keepdims=True))
            top_s[g, h] = top
            weights = jnp.exp2((scores - top[:, :1]) * FACTOR).astype(BF)
            fade = jnp.exp2((before - top) * FACTOR)
            fade = jnp.concatenate([fade, fade], axis=1)
            sum_s[g, h] = sum_s[g, h] * fade + dot(weights, values)

        in_turn(range(pairs), scored, weighed)

    def group(g, carry):
        place = jnp.where(g == 0, rank, partner)
        chip, side = (place // 2, place % 2)
        for p, ref in enumerate((mine_ref, other_s)):
            parity = core if p == 0 else 1 - core
            same = jnp.where(parity == side, 1, 0)
            before = (chip + jnp.where(parity < side, 1, 0)) * ROWS
            whole_steps = before // WIDE

            def plain(b, carry, p=p, ref=ref):
                step(g, p, ref, b, None)
                return carry

            lax.fori_loop(0, whole_steps, plain, 0)

            @pl.when((before % WIDE > 0) | (same > 0))
            def _(p=p, ref=ref):
                step(g, p, ref, whole_steps, (before + same * (PART * g + 1), same))

        return carry

    lax.fori_loop(0, 2, group, 0)
    for g, ref in enumerate((own_out, far_out)):
        for h in range(GROUP):
            total = sum_s[g, h // 2, (h % 2) * PART : (h % 2) * PART + PART]
            ref[:, h * HD : (h + 1) * HD] = (total[:, :HD] / total[:, HD:]).astype(BF)
    stores = [
        pltpu.make_async_copy(own_out, own_to, sems.at[1]),
        pltpu.make_async_copy(far_out, far_to, sems.at[2]),
    ]
    for copy in stores:
        copy.start()
    for copy in stores:
        copy.wait()


def attend(own, far, mine, other):
    tokens = 2 * mine.shape[0]
    vmem = pl.BlockSpec(memory_space=pltpu.VMEM)
    hbm = pl.BlockSpec(memory_space=pl.ANY)
    other = pltpu.with_memory_space_constraint(other, pltpu.HBM)
    out = pltpu.HBM(own.shape, BF)
    return pl.pallas_call(
        attend_kernel,
        out_shape=(out, out),
        in_specs=[vmem, vmem, vmem, hbm],
        out_specs=(hbm, hbm),
        scratch_shapes=[
            pltpu.VMEM((2, GROUP // 2, 2 * PART, HD), BF),
            pltpu.VMEM((2, GROUP // 2, 2 * PART, HD), F32),
            pltpu.VMEM((2, GROUP // 2, 2 * PART, 2 * HD), F32),
            pltpu.VMEM((2, tokens // 2, 2 * HD), BF),
            pltpu.VMEM((2 * PART, WIDE), F32),
            pltpu.VMEM(other.shape, BF),
            pltpu.VMEM(own.shape, BF),
            pltpu.VMEM(own.shape, BF),
            pltpu.SemaphoreType.DMA((3,)),
        ],
        compiler_params=pltpu.CompilerParams(vmem_limit_bytes=28 << 20),
        cost_estimate=pl.CostEstimate(
            flops=4 * GROUP * PART * tokens * HD,
            transcendentals=GROUP * PART * tokens,
            bytes_accessed=4 * tokens * HD,
        ),
        name="attend2",
    )(own, far, mine, other)


CHUNK = 8


def text_kernel(text, rows_ref, q_ref, mine_ref, other_hbm, high_ref, low_ref, out_ref, other_ref, sem):
    rank = lax.axis_index("seq")
    core, first = (rank % 2, rank * ROWS)
    before = jnp.where(rows_ref[...] < first, 1.0, 0.0)
    within = jnp.where(rows_ref[...] < first + ROWS, 1.0, 0.0) - before
    low, count = (jnp.sum(x).astype(jnp.int32) for x in (before, within))
    half = mine_ref.shape[0]
    fetch = pltpu.make_async_copy(other_hbm, other_ref, sem)
    fetch.start()
    out_ref[...] = jnp.zeros_like(out_ref)
    rows = GROUP * CHUNK
    fetch.wait()

    def chunk(c, carry):
        place = jnp.zeros((CHUNK, ROWS), jnp.int32)
        sub = lax.broadcasted_iota(jnp.int32, (CHUNK, ROWS), 0)
        for i in range(CHUNK):
            n = c * CHUNK + i
            at = text[jnp.minimum(low + n, text.shape[0] - 1)] - first
            place = jnp.where(sub == i, jnp.where(n < count, at, -1), place)
        lane = lax.broadcasted_iota(jnp.int32, (CHUNK, ROWS), 1)
        select = jnp.where(lane == place, 1.0, 0.0).astype(BF)
        picked = dot(select, q_ref[...]).astype(BF)
        queries = jnp.concatenate(
            [picked[:, h * HD : (h + 1) * HD] for h in range(GROUP)], axis=0
        )
        place = jnp.concatenate([place[:, :HD]] * GROUP, axis=0)[:, :1]
        limit = first + jnp.maximum(place, 0)
        lane = lax.broadcasted_iota(jnp.int32, (1, half), 1)
        spread = lane + (lane // ROWS) * ROWS
        parts = []
        for ref, parity in ((mine_ref, core), (other_ref, 1 - core)):
            live = spread + parity * ROWS <= limit
            parts.append(jnp.where(live, dot_t(queries, ref[:, :HD]), LOW))
        top = jnp.maximum(*(jnp.max(x, axis=1, keepdims=True) for x in parts))
        parts = [jnp.exp2((x - top) * FACTOR) for x in parts]
        total = sum(jnp.sum(x, axis=1, keepdims=True) for x in parts)
        share = jnp.where(place >= 0, 1.0 / total, 0.0)
        for p, x in enumerate(parts):
            out_ref[p : p + 1, :] += jnp.sum(x * share, axis=0, keepdims=True)
        return carry

    lax.fori_loop(0, (count + CHUNK - 1) // CHUNK, chunk, 0)
    mine, other = (out_ref[0:1, :], out_ref[1:2, :])
    even, odd = (jnp.where(core == 0, mine, other), jnp.where(core == 0, other, mine))
    for p, x in enumerate((even, odd)):
        high = x.astype(BF)
        high_ref[p : p + 1, :] = high
        low_ref[p : p + 1, :] = (x - high.astype(F32)).astype(BF)


def text_sums(text_rows, q2, mine, other):
    tokens = 2 * mine.shape[0]
    vmem = pl.BlockSpec(memory_space=pltpu.VMEM)
    return pl.pallas_call(
        text_kernel,
        out_shape=(jax.ShapeDtypeStruct((2, tokens // 2), BF),) * 2,
        in_specs=[smem(), vmem, vmem, vmem, pl.BlockSpec(memory_space=pl.ANY)],
        out_specs=(vmem, vmem),
        scratch_shapes=[
            pltpu.VMEM((2, tokens // 2), F32),
            pltpu.VMEM(other.shape, BF),
            pltpu.SemaphoreType.DMA(()),
        ],
        compiler_params=pltpu.CompilerParams(vmem_limit_bytes=24 << 20),
        cost_estimate=pl.CostEstimate(
            flops=2 * GROUP * CHUNK * tokens * HD,
            transcendentals=GROUP * CHUNK * tokens,
            bytes_accessed=4 * tokens * HD,
        ),
        name="text_sums",
    )(text_rows, text_rows.reshape(1, -1), q2, mine, other)


def attend3_kernel(q_hbm, mine_ref, other_ref, out_ref, v_s, bias_s, q_ref, sem):
    fetch = pltpu.make_async_copy(q_hbm, q_ref, sem)
    fetch.start()
    rank = lax.axis_index("seq")
    chip, core = (rank // 2, rank % 2)
    half = mine_ref.shape[0]
    v_s[:half, :HD] = mine_ref[:, HD:]
    v_s[half:, :HD] = other_ref[:, HD:]
    v_s[:, HD:] = jnp.ones((2 * half, HD), BF)
    row = lax.broadcasted_iota(jnp.int32, (1, half), 1)
    rest = row % PAD
    live = rest < SHARE
    query = lax.broadcasted_iota(jnp.int32, (PAD, half), 0)
    start = chip * PAD
    own = (row - start <= query) & live
    bias_s[:, :half] = jnp.where(own, 0.0, LOW)
    earlier = (row < start + core * PAD) & live
    bias_s[:, half:] = jnp.where(earlier & (query >= 0), 0.0, LOW)

    def scored(h):
        q = q_ref[:, h * HD : (h + 1) * HD]
        left = dot_t(q, mine_ref[:, :HD]) + bias_s[:, :half]
        right = dot_t(q, other_ref[:, :HD]) + bias_s[:, half:]
        return left, right

    def weighed(h, scores):
        left, right = scores
        top = jnp.maximum(
            jnp.max(left, axis=1, keepdims=True), jnp.max(right, axis=1, keepdims=True)
        )
        left = jnp.exp2((left - top) * FACTOR).astype(BF)
        right = jnp.exp2((right - top) * FACTOR).astype(BF)
        total = dot(left, v_s[:half]) + dot(right, v_s[half:])
        out = (total[:, :HD] / total[:, HD:]).astype(BF)
        out_ref[:, h * HD : (h + 1) * HD] = out[:SHARE]

    fetch.wait()
    in_turn(range(GROUP), scored, weighed)


def attend3(q3, mine, other):
    vmem = pl.BlockSpec(memory_space=pltpu.VMEM)
    keys = 2 * mine.shape[0]
    q3 = pltpu.with_memory_space_constraint(q3, pltpu.HBM)
    return pl.pallas_call(
        attend3_kernel,
        out_shape=jax.ShapeDtypeStruct((SHARE, q3.shape[1]), BF),
        in_specs=[pl.BlockSpec(memory_space=pl.ANY), vmem, vmem],
        out_specs=vmem,
        scratch_shapes=[
            pltpu.VMEM((keys, 2 * HD), BF),
            pltpu.VMEM((PAD, keys), F32),
            pltpu.VMEM(q3.shape, BF),
            pltpu.SemaphoreType.DMA(()),
        ],
        compiler_params=pltpu.CompilerParams(vmem_limit_bytes=28 << 20),
        cost_estimate=pl.CostEstimate(
            flops=6 * GROUP * PAD * keys * HD,
            transcendentals=GROUP * PAD * keys,
            bytes_accessed=4 * keys * HD,
        ),
        name="attend3",
    )(q3, mine, other)


def from_core(x):
    count = lax.axis_size("seq")
    return lax.ppermute(x, "seq", [(i ^ 1, i) for i in range(count)])


def from_head(x, distance):
    count = lax.axis_size("head")
    return lax.ppermute(x, "head", [((i + distance) % count, i) for i in range(count)])


def over_chips(many):
    count = lax.axis_size("seq")
    groups = [[i for i in range(count) if i % 2 == core] for core in range(2)]
    return lax.all_to_all(many, "seq", 0, 0, axis_index_groups=groups, tiled=True)


def over_heads(x):
    count = lax.axis_size("head")
    return [x] + [
        lax.ppermute(x, "head", [(i ^ step, i) for i in range(count)]) for step in range(1, count)
    ]


def from_partner(x):
    count = lax.axis_size("seq")
    return lax.ppermute(x, "seq", [(count - 1 - i, i) for i in range(count)])


def body(
    q2,
    k2,
    v2,
    hidden,
    w_query,
    b_query,
    w_key,
    b_key,
    w_value,
    b_value,
    kept_index,
    block_count,
    text_rows,
):
    seq_count = lax.axis_size("seq")
    head_count = lax.axis_size("head")
    depth = hidden.shape[1]

    chips = seq_count // 2
    kv2 = jnp.concatenate([k2, v2], axis=1)
    mine2 = over_chips(jnp.broadcast_to(kv2[None], (chips, *kv2.shape)))
    mine2 = mine2.reshape(-1, 2 * HD)

    own, sent = pick_rows(block_count, kept_index, hidden)
    x = own + from_core(sent)
    marks = x[:, depth : depth + 2].astype(jnp.int32)
    half = depth // 2
    low, high = (x[:, :half], x[:, half:depth])
    weights = (w_query, w_key, w_value)

    low_before, high_next = (from_head(low, -1), from_head(high, 1))
    high_before, low_next = (from_head(high, -1), from_head(low, 1))
    partial = project([(0, 0), (0, 1)], [low, high], weights)
    low_far, high_far = (from_head(low_before, -1), from_head(high_next, 1))

    sums, marks, far = lax.optimization_barrier((partial[1], marks, q2[PART:]))
    partial = (partial[0], sums)
    positions = marks[:, 0] * 128 + marks[:, 1]
    lane = jnp.arange(HD, dtype=jnp.int32)
    freqs = 1000000.0 ** (-((lane % (HD // 2)).astype(F32) * 2.0) / HD)
    angles = positions.astype(F32)[:, None] * freqs[None, :]
    cosine = jnp.cos(angles)
    sine = jnp.sin(angles) * jnp.where(lane < HD // 2, -1.0, 1.0)[None, :]
    biases = tuple(b[None, :] for b in (b_query, b_key, b_value))
    partial = project(
        [(-1, 0), (1, 1), (-1, 1), (1, 0)],
        [low_before, high_next, high_before, low_next],
        weights,
        partial,
    )
    last = [pltpu.with_memory_space_constraint(x, pltpu.HBM) for x in (low_far, high_far)]
    sums, far, cosine, sine, mine2, last = lax.optimization_barrier(
        (partial[1], far, cosine, sine, mine2, last)
    )
    partial = (partial[0], sums)
    other2 = from_core(mine2)
    far = from_partner(far)
    q3, kv3 = project([(-2, 0), (2, 1)], last, weights, partial, (*biases, cosine, sine))
    kv3, other2, far = lax.optimization_barrier((kv3, other2, far))
    sums = text_sums(text_rows, q2, mine2, other2)

    sums = [part.reshape(2, chips, ROWS).swapaxes(0, 1) for part in sums]
    kept = jnp.broadcast_to(kv3[None, :SHARE], (chips, SHARE, 2 * HD))
    many = jnp.concatenate([kept, *sums], axis=1)
    mine = over_chips(many)
    far, many = lax.optimization_barrier((far, many))
    near, far = attend(q2[:PART], far, mine2, other2)
    far, mine = lax.optimization_barrier((far, mine))
    other = from_core(mine)
    far = from_partner(far)

    got = sum(jnp.sum(x[:, SHARE:].astype(F32), axis=0) for x in (mine, other))
    got = got[:2] + got[2:]
    got = over_heads(jnp.where(lax.axis_index("seq") % 2 == 0, got[0], got[1]))
    attn3 = attend3(q3, mine.reshape(-1, 2 * HD), other.reshape(-1, 2 * HD))
    attn3, far, *got = lax.optimization_barrier((attn3, far, *got))
    attn2 = jnp.concatenate([near, far], axis=0)
    tokens = seq_count * ROWS
    importance = (got[0] + got[1]) + (got[2] + got[3])
    importance = importance * (tokens / (GROUP * head_count * text_rows.shape[0]))
    return (attn2, importance, attn3)


def solution(mesh):
    placed = (
        P("seq", "head"),
        P("seq", "head"),
        P("seq", "head"),
        P("seq", "head"),
        P(None, "head"),
        P("head"),
        P(None, "head"),
        P("head"),
        P(None, "head"),
        P("head"),
        P("seq"),
        P("seq"),
        P(),
    )
    return jax.shard_map(
        body,
        mesh=mesh,
        in_specs=placed,
        out_specs=(P("seq", "head"), P("seq"), P("seq", "head")),
        check_vma=False,
    )
```

```python
import math

import jax
import jax.numpy as jnp
from jax import lax
from jax.experimental import pallas as pl
from jax.experimental.pallas import tpu as pltpu
from jax.sharding import PartitionSpec as P

HD = 128
GROUP = 8
BLOCK = 128
ROWS = 256
SHARE = 132
PAD = 136
PART = ROWS // 2
WIDE = 1024
FACTOR = math.log2(math.e) / math.sqrt(HD)
LOW = -1e30
BF = jnp.bfloat16
F32 = jnp.float32


def dot(a, b):
    return jnp.dot(a, b, preferred_element_type=F32)


def dot_t(a, b):
    return lax.dot_general(a, b, (((1,), (1,)), ((), ())), preferred_element_type=F32)


def whole(shape):
    return pl.BlockSpec(shape, lambda *_: (0,) * len(shape))


def smem():
    return pl.BlockSpec(memory_space=pltpu.SMEM)


def pick_kernel(counts, index_ref, hidden_ref, own_ref, send_ref):
    rank = lax.axis_index("seq")
    core, first = (rank % 2, rank * ROWS)
    live0, live1 = (counts[0], counts[1])
    count = live0 + live1
    start = jnp.where(core == 0, 0, 2 * SHARE - count)
    lane = lax.broadcasted_iota(jnp.int32, (PAD, ROWS), 1)
    place = lax.broadcasted_iota(jnp.int32, (PAD, ROWS), 0)
    second = lane >= BLOCK
    within = jnp.where(second, lane - BLOCK, lane)
    rank = jnp.where(second, within + live0, within)
    live = within < jnp.where(second, live1, live0)
    row = index_ref[...] + jnp.where(second, BLOCK, 0)
    column = lax.broadcasted_iota(jnp.int32, (PAD, BLOCK), 1)
    for out_ref, base in ((own_ref, SHARE * core), (send_ref, SHARE * (1 - core))):
        wanted = place + (base - start)
        match = (rank == wanted) & live & (place < SHARE)
        source = jnp.sum(jnp.where(match, (row + 1).astype(F32), 0.0), axis=1, keepdims=True)
        source = source.astype(jnp.int32) - 1
        select = jnp.where(lane == source, 1.0, 0.0).astype(BF)
        out_ref[:, : hidden_ref.shape[1]] = dot(select, hidden_ref[...]).astype(BF)
        position = jnp.where(source >= 0, source + first, 0)
        high = jnp.where(column == 0, position >> 7, 0)
        marks = jnp.where(column == 1, position & 127, high)
        out_ref[:, hidden_ref.shape[1] :] = marks.astype(F32).astype(BF)


def pick_rows(block_count, kept_index, hidden):
    width = hidden.shape[1] + BLOCK
    shape = jax.ShapeDtypeStruct((PAD, width), BF)
    return pl.pallas_call(
        pick_kernel,
        out_shape=(shape, shape),
        in_specs=[smem(), pl.BlockSpec(memory_space=pltpu.VMEM), pl.BlockSpec(memory_space=pltpu.VMEM)],
        out_specs=(pl.BlockSpec(memory_space=pltpu.VMEM),) * 2,
        compiler_params=pltpu.CompilerParams(vmem_limit_bytes=16 << 20),
        cost_estimate=pl.CostEstimate(
            flops=4 * PAD * ROWS * width, transcendentals=0, bytes_accessed=4 * ROWS * width
        ),
        name="pick_rows",
    )(block_count, kept_index.reshape(1, ROWS), hidden)


def rotated(u, cosine, sine):
    return u * cosine + pltpu.roll(u, HD // 2, 1) * sine


STEP = 1024


def project_kernel(places, first, last, *refs):
    pieces = len(places)
    here, heads = (lax.axis_index("head"), lax.axis_size("head"))
    x_refs = refs[:pieces]
    weights = refs[pieces : pieces + 3]
    rest = refs[pieces + 3 :]
    if not first:
        before = rest[:2]
        rest = rest[2:]
    if last:
        bq, bk, bv, cosine, sine = rest[:5]
        rest = rest[5:]
    q_to, kv_out, *held, kv_s, q_s, q_out, sems, part_sems = rest
    if last:
        q_out = q_to
    sums = (q_s, kv_s)
    loads = []
    if not first:
        loads = [
            pltpu.make_async_copy(x, to, part_sems.at[i])
            for i, (x, to) in enumerate(zip(before, sums))
        ]
    depth = x_refs[0].shape[1]
    copies = []
    for p in range(pieces):
        for part in range(depth // STEP):
            at = len(copies) * STEP
            distance, side = places[p]
            block = 2 * ((here + heads + distance) % heads) + side
            start = pl.multiple_of(block * depth + part * STEP, STEP)
            copies.append(
                [
                    pltpu.make_async_copy(
                        w.at[pl.ds(start, STEP), :], to.at[at : at + STEP, :], sems.at[len(copies), i]
                    )
                    for i, (w, to) in enumerate(zip(weights, held))
                ]
            )
    for group in [*copies, loads]:
        for copy in group:
            copy.start()
    totals = [0.0, 0.0, 0.0]
    for n, group in enumerate(copies):
        p, part = divmod(n, depth // STEP)
        x = x_refs[p][:, part * STEP : (part + 1) * STEP]
        for copy in group:
            copy.wait()
        at = slice(n * STEP, (n + 1) * STEP)
        totals = [old + dot(x, w[at, :]) for old, w in zip(totals, held)]
    for copy in loads:
        copy.wait()
    q, k, v = totals
    if not first:
        q, k, v = (q + q_s[...], k + kv_s[:, :HD], v + kv_s[:, HD:])
    if last:
        c, s = (cosine[...], sine[...])
        for h in range(GROUP):
            at = slice(h * HD, (h + 1) * HD)
            q_out[:, at] = rotated(q[:, at] + bq[:, at], c, s).astype(BF)
        kv_out[:, :HD] = rotated(k + bk[...], c, s).astype(BF)
        kv_out[:, HD:] = (v + bv[...]).astype(BF)
        stores = []
    else:
        q_out[...] = q
        kv_s[:, :HD] = k
        kv_s[:, HD:] = v
        stores = [
            pltpu.make_async_copy(q_out, q_to, part_sems.at[2]),
            pltpu.make_async_copy(kv_s, kv_out, part_sems.at[3]),
        ]
    for copy in stores:
        copy.start()
    for copy in stores:
        copy.wait()


def project(places, xs, weights, partial=(), finish=()):
    pieces = len(xs)
    depth = xs[0].shape[1]
    widths = [w.shape[1] for w in weights]
    kind = BF if finish else F32
    vmem = pl.BlockSpec(memory_space=pltpu.VMEM)
    weights = [pltpu.with_memory_space_constraint(w, pltpu.HBM) for w in weights]
    hbm = pl.BlockSpec(memory_space=pl.ANY)
    partial = [pltpu.with_memory_space_constraint(part, pltpu.HBM) for part in partial]

    def kernel(*refs):
        project_kernel(places, not partial, bool(finish), *refs)

    outs = ((PAD, widths[0]), (PAD, 2 * HD))
    return pl.pallas_call(
        kernel,
        out_shape=(
            *(jax.ShapeDtypeStruct(o, kind) if finish else pltpu.HBM(o, kind) for o in outs),
        ),
        in_specs=[vmem] * pieces
        + [hbm] * (3 + len(partial))
        + [vmem] * len(finish),
        out_specs=(vmem, vmem) if finish else (hbm, hbm),
        scratch_shapes=[pltpu.VMEM((pieces * depth, width), BF) for width in widths]
        + [
            pltpu.VMEM(outs[1], F32),
            pltpu.VMEM(outs[0], F32),
            pltpu.VMEM(outs[0], kind),
            pltpu.SemaphoreType.DMA((pieces * depth // STEP, 3)),
            pltpu.SemaphoreType.DMA((4,)),
        ],
        compiler_params=pltpu.CompilerParams(vmem_limit_bytes=28 << 20),
        cost_estimate=pl.CostEstimate(
            flops=2 * pieces * PAD * depth * sum(widths),
            transcendentals=0,
            bytes_accessed=2 * pieces * depth * sum(widths),
        ),
        name="project",
    )(*xs, *weights, *partial, *finish)


def in_turn(heads, scored, weighed):
    ahead = scored(heads[0])
    for at, h in enumerate(heads):
        scores = ahead
        if at + 1 < len(heads):
            ahead = scored(heads[at + 1])
        weighed(h, scores)


def attend_kernel(own_ref, far_ref, mine_ref, other_ref, *refs):
    rank = lax.axis_index("seq")
    partner = lax.axis_size("seq") - 1 - rank
    own_to, far_to, q_s, top_s, sum_s, v_s, bias_s, other_s, own_out, far_out, sems = refs
    fetch = pltpu.make_async_copy(other_ref, other_s, sems.at[0])
    fetch.start()
    core = rank % 2
    half = mine_ref.shape[0]
    pairs = GROUP // 2
    for g, ref in enumerate((own_ref, far_ref)):
        for h in range(GROUP):
            to = (h % 2) * PART
            q_s[g, h // 2, to : to + PART] = ref[:, h * HD : (h + 1) * HD]
    top_s[...] = jnp.full_like(top_s, LOW)
    sum_s[...] = jnp.zeros_like(sum_s)
    v_s[0, :, :HD] = mine_ref[:, HD:]
    v_s[:, :, HD:] = jnp.ones((2, half, HD), BF)
    fetch.wait()
    v_s[1, :, :HD] = other_s[:, HD:]

    def step(g, p, ref, b, bound):
        at = pl.ds(pl.multiple_of(b * WIDE, WIDE), WIDE)
        keys = ref[at, :HD]
        values = v_s[p, at, :]
        if bound is not None:
            key = lax.broadcasted_iota(jnp.int32, (PART, WIDE), 1)
            query = lax.broadcasted_iota(jnp.int32, (PART, WIDE), 0)
            bias = jnp.where(key + b * WIDE < bound[0] + bound[1] * query, 0.0, LOW)
            bias_s[:PART] = bias
            bias_s[PART:] = bias

        def scored(h):
            scores = dot_t(q_s[g, h], keys)
            return scores if bound is None else scores + bias_s[...]

        def weighed(h, scores):
            before = top_s[g, h]
            top = jnp.maximum(before, jnp.max(scores, axis=1, keepdims=True))
            top_s[g, h] = top
            weights = jnp.exp2((scores - top[:, :1]) * FACTOR).astype(BF)
            fade = jnp.exp2((before - top) * FACTOR)
            fade = jnp.concatenate([fade, fade], axis=1)
            sum_s[g, h] = sum_s[g, h] * fade + dot(weights, values)

        in_turn(range(pairs), scored, weighed)

    def group(g, carry):
        place = jnp.where(g == 0, rank, partner)
        chip, side = (place // 2, place % 2)
        for p, ref in enumerate((mine_ref, other_s)):
            parity = core if p == 0 else 1 - core
            same = jnp.where(parity == side, 1, 0)
            before = (chip + jnp.where(parity < side, 1, 0)) * ROWS
            whole_steps = before // WIDE

            def plain(b, carry, p=p, ref=ref):
                step(g, p, ref, b, None)
                return carry

            lax.fori_loop(0, whole_steps, plain, 0)

            @pl.when((before % WIDE > 0) | (same > 0))
            def _(p=p, ref=ref):
                step(g, p, ref, whole_steps, (before + same * (PART * g + 1), same))

        return carry

    lax.fori_loop(0, 2, group, 0)
    for g, ref in enumerate((own_out, far_out)):
        for h in range(GROUP):
            total = sum_s[g, h // 2, (h % 2) * PART : (h % 2) * PART + PART]
            ref[:, h * HD : (h + 1) * HD] = (total[:, :HD] / total[:, HD:]).astype(BF)
    stores = [
        pltpu.make_async_copy(own_out, own_to, sems.at[1]),
        pltpu.make_async_copy(far_out, far_to, sems.at[2]),
    ]
    for copy in stores:
        copy.start()
    for copy in stores:
        copy.wait()


def attend(own, far, mine, other):
    tokens = 2 * mine.shape[0]
    vmem = pl.BlockSpec(memory_space=pltpu.VMEM)
    hbm = pl.BlockSpec(memory_space=pl.ANY)
    far, other = (pltpu.with_memory_space_constraint(x, pltpu.HBM) for x in (far, other))
    out = pltpu.HBM(own.shape, BF)
    return pl.pallas_call(
        attend_kernel,
        out_shape=(out, out),
        in_specs=[vmem, vmem, vmem, hbm],
        out_specs=(hbm, hbm),
        scratch_shapes=[
            pltpu.VMEM((2, GROUP // 2, 2 * PART, HD), BF),
            pltpu.VMEM((2, GROUP // 2, 2 * PART, HD), F32),
            pltpu.VMEM((2, GROUP // 2, 2 * PART, 2 * HD), F32),
            pltpu.VMEM((2, tokens // 2, 2 * HD), BF),
            pltpu.VMEM((2 * PART, WIDE), F32),
            pltpu.VMEM(other.shape, BF),
            pltpu.VMEM(own.shape, BF),
            pltpu.VMEM(own.shape, BF),
            pltpu.SemaphoreType.DMA((3,)),
        ],
        compiler_params=pltpu.CompilerParams(vmem_limit_bytes=28 << 20),
        cost_estimate=pl.CostEstimate(
            flops=4 * GROUP * PART * tokens * HD,
            transcendentals=GROUP * PART * tokens,
            bytes_accessed=4 * tokens * HD,
        ),
        name="attend2",
    )(own, far, mine, other)


CHUNK = 8


def text_kernel(text, rows_ref, q_ref, mine_ref, other_hbm, high_ref, low_ref, out_ref, other_ref, sem):
    rank = lax.axis_index("seq")
    core, first = (rank % 2, rank * ROWS)
    before = jnp.where(rows_ref[...] < first, 1.0, 0.0)
    within = jnp.where(rows_ref[...] < first + ROWS, 1.0, 0.0) - before
    low, count = (jnp.sum(x).astype(jnp.int32) for x in (before, within))
    half = mine_ref.shape[0]
    fetch = pltpu.make_async_copy(other_hbm, other_ref, sem)
    fetch.start()
    out_ref[...] = jnp.zeros_like(out_ref)
    rows = GROUP * CHUNK
    fetch.wait()

    def chunk(c, carry):
        place = jnp.zeros((CHUNK, ROWS), jnp.int32)
        sub = lax.broadcasted_iota(jnp.int32, (CHUNK, ROWS), 0)
        for i in range(CHUNK):
            n = c * CHUNK + i
            at = text[jnp.minimum(low + n, text.shape[0] - 1)] - first
            place = jnp.where(sub == i, jnp.where(n < count, at, -1), place)
        lane = lax.broadcasted_iota(jnp.int32, (CHUNK, ROWS), 1)
        select = jnp.where(lane == place, 1.0, 0.0).astype(BF)
        picked = dot(select, q_ref[...]).astype(BF)
        queries = jnp.concatenate(
            [picked[:, h * HD : (h + 1) * HD] for h in range(GROUP)], axis=0
        )
        place = jnp.concatenate([place[:, :HD]] * GROUP, axis=0)[:, :1]
        limit = first + jnp.maximum(place, 0)
        lane = lax.broadcasted_iota(jnp.int32, (1, half), 1)
        spread = lane + (lane // ROWS) * ROWS
        parts = []
        for ref, parity in ((mine_ref, core), (other_ref, 1 - core)):
            live = spread + parity * ROWS <= limit
            parts.append(jnp.where(live, dot_t(queries, ref[:, :HD]), LOW))
        top = jnp.maximum(*(jnp.max(x, axis=1, keepdims=True) for x in parts))
        parts = [jnp.exp2((x - top) * FACTOR) for x in parts]
        total = sum(jnp.sum(x, axis=1, keepdims=True) for x in parts)
        share = jnp.where(place >= 0, 1.0 / total, 0.0)
        for p, x in enumerate(parts):
            out_ref[p : p + 1, :] += jnp.sum(x * share, axis=0, keepdims=True)
        return carry

    lax.fori_loop(0, (count + CHUNK - 1) // CHUNK, chunk, 0)
    mine, other = (out_ref[0:1, :], out_ref[1:2, :])
    even, odd = (jnp.where(core == 0, mine, other), jnp.where(core == 0, other, mine))
    for p, x in enumerate((even, odd)):
        high = x.astype(BF)
        high_ref[p : p + 1, :] = high
        low_ref[p : p + 1, :] = (x - high.astype(F32)).astype(BF)


def text_sums(text_rows, q2, mine, other):
    tokens = 2 * mine.shape[0]
    vmem = pl.BlockSpec(memory_space=pltpu.VMEM)
    return pl.pallas_call(
        text_kernel,
        out_shape=(jax.ShapeDtypeStruct((2, tokens // 2), BF),) * 2,
        in_specs=[smem(), vmem, vmem, vmem, pl.BlockSpec(memory_space=pl.ANY)],
        out_specs=(vmem, vmem),
        scratch_shapes=[
            pltpu.VMEM((2, tokens // 2), F32),
            pltpu.VMEM(other.shape, BF),
            pltpu.SemaphoreType.DMA(()),
        ],
        compiler_params=pltpu.CompilerParams(vmem_limit_bytes=24 << 20),
        cost_estimate=pl.CostEstimate(
            flops=2 * GROUP * CHUNK * tokens * HD,
            transcendentals=GROUP * CHUNK * tokens,
            bytes_accessed=4 * tokens * HD,
        ),
        name="text_sums",
    )(text_rows, text_rows.reshape(1, -1), q2, mine, other)


def attend3_kernel(q_hbm, mine_ref, other_ref, out_ref, v_s, bias_s, q_ref, sem):
    fetch = pltpu.make_async_copy(q_hbm, q_ref, sem)
    fetch.start()
    rank = lax.axis_index("seq")
    chip, core = (rank // 2, rank % 2)
    half = mine_ref.shape[0]
    v_s[:half, :HD] = mine_ref[:, HD:]
    v_s[half:, :HD] = other_ref[:, HD:]
    v_s[:, HD:] = jnp.ones((2 * half, HD), BF)
    row = lax.broadcasted_iota(jnp.int32, (1, half), 1)
    rest = row % PAD
    live = rest < SHARE
    query = lax.broadcasted_iota(jnp.int32, (PAD, half), 0)
    start = chip * PAD
    own = (row - start <= query) & live
    bias_s[:, :half] = jnp.where(own, 0.0, LOW)
    earlier = (row < start + core * PAD) & live
    bias_s[:, half:] = jnp.where(earlier & (query >= 0), 0.0, LOW)

    def scored(h):
        q = q_ref[:, h * HD : (h + 1) * HD]
        left = dot_t(q, mine_ref[:, :HD]) + bias_s[:, :half]
        right = dot_t(q, other_ref[:, :HD]) + bias_s[:, half:]
        return left, right

    def weighed(h, scores):
        left, right = scores
        top = jnp.maximum(
            jnp.max(left, axis=1, keepdims=True), jnp.max(right, axis=1, keepdims=True)
        )
        left = jnp.exp2((left - top) * FACTOR).astype(BF)
        right = jnp.exp2((right - top) * FACTOR).astype(BF)
        total = dot(left, v_s[:half]) + dot(right, v_s[half:])
        out = (total[:, :HD] / total[:, HD:]).astype(BF)
        out_ref[:, h * HD : (h + 1) * HD] = out[:SHARE]

    fetch.wait()
    in_turn(range(GROUP), scored, weighed)


def attend3(q3, mine, other):
    vmem = pl.BlockSpec(memory_space=pltpu.VMEM)
    keys = 2 * mine.shape[0]
    q3 = pltpu.with_memory_space_constraint(q3, pltpu.HBM)
    return pl.pallas_call(
        attend3_kernel,
        out_shape=jax.ShapeDtypeStruct((SHARE, q3.shape[1]), BF),
        in_specs=[pl.BlockSpec(memory_space=pl.ANY), vmem, vmem],
        out_specs=vmem,
        scratch_shapes=[
            pltpu.VMEM((keys, 2 * HD), BF),
            pltpu.VMEM((PAD, keys), F32),
            pltpu.VMEM(q3.shape, BF),
            pltpu.SemaphoreType.DMA(()),
        ],
        compiler_params=pltpu.CompilerParams(vmem_limit_bytes=28 << 20),
        cost_estimate=pl.CostEstimate(
            flops=6 * GROUP * PAD * keys * HD,
            transcendentals=GROUP * PAD * keys,
            bytes_accessed=4 * keys * HD,
        ),
        name="attend3",
    )(q3, mine, other)


def from_core(x):
    count = lax.axis_size("seq")
    return lax.ppermute(x, "seq", [(i ^ 1, i) for i in range(count)])


def from_head(x, distance):
    count = lax.axis_size("head")
    return lax.ppermute(x, "head", [((i + distance) % count, i) for i in range(count)])


def over_chips(many):
    count = lax.axis_size("seq")
    groups = [[i for i in range(count) if i % 2 == core] for core in range(2)]
    return lax.all_to_all(many, "seq", 0, 0, axis_index_groups=groups, tiled=True)


def over_heads(x):
    count = lax.axis_size("head")
    return [x] + [
        lax.ppermute(x, "head", [(i ^ step, i) for i in range(count)]) for step in range(1, count)
    ]


def from_partner(x):
    count = lax.axis_size("seq")
    return lax.ppermute(x, "seq", [(count - 1 - i, i) for i in range(count)])


def body(
    q2,
    k2,
    v2,
    hidden,
    w_query,
    b_query,
    w_key,
    b_key,
    w_value,
    b_value,
    kept_index,
    block_count,
    text_rows,
):
    seq_count = lax.axis_size("seq")
    head_count = lax.axis_size("head")
    depth = hidden.shape[1]

    chips = seq_count // 2
    kv2 = jnp.concatenate([k2, v2], axis=1)
    mine2 = over_chips(jnp.broadcast_to(kv2[None], (chips, *kv2.shape)))
    mine2 = mine2.reshape(-1, 2 * HD)

    own, sent = pick_rows(block_count, kept_index, hidden)
    x = own + from_core(sent)
    marks = x[:, depth : depth + 2].astype(jnp.int32)
    half = depth // 2
    low, high = (x[:, :half], x[:, half:depth])
    weights = (w_query, w_key, w_value)

    low_before, high_next = (from_head(low, -1), from_head(high, 1))
    high_before, low_next = (from_head(high, -1), from_head(low, 1))
    partial = project([(0, 0), (0, 1)], [low, high], weights)
    low_far, high_far = (from_head(low_before, -1), from_head(high_next, 1))

    sums, marks, far = lax.optimization_barrier((partial[1], marks, q2[PART:]))
    partial = (partial[0], sums)
    far = from_partner(far)
    positions = marks[:, 0] * 128 + marks[:, 1]
    lane = jnp.arange(HD, dtype=jnp.int32)
    freqs = 1000000.0 ** (-((lane % (HD // 2)).astype(F32) * 2.0) / HD)
    angles = positions.astype(F32)[:, None] * freqs[None, :]
    cosine = jnp.cos(angles)
    sine = jnp.sin(angles) * jnp.where(lane < HD // 2, -1.0, 1.0)[None, :]
    biases = tuple(b[None, :] for b in (b_query, b_key, b_value))
    partial = project(
        [(-1, 0), (1, 1), (-1, 1), (1, 0)],
        [low_before, high_next, high_before, low_next],
        weights,
        partial,
    )
    last = [pltpu.with_memory_space_constraint(x, pltpu.HBM) for x in (low_far, high_far)]
    sums, far, cosine, sine, mine2, last = lax.optimization_barrier(
        (partial[1], far, cosine, sine, mine2, last)
    )
    partial = (partial[0], sums)
    other2 = from_core(mine2)
    q3, kv3 = project([(-2, 0), (2, 1)], last, weights, partial, (*biases, cosine, sine))
    kv3, other2 = lax.optimization_barrier((kv3, other2))
    sums = text_sums(text_rows, q2, mine2, other2)

    sums = [part.reshape(2, chips, ROWS).swapaxes(0, 1) for part in sums]
    kept = jnp.broadcast_to(kv3[None, :SHARE], (chips, SHARE, 2 * HD))
    many = jnp.concatenate([kept, *sums], axis=1)
    mine = over_chips(many)
    far, many = lax.optimization_barrier((far, many))
    near, far = attend(q2[:PART], far, mine2, other2)
    far, mine = lax.optimization_barrier((far, mine))
    other = from_core(mine)
    far = from_partner(far)

    got = sum(jnp.sum(x[:, SHARE:].astype(F32), axis=0) for x in (mine, other))
    got = got[:2] + got[2:]
    got = over_heads(jnp.where(lax.axis_index("seq") % 2 == 0, got[0], got[1]))
    attn3 = attend3(q3, mine.reshape(-1, 2 * HD), other.reshape(-1, 2 * HD))
    attn3, far, *got = lax.optimization_barrier((attn3, far, *got))
    attn2 = jnp.concatenate([near, far], axis=0)
    tokens = seq_count * ROWS
    importance = (got[0] + got[1]) + (got[2] + got[3])
    importance = importance * (tokens / (GROUP * head_count * text_rows.shape[0]))
    return (attn2, importance, attn3)


def solution(mesh):
    placed = (
        P("seq", "head"),
        P("seq", "head"),
        P("seq", "head"),
        P("seq", "head"),
        P(None, "head"),
        P("head"),
        P(None, "head"),
        P("head"),
        P(None, "head"),
        P("head"),
        P("seq"),
        P("seq"),
        P(),
    )
    return jax.shard_map(
        body,
        mesh=mesh,
        in_specs=placed,
        out_specs=(P("seq", "head"), P("seq"), P("seq", "head")),
        check_vma=False,
    )
```

```python
import math

import jax
import jax.numpy as jnp
from jax import lax
from jax.experimental import pallas as pl
from jax.experimental.pallas import tpu as pltpu
from jax.sharding import PartitionSpec as P

HD = 128
GROUP = 8
BLOCK = 128
ROWS = 256
SHARE = 132
PAD = 136
PART = ROWS // 2
WIDE = 1024
FACTOR = math.log2(math.e) / math.sqrt(HD)
LOW = -1e30
BF = jnp.bfloat16
F32 = jnp.float32


def dot(a, b):
    return jnp.dot(a, b, preferred_element_type=F32)


def dot_t(a, b):
    return lax.dot_general(a, b, (((1,), (1,)), ((), ())), preferred_element_type=F32)


def whole(shape):
    return pl.BlockSpec(shape, lambda *_: (0,) * len(shape))


def smem():
    return pl.BlockSpec(memory_space=pltpu.SMEM)


def pick_kernel(counts, index_ref, hidden_ref, own_ref, send_ref):
    rank = lax.axis_index("seq")
    core, first = (rank % 2, rank * ROWS)
    live0, live1 = (counts[0], counts[1])
    count = live0 + live1
    start = jnp.where(core == 0, 0, 2 * SHARE - count)
    lane = lax.broadcasted_iota(jnp.int32, (PAD, ROWS), 1)
    place = lax.broadcasted_iota(jnp.int32, (PAD, ROWS), 0)
    second = lane >= BLOCK
    within = jnp.where(second, lane - BLOCK, lane)
    rank = jnp.where(second, within + live0, within)
    live = within < jnp.where(second, live1, live0)
    row = index_ref[...] + jnp.where(second, BLOCK, 0)
    column = lax.broadcasted_iota(jnp.int32, (PAD, BLOCK), 1)
    for out_ref, base in ((own_ref, SHARE * core), (send_ref, SHARE * (1 - core))):
        wanted = place + (base - start)
        match = (rank == wanted) & live & (place < SHARE)
        source = jnp.sum(jnp.where(match, (row + 1).astype(F32), 0.0), axis=1, keepdims=True)
        source = source.astype(jnp.int32) - 1
        select = jnp.where(lane == source, 1.0, 0.0).astype(BF)
        out_ref[:, : hidden_ref.shape[1]] = dot(select, hidden_ref[...]).astype(BF)
        position = jnp.where(source >= 0, source + first, 0)
        high = jnp.where(column == 0, position >> 7, 0)
        marks = jnp.where(column == 1, position & 127, high)
        out_ref[:, hidden_ref.shape[1] :] = marks.astype(F32).astype(BF)


def pick_rows(block_count, kept_index, hidden):
    width = hidden.shape[1] + BLOCK
    shape = jax.ShapeDtypeStruct((PAD, width), BF)
    return pl.pallas_call(
        pick_kernel,
        out_shape=(shape, shape),
        in_specs=[smem(), pl.BlockSpec(memory_space=pltpu.VMEM), pl.BlockSpec(memory_space=pltpu.VMEM)],
        out_specs=(pl.BlockSpec(memory_space=pltpu.VMEM),) * 2,
        compiler_params=pltpu.CompilerParams(vmem_limit_bytes=16 << 20),
        cost_estimate=pl.CostEstimate(
            flops=4 * PAD * ROWS * width, transcendentals=0, bytes_accessed=4 * ROWS * width
        ),
        name="pick_rows",
    )(block_count, kept_index.reshape(1, ROWS), hidden)


def rotated(u, cosine, sine):
    return u * cosine + pltpu.roll(u, HD // 2, 1) * sine


STEP = 1024


def project_kernel(places, first, last, *refs):
    pieces = len(places)
    here, heads = (lax.axis_index("head"), lax.axis_size("head"))
    x_refs = refs[:pieces]
    weights = refs[pieces : pieces + 3]
    rest = refs[pieces + 3 :]
    if not first:
        before = rest[:2]
        rest = rest[2:]
    if last:
        bq, bk, bv, cosine, sine = rest[:5]
        rest = rest[5:]
    q_to, kv_out, *held, kv_s, q_s, q_out, sems, part_sems = rest
    if last:
        q_out = q_to
    sums = (q_s, kv_s)
    loads = []
    if not first:
        loads = [
            pltpu.make_async_copy(x, to, part_sems.at[i])
            for i, (x, to) in enumerate(zip(before, sums))
        ]
    depth = x_refs[0].shape[1]
    copies = []
    for p in range(pieces):
        for part in range(depth // STEP):
            at = len(copies) * STEP
            distance, side = places[p]
            block = 2 * ((here + heads + distance) % heads) + side
            start = pl.multiple_of(block * depth + part * STEP, STEP)
            copies.append(
                [
                    pltpu.make_async_copy(
                        w.at[pl.ds(start, STEP), :], to.at[at : at + STEP, :], sems.at[len(copies), i]
                    )
                    for i, (w, to) in enumerate(zip(weights, held))
                ]
            )
    for group in [*copies, loads]:
        for copy in group:
            copy.start()
    totals = [0.0, 0.0, 0.0]
    for n, group in enumerate(copies):
        p, part = divmod(n, depth // STEP)
        x = x_refs[p][:, part * STEP : (part + 1) * STEP]
        for copy in group:
            copy.wait()
        at = slice(n * STEP, (n + 1) * STEP)
        totals = [old + dot(x, w[at, :]) for old, w in zip(totals, held)]
    for copy in loads:
        copy.wait()
    q, k, v = totals
    if not first:
        q, k, v = (q + q_s[...], k + kv_s[:, :HD], v + kv_s[:, HD:])
    if last:
        c, s = (cosine[...], sine[...])
        for h in range(GROUP):
            at = slice(h * HD, (h + 1) * HD)
            q_out[:, at] = rotated(q[:, at] + bq[:, at], c, s).astype(BF)
        kv_out[:, :HD] = rotated(k + bk[...], c, s).astype(BF)
        kv_out[:, HD:] = (v + bv[...]).astype(BF)
        stores = []
    else:
        q_out[...] = q
        kv_s[:, :HD] = k
        kv_s[:, HD:] = v
        stores = [
            pltpu.make_async_copy(q_out, q_to, part_sems.at[2]),
            pltpu.make_async_copy(kv_s, kv_out, part_sems.at[3]),
        ]
    for copy in stores:
        copy.start()
    for copy in stores:
        copy.wait()


def project(places, xs, weights, partial=(), finish=()):
    pieces = len(xs)
    depth = xs[0].shape[1]
    widths = [w.shape[1] for w in weights]
    kind = BF if finish else F32
    vmem = pl.BlockSpec(memory_space=pltpu.VMEM)
    weights = [pltpu.with_memory_space_constraint(w, pltpu.HBM) for w in weights]
    hbm = pl.BlockSpec(memory_space=pl.ANY)
    partial = [pltpu.with_memory_space_constraint(part, pltpu.HBM) for part in partial]

    def kernel(*refs):
        project_kernel(places, not partial, bool(finish), *refs)

    outs = ((PAD, widths[0]), (PAD, 2 * HD))
    return pl.pallas_call(
        kernel,
        out_shape=(
            *(jax.ShapeDtypeStruct(o, kind) if finish else pltpu.HBM(o, kind) for o in outs),
        ),
        in_specs=[vmem] * pieces
        + [hbm] * (3 + len(partial))
        + [vmem] * len(finish),
        out_specs=(vmem, vmem) if finish else (hbm, hbm),
        scratch_shapes=[pltpu.VMEM((pieces * depth, width), BF) for width in widths]
        + [
            pltpu.VMEM(outs[1], F32),
            pltpu.VMEM(outs[0], F32),
            pltpu.VMEM(outs[0], kind),
            pltpu.SemaphoreType.DMA((pieces * depth // STEP, 3)),
            pltpu.SemaphoreType.DMA((4,)),
        ],
        compiler_params=pltpu.CompilerParams(vmem_limit_bytes=28 << 20),
        cost_estimate=pl.CostEstimate(
            flops=2 * pieces * PAD * depth * sum(widths),
            transcendentals=0,
            bytes_accessed=2 * pieces * depth * sum(widths),
        ),
        name="project",
    )(*xs, *weights, *partial, *finish)


def in_turn(heads, scored, weighed):
    ahead = scored(heads[0])
    for at, h in enumerate(heads):
        scores = ahead
        if at + 1 < len(heads):
            ahead = scored(heads[at + 1])
        weighed(h, scores)


def attend_kernel(own_ref, far_ref, mine_ref, other_ref, *refs):
    rank = lax.axis_index("seq")
    partner = lax.axis_size("seq") - 1 - rank
    own_to, far_to, q_s, top_s, sum_s, v_s, bias_s, other_s, own_out, far_out, sems = refs
    fetch = pltpu.make_async_copy(other_ref, other_s, sems.at[0])
    fetch.start()
    core = rank % 2
    half = mine_ref.shape[0]
    pairs = GROUP // 2
    for g, ref in enumerate((own_ref, far_ref)):
        for h in range(GROUP):
            to = (h % 2) * PART
            q_s[g, h // 2, to : to + PART] = ref[:, h * HD : (h + 1) * HD]
    top_s[...] = jnp.full_like(top_s, LOW)
    sum_s[...] = jnp.zeros_like(sum_s)
    v_s[0, :, :HD] = mine_ref[:, HD:]
    v_s[:, :, HD:] = jnp.ones((2, half, HD), BF)
    fetch.wait()
    v_s[1, :, :HD] = other_s[:, HD:]

    def step(g, p, ref, b, bound, width=WIDE):
        at = pl.ds(pl.multiple_of(b * WIDE, WIDE), width)
        keys = ref[at, :HD]
        values = v_s[p, at, :]
        if bound is not None:
            key = lax.broadcasted_iota(jnp.int32, (PART, width), 1)
            query = lax.broadcasted_iota(jnp.int32, (PART, width), 0)
            bias = jnp.where(key + b * WIDE < bound[0] + bound[1] * query, 0.0, LOW)
            bias_s[:PART, :width] = bias
            bias_s[PART:, :width] = bias

        def scored(h):
            scores = dot_t(q_s[g, h], keys)
            return scores if bound is None else scores + bias_s[:, :width]

        def weighed(h, scores):
            before = top_s[g, h]
            top = jnp.maximum(before, jnp.max(scores, axis=1, keepdims=True))
            top_s[g, h] = top
            weights = jnp.exp2((scores - top[:, :1]) * FACTOR).astype(BF)
            fade = jnp.exp2((before - top) * FACTOR)
            fade = jnp.concatenate([fade, fade], axis=1)
            sum_s[g, h] = sum_s[g, h] * fade + dot(weights, values)

        in_turn(range(pairs), scored, weighed)

    def group(g, carry):
        place = jnp.where(g == 0, rank, partner)
        chip, side = (place // 2, place % 2)
        for p, ref in enumerate((mine_ref, other_s)):
            parity = core if p == 0 else 1 - core
            same = jnp.where(parity == side, 1, 0)
            before = (chip + jnp.where(parity < side, 1, 0)) * ROWS
            whole_steps = before // WIDE

            def plain(b, carry, p=p, ref=ref):
                step(g, p, ref, b, None)
                return carry

            lax.fori_loop(0, whole_steps, plain, 0)

            rest = before % WIDE + same * ROWS
            bound = (before + same * (PART * g + 1), same)

            @pl.when((rest > 0) & (rest <= WIDE // 2))
            def _(p=p, ref=ref, whole_steps=whole_steps, bound=bound):
                step(g, p, ref, whole_steps, bound, WIDE // 2)

            @pl.when(rest > WIDE // 2)
            def _(p=p, ref=ref, whole_steps=whole_steps, bound=bound):
                step(g, p, ref, whole_steps, bound)

        return carry

    lax.fori_loop(0, 2, group, 0)
    for g, ref in enumerate((own_out, far_out)):
        for h in range(GROUP):
            total = sum_s[g, h // 2, (h % 2) * PART : (h % 2) * PART + PART]
            ref[:, h * HD : (h + 1) * HD] = (total[:, :HD] / total[:, HD:]).astype(BF)
    stores = [
        pltpu.make_async_copy(own_out, own_to, sems.at[1]),
        pltpu.make_async_copy(far_out, far_to, sems.at[2]),
    ]
    for copy in stores:
        copy.start()
    for copy in stores:
        copy.wait()


def attend(own, far, mine, other):
    tokens = 2 * mine.shape[0]
    vmem = pl.BlockSpec(memory_space=pltpu.VMEM)
    hbm = pl.BlockSpec(memory_space=pl.ANY)
    far, other = (pltpu.with_memory_space_constraint(x, pltpu.HBM) for x in (far, other))
    out = pltpu.HBM(own.shape, BF)
    return pl.pallas_call(
        attend_kernel,
        out_shape=(out, out),
        in_specs=[vmem, vmem, vmem, hbm],
        out_specs=(hbm, hbm),
        scratch_shapes=[
            pltpu.VMEM((2, GROUP // 2, 2 * PART, HD), BF),
            pltpu.VMEM((2, GROUP // 2, 2 * PART, HD), F32),
            pltpu.VMEM((2, GROUP // 2, 2 * PART, 2 * HD), F32),
            pltpu.VMEM((2, tokens // 2, 2 * HD), BF),
            pltpu.VMEM((2 * PART, WIDE), F32),
            pltpu.VMEM(other.shape, BF),
            pltpu.VMEM(own.shape, BF),
            pltpu.VMEM(own.shape, BF),
            pltpu.SemaphoreType.DMA((3,)),
        ],
        compiler_params=pltpu.CompilerParams(vmem_limit_bytes=28 << 20),
        cost_estimate=pl.CostEstimate(
            flops=4 * GROUP * PART * tokens * HD,
            transcendentals=GROUP * PART * tokens,
            bytes_accessed=4 * tokens * HD,
        ),
        name="attend2",
    )(own, far, mine, other)


CHUNK = 8


def text_kernel(text, rows_ref, q_ref, mine_ref, other_hbm, high_ref, low_ref, out_ref, other_ref, sem):
    rank = lax.axis_index("seq")
    core, first = (rank % 2, rank * ROWS)
    before = jnp.where(rows_ref[...] < first, 1.0, 0.0)
    within = jnp.where(rows_ref[...] < first + ROWS, 1.0, 0.0) - before
    low, count = (jnp.sum(x).astype(jnp.int32) for x in (before, within))
    half = mine_ref.shape[0]
    fetch = pltpu.make_async_copy(other_hbm, other_ref, sem)
    fetch.start()
    out_ref[...] = jnp.zeros_like(out_ref)
    rows = GROUP * CHUNK
    fetch.wait()

    def chunk(c, carry):
        place = jnp.zeros((CHUNK, ROWS), jnp.int32)
        sub = lax.broadcasted_iota(jnp.int32, (CHUNK, ROWS), 0)
        for i in range(CHUNK):
            n = c * CHUNK + i
            at = text[jnp.minimum(low + n, text.shape[0] - 1)] - first
            place = jnp.where(sub == i, jnp.where(n < count, at, -1), place)
        lane = lax.broadcasted_iota(jnp.int32, (CHUNK, ROWS), 1)
        select = jnp.where(lane == place, 1.0, 0.0).astype(BF)
        picked = dot(select, q_ref[...]).astype(BF)
        queries = jnp.concatenate(
            [picked[:, h * HD : (h + 1) * HD] for h in range(GROUP)], axis=0
        )
        place = jnp.concatenate([place[:, :HD]] * GROUP, axis=0)[:, :1]
        limit = first + jnp.maximum(place, 0)
        lane = lax.broadcasted_iota(jnp.int32, (1, half), 1)
        spread = lane + (lane // ROWS) * ROWS
        parts = []
        for ref, parity in ((mine_ref, core), (other_ref, 1 - core)):
            live = spread + parity * ROWS <= limit
            parts.append(jnp.where(live, dot_t(queries, ref[:, :HD]), LOW))
        top = jnp.maximum(*(jnp.max(x, axis=1, keepdims=True) for x in parts))
        parts = [jnp.exp2((x - top) * FACTOR) for x in parts]
        total = sum(jnp.sum(x, axis=1, keepdims=True) for x in parts)
        share = jnp.where(place >= 0, 1.0 / total, 0.0)
        for p, x in enumerate(parts):
            out_ref[p : p + 1, :] += jnp.sum(x * share, axis=0, keepdims=True)
        return carry

    lax.fori_loop(0, (count + CHUNK - 1) // CHUNK, chunk, 0)
    mine, other = (out_ref[0:1, :], out_ref[1:2, :])
    even, odd = (jnp.where(core == 0, mine, other), jnp.where(core == 0, other, mine))
    for p, x in enumerate((even, odd)):
        high = x.astype(BF)
        high_ref[p : p + 1, :] = high
        low_ref[p : p + 1, :] = (x - high.astype(F32)).astype(BF)


def text_sums(text_rows, q2, mine, other):
    tokens = 2 * mine.shape[0]
    vmem = pl.BlockSpec(memory_space=pltpu.VMEM)
    return pl.pallas_call(
        text_kernel,
        out_shape=(jax.ShapeDtypeStruct((2, tokens // 2), BF),) * 2,
        in_specs=[smem(), vmem, vmem, vmem, pl.BlockSpec(memory_space=pl.ANY)],
        out_specs=(vmem, vmem),
        scratch_shapes=[
            pltpu.VMEM((2, tokens // 2), F32),
            pltpu.VMEM(other.shape, BF),
            pltpu.SemaphoreType.DMA(()),
        ],
        compiler_params=pltpu.CompilerParams(vmem_limit_bytes=24 << 20),
        cost_estimate=pl.CostEstimate(
            flops=2 * GROUP * CHUNK * tokens * HD,
            transcendentals=GROUP * CHUNK * tokens,
            bytes_accessed=4 * tokens * HD,
        ),
        name="text_sums",
    )(text_rows, text_rows.reshape(1, -1), q2, mine, other)


def attend3_kernel(q_hbm, mine_ref, other_ref, out_ref, v_s, bias_s, q_ref, sem):
    fetch = pltpu.make_async_copy(q_hbm, q_ref, sem)
    fetch.start()
    rank = lax.axis_index("seq")
    chip, core = (rank // 2, rank % 2)
    half = mine_ref.shape[0]
    v_s[:half, :HD] = mine_ref[:, HD:]
    v_s[half:, :HD] = other_ref[:, HD:]
    v_s[:, HD:] = jnp.ones((2 * half, HD), BF)
    row = lax.broadcasted_iota(jnp.int32, (1, half), 1)
    rest = row % PAD
    live = rest < SHARE
    query = lax.broadcasted_iota(jnp.int32, (PAD, half), 0)
    start = chip * PAD
    own = (row - start <= query) & live
    bias_s[:, :half] = jnp.where(own, 0.0, LOW)
    earlier = (row < start + core * PAD) & live
    bias_s[:, half:] = jnp.where(earlier & (query >= 0), 0.0, LOW)

    def scored(h):
        q = q_ref[:, h * HD : (h + 1) * HD]
        left = dot_t(q, mine_ref[:, :HD]) + bias_s[:, :half]
        right = dot_t(q, other_ref[:, :HD]) + bias_s[:, half:]
        return left, right

    def weighed(h, scores):
        left, right = scores
        top = jnp.maximum(
            jnp.max(left, axis=1, keepdims=True), jnp.max(right, axis=1, keepdims=True)
        )
        left = jnp.exp2((left - top) * FACTOR).astype(BF)
        right = jnp.exp2((right - top) * FACTOR).astype(BF)
        total = dot(left, v_s[:half]) + dot(right, v_s[half:])
        out = (total[:, :HD] / total[:, HD:]).astype(BF)
        out_ref[:, h * HD : (h + 1) * HD] = out[:SHARE]

    fetch.wait()
    in_turn(range(GROUP), scored, weighed)


def attend3(q3, mine, other):
    vmem = pl.BlockSpec(memory_space=pltpu.VMEM)
    keys = 2 * mine.shape[0]
    q3 = pltpu.with_memory_space_constraint(q3, pltpu.HBM)
    return pl.pallas_call(
        attend3_kernel,
        out_shape=jax.ShapeDtypeStruct((SHARE, q3.shape[1]), BF),
        in_specs=[pl.BlockSpec(memory_space=pl.ANY), vmem, vmem],
        out_specs=vmem,
        scratch_shapes=[
            pltpu.VMEM((keys, 2 * HD), BF),
            pltpu.VMEM((PAD, keys), F32),
            pltpu.VMEM(q3.shape, BF),
            pltpu.SemaphoreType.DMA(()),
        ],
        compiler_params=pltpu.CompilerParams(vmem_limit_bytes=28 << 20),
        cost_estimate=pl.CostEstimate(
            flops=6 * GROUP * PAD * keys * HD,
            transcendentals=GROUP * PAD * keys,
            bytes_accessed=4 * keys * HD,
        ),
        name="attend3",
    )(q3, mine, other)


def from_core(x):
    count = lax.axis_size("seq")
    return lax.ppermute(x, "seq", [(i ^ 1, i) for i in range(count)])


def from_head(x, distance):
    count = lax.axis_size("head")
    return lax.ppermute(x, "head", [((i + distance) % count, i) for i in range(count)])


def over_chips(many):
    count = lax.axis_size("seq")
    groups = [[i for i in range(count) if i % 2 == core] for core in range(2)]
    return lax.all_to_all(many, "seq", 0, 0, axis_index_groups=groups, tiled=True)


def over_heads(x):
    count = lax.axis_size("head")
    return [x] + [
        lax.ppermute(x, "head", [(i ^ step, i) for i in range(count)]) for step in range(1, count)
    ]


def from_partner(x):
    count = lax.axis_size("seq")
    return lax.ppermute(x, "seq", [(count - 1 - i, i) for i in range(count)])


def body(
    q2,
    k2,
    v2,
    hidden,
    w_query,
    b_query,
    w_key,
    b_key,
    w_value,
    b_value,
    kept_index,
    block_count,
    text_rows,
):
    seq_count = lax.axis_size("seq")
    head_count = lax.axis_size("head")
    depth = hidden.shape[1]

    chips = seq_count // 2
    kv2 = jnp.concatenate([k2, v2], axis=1)
    mine2 = over_chips(jnp.broadcast_to(kv2[None], (chips, *kv2.shape)))
    mine2 = mine2.reshape(-1, 2 * HD)

    own, sent = pick_rows(block_count, kept_index, hidden)
    x = own + from_core(sent)
    marks = x[:, depth : depth + 2].astype(jnp.int32)
    half = depth // 2
    low, high = (x[:, :half], x[:, half:depth])
    weights = (w_query, w_key, w_value)

    low_before, high_next = (from_head(low, -1), from_head(high, 1))
    high_before, low_next = (from_head(high, -1), from_head(low, 1))
    partial = project([(0, 0), (0, 1)], [low, high], weights)
    low_far, high_far = (from_head(low_before, -1), from_head(high_next, 1))

    sums, marks, far = lax.optimization_barrier((partial[1], marks, q2[PART:]))
    partial = (partial[0], sums)
    far = from_partner(far)
    positions = marks[:, 0] * 128 + marks[:, 1]
    lane = jnp.arange(HD, dtype=jnp.int32)
    freqs = 1000000.0 ** (-((lane % (HD // 2)).astype(F32) * 2.0) / HD)
    angles = positions.astype(F32)[:, None] * freqs[None, :]
    cosine = jnp.cos(angles)
    sine = jnp.sin(angles) * jnp.where(lane < HD // 2, -1.0, 1.0)[None, :]
    biases = tuple(b[None, :] for b in (b_query, b_key, b_value))
    partial = project(
        [(-1, 0), (1, 1), (-1, 1), (1, 0)],
        [low_before, high_next, high_before, low_next],
        weights,
        partial,
    )
    last = [pltpu.with_memory_space_constraint(x, pltpu.HBM) for x in (low_far, high_far)]
    sums, far, cosine, sine, mine2, last = lax.optimization_barrier(
        (partial[1], far, cosine, sine, mine2, last)
    )
    partial = (partial[0], sums)
    other2 = from_core(mine2)
    q3, kv3 = project([(-2, 0), (2, 1)], last, weights, partial, (*biases, cosine, sine))
    kv3, other2 = lax.optimization_barrier((kv3, other2))
    sums = text_sums(text_rows, q2, mine2, other2)

    sums = [part.reshape(2, chips, ROWS).swapaxes(0, 1) for part in sums]
    kept = jnp.broadcast_to(kv3[None, :SHARE], (chips, SHARE, 2 * HD))
    many = jnp.concatenate([kept, *sums], axis=1)
    mine = over_chips(many)
    far, many = lax.optimization_barrier((far, many))
    near, far = attend(q2[:PART], far, mine2, other2)
    far, mine = lax.optimization_barrier((far, mine))
    other = from_core(mine)
    far = from_partner(far)

    got = sum(jnp.sum(x[:, SHARE:].astype(F32), axis=0) for x in (mine, other))
    got = got[:2] + got[2:]
    got = over_heads(jnp.where(lax.axis_index("seq") % 2 == 0, got[0], got[1]))
    attn3 = attend3(q3, mine.reshape(-1, 2 * HD), other.reshape(-1, 2 * HD))
    attn3, far, *got = lax.optimization_barrier((attn3, far, *got))
    attn2 = jnp.concatenate([near, far], axis=0)
    tokens = seq_count * ROWS
    importance = (got[0] + got[1]) + (got[2] + got[3])
    importance = importance * (tokens / (GROUP * head_count * text_rows.shape[0]))
    return (attn2, importance, attn3)


def solution(mesh):
    placed = (
        P("seq", "head"),
        P("seq", "head"),
        P("seq", "head"),
        P("seq", "head"),
        P(None, "head"),
        P("head"),
        P(None, "head"),
        P("head"),
        P(None, "head"),
        P("head"),
        P("seq"),
        P("seq"),
        P(),
    )
    return jax.shard_map(
        body,
        mesh=mesh,
        in_specs=placed,
        out_specs=(P("seq", "head"), P("seq"), P("seq", "head")),
        check_vma=False,
    )
```
